32 devices in a mesh: dp: 8 (over y, x, core), tensor: 4 (over z).
Axes of the slice: x: 2, y: 2, z: 4, core: 2. Of those that a mesh axis runs over, the one named last changes fastest.
Arguments:
- inputs: bfloat16 [2, 8192, 1536], P(None, ('dp', 'tensor')), may hold values from -6 to 6
- seq_lengths: int32 [16], replicated, may hold values from 256 to 1024, as said below
- seq_assign: int32 [2, 8], P(None, 'dp'), may hold values from 0 to 15, as said below
- norm1_gain: float32 [1536], replicated, may hold values from 0.25 to 1.75
- w_query: bfloat16 [1536, 1536], P('dp', 'tensor'), may hold values from -0.15625 to 0.15625
- w_key: bfloat16 [1536, 1536], P('dp', 'tensor'), may hold values from -0.15625 to 0.15625
- w_value: bfloat16 [1536, 1536], P('dp', 'tensor'), may hold values from -0.15625 to 0.15625
- w_forget: bfloat16 [1536, 24], P('dp', 'tensor'), may hold values from -0.15625 to 0.15625
- forget_bias: float32 [24], replicated, may hold values from 3 to 9
- w_out: bfloat16 [1536, 1536], P('tensor', 'dp'), may hold values from -0.875 to 0.875
- norm2_gain: float32 [1536], replicated, may hold values from 0.25 to 1.75
- w_gate: bfloat16 [1536, 4096], P('dp', 'tensor'), may hold values from -0.15625 to 0.15625
- w_up: bfloat16 [1536, 4096], P('dp', 'tensor'), may hold values from -0.15625 to 0.15625
- w_down: bfloat16 [4096, 1536], P('tensor', 'dp'), may hold values from -0.1875 to 0.1875
- out_grad: bfloat16 [2, 8192, 1536], P(None, ('dp', 'tensor')), may hold values from -6 to 6
Outputs:
- outputs: bfloat16 [2, 8192, 1536], P(None, ('dp', 'tensor'))
- input_grad: bfloat16 [2, 8192, 1536], P(None, ('dp', 'tensor'))
- norm1_gain_grad: float32 [1536], replicated
- w_query_grad: float32 [1536, 1536], P('dp', 'tensor')
- w_key_grad: float32 [1536, 1536], P('dp', 'tensor')
- w_value_grad: float32 [1536, 1536], P('dp', 'tensor')
- w_forget_grad: float32 [1536, 24], P('dp', 'tensor')
- forget_bias_grad: float32 [24], replicated
- w_out_grad: float32 [1536, 1536], P('tensor', 'dp')
- norm2_gain_grad: float32 [1536], replicated
- w_gate_grad: float32 [1536, 4096], P('dp', 'tensor')
- w_up_grad: float32 [1536, 4096], P('dp', 'tensor')
- w_down_grad: float32 [4096, 1536], P('tensor', 'dp')
The draws below stay inside these ranges and needn't reach their ends.
Inputs may be any that keep to these rules, and one draw needn't show every extreme that they name: `seq_lengths`: each sequence's valid slots are a prefix of its 1024 slots; some sequence has exactly 1024 valid slots and another exactly 256. `seq_assign`: A permutation of the 16 sequence numbers: every sequence occupies exactly one block.
All inputs are finite; a program needn't handle non-finite values.
Results may differ from the reference program's by a relative error of at most 0.015.
Values may be sent and summed in bfloat16 or wider, within the bound.
A program may use at most 256 MiB of HBM per device.

```python
import math
import jax
import jax.numpy as jnp
from jax import lax

D = 1536
HEADS = 24
HEAD_DIM = 64
FF = 4096
SLOTS = 1024
MICRO = 2
MIN_LEN = 256
ROWS = 8192
NSEQ = 16
N_DP = 8


def draw_seq_lengths(key, part):
    key_one, key_two, key_three = jax.random.split(jax.random.fold_in(key, 11), 3)
    lengths = jax.random.randint(key_one, (NSEQ,), MIN_LEN, SLOTS + 1)
    longest = jax.random.randint(key_two, (), 0, NSEQ)
    shortest = (longest + 1 + jax.random.randint(key_three, (), 0, NSEQ - 1)) % NSEQ
    places = jnp.arange(NSEQ)
    lengths = jnp.where(places == longest, SLOTS, lengths)
    lengths = jnp.where(places == shortest, MIN_LEN, lengths)
    return lengths.astype(jnp.int32)


def draw_seq_assign(key, part):
    order = jax.random.permutation(jax.random.fold_in(key, 23), NSEQ)
    return order.reshape(MICRO, NSEQ // MICRO).astype(jnp.int32)


def block_scale(rng, extent, shards, smallest, top_value):
    def one(dim, blocks):
        heights = jax.random.uniform(jax.random.fold_in(jax.random.fold_in(rng, 6), dim), (blocks,), jnp.float32, smallest / len(shards), top_value / len(shards))
        return jnp.repeat(jnp.exp(heights), extent[dim] // blocks).reshape((-1,) + (1,) * (len(extent) - dim - 1))

    level = one(*shards[0])
    for cut in shards[1:]:
        level = level * one(*cut)
    return level


def scatter_about(key, shape, width, bound, cuts=(), kind=jnp.bfloat16):
    values = width * jax.random.normal(key, shape, jnp.float32)
    if cuts:
        values = values * block_scale(key, shape, cuts, -0.22, 0.18)
    return jnp.clip(values, -bound, bound).astype(kind)


def setup_inputs(seed: int = 0) -> dict:
    keys = jax.random.split(jax.random.key(seed), 16)
    return {
        "inputs": scatter_about(keys[0], (MICRO, ROWS, D), 1.0, 6.0, ((1, 32),)),
        "seq_lengths": draw_seq_lengths(jax.random.fold_in(keys[15], 71), 0),
        "seq_assign": draw_seq_assign(jax.random.fold_in(keys[15], 71), 0),
        "norm1_gain": jnp.clip(1.0 + 0.15 * jax.random.normal(keys[3], (D,), jnp.float32), 0.25, 1.75),
        "w_query": scatter_about(keys[4], (D, D), D ** -0.5, 0.15625, ((0, 8), (1, 4))),
        "w_key": scatter_about(keys[5], (D, D), D ** -0.5, 0.15625, ((0, 8), (1, 4))),
        "w_value": scatter_about(keys[6], (D, D), D ** -0.5, 0.15625, ((0, 8), (1, 4))),
        "w_forget": scatter_about(keys[7], (D, HEADS), D ** -0.5, 0.15625, ((0, 8), (1, 4))),
        "forget_bias": jnp.clip(jnp.exp(jax.random.uniform(keys[8], (HEADS,), jnp.float32, math.log(3.0), math.log(9.0))), 3.0, 9.0),
        "w_out": scatter_about(keys[9], (D, D), (D // 32) ** -0.5, 0.875, ((0, 4), (1, 8))),
        "norm2_gain": jnp.clip(1.0 + 0.15 * jax.random.normal(keys[10], (D,), jnp.float32), 0.25, 1.75),
        "w_gate": scatter_about(keys[11], (D, FF), D ** -0.5, 0.15625, ((0, 8), (1, 4))),
        "w_up": scatter_about(keys[12], (D, FF), D ** -0.5, 0.15625, ((0, 8), (1, 4))),
        "w_down": scatter_about(keys[13], (FF, D), (FF // 4) ** -0.5, 0.1875, ((0, 4), (1, 8))),
        "out_grad": scatter_about(keys[14], (MICRO, ROWS, D), 1.0, 6.0, ((1, 32),)),
    }


@jax.custom_vjp
def low(v):
    return lax.optimization_barrier(v.astype(jnp.bfloat16)).astype(jnp.float32)

@jax.custom_vjp
def low_back(v):
    return v

def low_keep(v):
    return (low(v), None)

def low_pass(kept, grad):
    return (grad,)

def back_keep(v):
    return (v, None)

def back_low(kept, grad):
    return (low(grad),)
low.defvjp(low_keep, low_pass)
low_back.defvjp(back_keep, back_low)
EPS = 1e-06
NEG_BIG = -1e+30
HIGH = lax.Precision.HIGHEST

def row_scale(tokens):
    return lax.rsqrt(lax.optimization_barrier(jnp.mean(tokens * tokens, axis=-1, keepdims=True)) + EPS)

def product(left, right):
    return jnp.dot(left, right, precision=HIGH, preferred_element_type=jnp.float32)

def layer_forward(params, rows_in, valid_rows):
    gain_one, w_query, w_key, w_value, w_forget, forget_bias, w_out, gain_two, w_gate, w_up, w_down = params
    seq_rows = rows_in.shape[0]
    normed_one = low(rows_in * row_scale(rows_in) * gain_one)
    queries = low(low_back(product(normed_one, w_query))).reshape(seq_rows, HEADS, HEAD_DIM)
    key_rows = low(low_back(product(normed_one, w_key))).reshape(seq_rows, HEADS, HEAD_DIM)
    value_rows = low(low_back(product(normed_one, w_value))).reshape(seq_rows, HEADS, HEAD_DIM)
    forget_logit = low_back(product(normed_one, w_forget)) + forget_bias
    cumul_gate = jnp.cumsum(jax.nn.log_sigmoid(forget_logit), axis=0)
    raw_dot = low_back(0.125 * jnp.einsum('ihd,jhd->hij', queries, key_rows, precision=HIGH))
    scores = raw_dot + cumul_gate.T[:, :, None] - cumul_gate.T[:, None, :]
    positions = jnp.arange(seq_rows)
    allowed = (positions[None, :] <= positions[:, None]) & (valid_rows[None, :] > 0.5)
    scores = jnp.where(allowed[None], scores, NEG_BIG)
    attn_probs = low(jax.nn.softmax(scores, axis=-1))
    mixed = jnp.einsum('hij,jhd->ihd', attn_probs, value_rows, precision=HIGH).reshape(seq_rows, D)
    mixed = low(low_back(mixed * valid_rows[:, None]))
    hidden_in = rows_in + low_back(product(mixed, w_out))
    normed_two = low(hidden_in * row_scale(hidden_in) * gain_two)
    gate_pre = low_back(product(normed_two, w_gate))
    up_pre = low_back(product(normed_two, w_up))
    inner = low(jax.nn.silu(gate_pre) * up_pre)
    return valid_rows[:, None] * (hidden_in + low_back(product(inner, w_down)))

def reference(inputs, seq_lengths, seq_assign, norm1_gain, w_query, w_key, w_value, w_forget, forget_bias, w_out, norm2_gain, w_gate, w_up, w_down, out_grad):
    params = tuple((item.astype(jnp.float32) for item in (norm1_gain, w_query, w_key, w_value, w_forget, forget_bias, w_out, norm2_gain, w_gate, w_up, w_down)))
    block_lengths = seq_lengths[seq_assign].reshape(MICRO * N_DP)
    seq_inputs = inputs.astype(jnp.float32).reshape(MICRO * N_DP, SLOTS, D)
    seq_cot = out_grad.astype(jnp.float32).reshape(MICRO * N_DP, SLOTS, D)

    def one_sequence(grad_sum, entry):
        rows_in, cotangent, length = entry
        valid_rows = (jnp.arange(SLOTS) < length).astype(jnp.float32)
        result, pullback = jax.vjp(lambda weights, tokens: layer_forward(weights, tokens, valid_rows), params, rows_in)
        weight_grads, token_grad = pullback(cotangent)
        grad_sum = jax.tree.map(jnp.add, grad_sum, weight_grads)
        return (grad_sum, (result.astype(jnp.bfloat16), token_grad.astype(jnp.bfloat16)))
    zero_grads = jax.tree.map(jnp.zeros_like, params)
    grad_sum, (seq_out, seq_grad) = lax.scan(one_sequence, zero_grads, (seq_inputs, seq_cot, block_lengths))
    outputs = seq_out.reshape(MICRO, N_DP * SLOTS, D)
    input_grad = seq_grad.reshape(MICRO, N_DP * SLOTS, D)
    return (outputs, input_grad, grad_sum[0], grad_sum[1], grad_sum[2], grad_sum[3], grad_sum[4], grad_sum[5], grad_sum[6], grad_sum[7], grad_sum[8], grad_sum[9], grad_sum[10])
```

```python
import functools

import jax
import jax.numpy as jnp
from jax import lax
from jax.experimental import pallas as pl
from jax.experimental.pallas import tpu as pltpu
from jax.sharding import PartitionSpec as P

EPS = 1e-06
NEG_BIG = -1e30
F32 = jnp.float32
BF16 = jnp.bfloat16
FORGET_PAD = 16
UNIT_BLOCK = 256
VMEM_BYTES = 60 << 20


def row_scale(tokens):
    return lax.rsqrt(jnp.mean(tokens * tokens, axis=-1, keepdims=True) + EPS)


def norm_back(tokens, scaling, gain, grad_out):
    weighted = grad_out * gain
    cubed = scaling * scaling * scaling
    return scaling * weighted - tokens * cubed * jnp.mean(weighted * tokens, axis=-1, keepdims=True)


def dot_first(left, right):
    return lax.dot_general(left, right, (((0,), (0,)), ((), ())), preferred_element_type=F32)

def nt(a, b):
    return lax.dot_general(a, b, (((1,), (1,)), ((), ())), preferred_element_type=F32)

def nn(a, b):
    return lax.dot_general(a, b, (((1,), (0,)), ((), ())), preferred_element_type=F32)

def pieces(x):
    top = x.astype(BF16).astype(F32)
    rest = x - top
    mid = rest.astype(BF16).astype(F32)
    return top, mid, rest - mid

def side(lane, base, values, rest):
    for n, value in enumerate(values):
        rest = jnp.where(lane == base + n, value, rest)
    return rest

def gate_column(c_ref, which, length, rows):
    col = c_ref[0, :, which : which + 1]
    pos = lax.broadcasted_iota(jnp.int32, (rows, 1), 0)
    return jnp.where(pos < length, -col, NEG_BIG)

def attn_fwd_kernel(len_ref, q_ref, k_ref, v_ref, c_ref, o_ref, l_ref, *, blk):
    rows, wide = q_ref.shape
    hd = wide // 2
    length = len_ref[0]
    lane = lax.broadcasted_iota(jnp.int32, (rows, wide), 1)
    lane_b = lax.broadcasted_iota(jnp.int32, (blk, wide), 1)
    q = q_ref[...].astype(F32) * 0.125
    k = k_ref[...].astype(F32)
    v = v_ref[...].astype(F32)
    heads = []
    for h in range(2):
        inside = (lane < hd) if h == 0 else (lane >= hd)
        base = hd if h == 0 else 0
        bias = jnp.broadcast_to(gate_column(c_ref, h, length, rows), (rows, wide))
        kx = jnp.where(inside, k, side(lane, base, pieces(bias), 0.0)).astype(BF16)
        qx = jnp.where(inside, q, side(lane, base, (1.0, 1.0, 1.0), 0.0)).astype(BF16)
        vx = jnp.where(inside, v, 1.0).astype(BF16)
        heads.append((qx, kx, vx))
    tri = lax.broadcasted_iota(jnp.int32, (blk, blk), 1) <= lax.broadcasted_iota(jnp.int32, (blk, blk), 0)
    for i in range(rows // blk):
        lo, hi = i * blk, (i + 1) * blk
        got = []
        for h in range(2):
            qx, kx, vx = heads[h]
            s_d = jnp.where(tri, nt(qx[lo:hi], kx[lo:hi]), NEG_BIG)
            m = jnp.max(s_d, axis=1, keepdims=True)
            if i:
                s_o = nt(qx[lo:hi], kx[:lo])
                m = jnp.maximum(m, jnp.max(s_o, axis=1, keepdims=True))
            r = nn(jnp.exp(s_d - m).astype(BF16), vx[lo:hi])
            if i:
                r = r + nn(jnp.exp(s_o - m).astype(BF16), vx[:lo])
            total = pltpu.roll(r, hd, 1)
            got.append((r / total, m + jnp.log(total)))
        pos = lo + lax.broadcasted_iota(jnp.int32, (blk, wide), 0)
        o = jnp.where(lane_b < hd, got[0][0], got[1][0])
        o_ref[lo:hi, :] = jnp.where(pos < length, o, 0.0).astype(BF16)
        l_ref[lo:hi, :] = jnp.where(lane_b < hd, got[0][1], got[1][1])

def attn_fwd(length, q, k, v, c, blk=256):
    rows, cols = q.shape
    pairs = cols // 128
    spec = pl.BlockSpec((rows, 128), lambda p: (0, p))
    return pl.pallas_call(
        functools.partial(attn_fwd_kernel, blk=blk),
        grid=(pairs,),
        in_specs=[pl.BlockSpec(memory_space=pltpu.SMEM), spec, spec, spec,
                  pl.BlockSpec((1, rows, 2), lambda p: (p, 0, 0))],
        out_specs=[spec, spec],
        out_shape=[jax.ShapeDtypeStruct((rows, cols), BF16), jax.ShapeDtypeStruct((rows, cols), F32)],
        compiler_params=pltpu.CompilerParams(vmem_limit_bytes=VMEM_BYTES),
        cost_estimate=pl.CostEstimate(flops=rows*rows*128*4*pairs*2, bytes_accessed=rows*cols*12, transcendentals=rows*rows*pairs),
    )(length, q, k, v, c)

def attn_bwd_kernel(len_ref, q_ref, k_ref, v_ref, c_ref, l_ref, o_ref, g_ref, dq_ref, dk_ref, dv_ref, dc_ref, acc_k, acc_v, *, blk):
    rows, wide = q_ref.shape
    hd = wide // 2
    length = len_ref[0]
    lane = lax.broadcasted_iota(jnp.int32, (rows, wide), 1)
    q = q_ref[...].astype(F32) * 0.125
    k = k_ref[...].astype(F32)
    v = v_ref[...].astype(F32)
    g = g_ref[...].astype(F32)
    go = g * o_ref[...].astype(F32)
    tri = lax.broadcasted_iota(jnp.int32, (blk, blk), 0) <= lax.broadcasted_iota(jnp.int32, (blk, blk), 1)
    res = []
    for h in range(2):
        inside = (lane < hd) if h == 0 else (lane >= hd)
        base = hd if h == 0 else 0
        bias = jnp.broadcast_to(gate_column(c_ref, h, length, rows), (rows, wide))
        logt = l_ref[...]
        logt = jnp.where(inside, pltpu.roll(logt, hd, 1), logt)
        other = pltpu.roll(l_ref[...], hd, 1)
        logt = jnp.where(inside, l_ref[...], other)
        dot_o = jnp.broadcast_to(jnp.sum(jnp.where(inside, go, 0.0), axis=1, keepdims=True), (rows, wide))
        kx = jnp.where(inside, k, side(lane, base, pieces(bias) + (1.0, 1.0, 1.0), 0.0)).astype(BF16)
        qx = jnp.where(inside, q, side(lane, base, (1.0, 1.0, 1.0) + pieces(-logt), 0.0)).astype(BF16)
        vx = jnp.where(inside, v, side(lane, base, (1.0, 1.0, 1.0), 0.0)).astype(BF16)
        gx = jnp.where(inside, g, side(lane, base, pieces(-dot_o), 0.0)).astype(BF16)
        kt = kx.T
        dq_parts = []
        for i in range(rows // blk):
            lo, hi = i * blk, (i + 1) * blk
            dqt = None
            for a, b, diag in ((lo, hi, True),) + (((0, lo, False),) if i else ()):
                s = nt(kx[a:b], qx[lo:hi])
                if diag:
                    s = jnp.where(tri, s, NEG_BIG)
                p = jnp.exp(s)
                ds = (p * nt(vx[a:b], gx[lo:hi])).astype(BF16)
                dv = nn(p.astype(BF16), g_ref[lo:hi, :])
                dk = nn(ds, qx[lo:hi])
                t = nn(kt[:, a:b], ds)
                dqt = t if dqt is None else dqt + t
                if diag:
                    acc_v[a:b, :] = dv
                    acc_k[a:b, :] = dk
                else:
                    acc_v[a:b, :] += dv
                    acc_k[a:b, :] += dk
            dq_parts.append(dqt.T)
        dq = jnp.concatenate(dq_parts, axis=0)
        dk = acc_k[...]
        res.append((dq, dk, acc_v[...], dq - pltpu.roll(dk, 3, 1)))
    first = lane < hd
    dq_ref[...] = jnp.where(first, res[0][0] * 0.125, res[1][0] * 0.125).astype(BF16)
    dk_ref[...] = jnp.where(first, res[0][1], res[1][1]).astype(BF16)
    dv_ref[...] = jnp.where(first, res[0][2], res[1][2]).astype(BF16)
    dc_ref[...] = jnp.where(first, res[1][3], res[0][3])

def attn_bwd(length, q, k, v, c, l, o, g, blk=256):
    rows, cols = q.shape
    pairs = cols // 128
    spec = pl.BlockSpec((rows, 128), lambda p: (0, p))
    low = jax.ShapeDtypeStruct((rows, cols), BF16)
    dq, dk, dv, dc = pl.pallas_call(
        functools.partial(attn_bwd_kernel, blk=blk),
        grid=(pairs,),
        in_specs=[pl.BlockSpec(memory_space=pltpu.SMEM), spec, spec, spec,
                  pl.BlockSpec((1, rows, 2), lambda p: (p, 0, 0)), spec, spec, spec],
        out_specs=[spec]*4,
        out_shape=[low, low, low, jax.ShapeDtypeStruct((rows, cols), F32)],
        scratch_shapes=[pltpu.VMEM((rows, 128), F32)]*2,
        compiler_params=pltpu.CompilerParams(vmem_limit_bytes=VMEM_BYTES),
        cost_estimate=pl.CostEstimate(flops=rows*rows*128*10*pairs*2, bytes_accessed=rows*cols*24, transcendentals=rows*rows*pairs),
    )(length, q, k, v, c, l, o, g)
    d3 = dc.reshape(rows, pairs, 128)
    grad_cumul = jnp.stack([d3[:, :, 67], d3[:, :, 3]], axis=2).reshape(rows, 2 * pairs)
    return dq, dk, dv, grad_cumul


def whole(array):
    return pl.BlockSpec(array.shape, lambda *_: (0,) * array.ndim, pipeline_mode=pl.Buffered(1))


def cost(flops, arrays, more=0):
    size = sum(a.size * a.dtype.itemsize for a in arrays)
    return pl.CostEstimate(flops=flops, bytes_accessed=size + more, transcendentals=0)


def joined(refs, lo=None, hi=None):
    if lo is None:
        return jnp.concatenate([r[...] for r in refs], axis=1)
    return jnp.concatenate([r[lo:hi, :] for r in refs], axis=1)


def project_kernel(x_ref, *refs, shard):
    w_refs, (q_ref, k_ref, v_ref, f_ref) = refs[:-4], refs[-4:]
    step = w_refs[0].shape[0] // 2
    x = x_ref[...]
    for kind, out in enumerate((q_ref, k_ref, v_ref)):
        rows = [joined(w_refs, t * step + kind * shard, t * step + (kind + 1) * shard) for t in range(2)]
        out[...] = nt(x, jnp.concatenate(rows, axis=0)).astype(BF16)
    rows = [joined(w_refs, t * step + 3 * shard, (t + 1) * step) for t in range(2)]
    f_ref[0] = nt(x, jnp.concatenate(rows, axis=0))


def project(x, weights, shard, few):
    rows = x.shape[0]
    step = weights[0].shape[0] // 2
    low = jax.ShapeDtypeStruct((rows, 4 * shard), BF16)
    spec = pl.BlockSpec((rows, 2 * shard), lambda i: (0, i))
    pad = step // 2 - 3 * shard
    q, k, v, f = pl.pallas_call(
        functools.partial(project_kernel, shard=shard),
        grid=(2,),
        in_specs=[whole(x)]
        + [pl.BlockSpec((step, w.shape[1]), lambda i: (i, 0)) for w in weights],
        out_specs=[spec, spec, spec, pl.BlockSpec((1, rows, 2 * pad), lambda i: (i, 0, 0))],
        out_shape=[low, low, low, jax.ShapeDtypeStruct((2, rows, 2 * pad), F32)],
        compiler_params=pltpu.CompilerParams(vmem_limit_bytes=VMEM_BYTES),
        cost_estimate=cost(2 * rows * x.shape[1] * 4 * step // 2, [x, *weights, low, low, low]),
        name="project",
    )(x, *weights)
    logits = f.reshape(2, rows, 2, pad)[..., :few].transpose(1, 0, 2, 3).reshape(rows, 4 * few)
    return q, k, v, logits


def combine_kernel(core_ref, left_ref, *refs):
    w_refs, (give_ref, keep_ref) = refs[:-2], refs[-2:]
    step = pl.program_id(0)
    wide = w_refs[0].shape[1]
    for out, cond in ((give_ref, step < 2), (keep_ref, step >= 2)):

        @pl.when(cond)
        def _():
            for n, w in enumerate(w_refs):
                out[:, n * wide : (n + 1) * wide] = nn(left_ref[...], w[...]).astype(out.dtype)


def combine(core, left, weights):
    rows = left.shape[0]
    wide = weights[0].shape[1] * len(weights)
    block = rows // 4

    def place(i, core_ref):
        mine = core_ref[0]
        return (jnp.where(i < 2, (1 - mine) * 2 + i, mine * 2 + i - 2), 0)

    outs = [
        jax.ShapeDtypeStruct((rows // 2, wide), BF16),
        jax.ShapeDtypeStruct((rows // 2, wide), F32),
    ]
    return pl.pallas_call(
        combine_kernel,
        grid_spec=pltpu.PrefetchScalarGridSpec(
            num_scalar_prefetch=1,
            grid=(4,),
            in_specs=[pl.BlockSpec((block, left.shape[1]), place)] + [whole(w) for w in weights],
            out_specs=[
                pl.BlockSpec((block, wide), lambda i, c: (jnp.minimum(i, 1), 0)),
                pl.BlockSpec((block, wide), lambda i, c: (jnp.maximum(i - 2, 0), 0)),
            ],
        ),
        out_shape=outs,
        compiler_params=pltpu.CompilerParams(vmem_limit_bytes=VMEM_BYTES),
        cost_estimate=cost(2 * rows * left.shape[1] * wide, [left, *weights, *outs]),
        name="combine",
    )(core.reshape(1), left, *weights)


def spread_kernel(len_ref, x_ref, *refs):
    w_refs, out_ref = refs[:-1], refs[-1]
    rows = x_ref.shape[0]
    got = nt(x_ref[...], joined(w_refs))
    pos = pl.program_id(0) * rows + lax.broadcasted_iota(jnp.int32, got.shape, 0)
    out_ref[...] = jnp.where(pos < len_ref[0], got, 0.0).astype(BF16)


def spread(length, x, weights):
    rows, wide = x.shape[0], weights[0].shape[0]
    block = rows // 4
    out = jax.ShapeDtypeStruct((rows, wide), BF16)
    return pl.pallas_call(
        spread_kernel,
        grid=(4,),
        in_specs=[
            pl.BlockSpec(memory_space=pltpu.SMEM),
            pl.BlockSpec((block, x.shape[1]), lambda i: (i, 0)),
        ]
        + [whole(w) for w in weights],
        out_specs=pl.BlockSpec((block, wide), lambda i: (i, 0)),
        out_shape=out,
        compiler_params=pltpu.CompilerParams(vmem_limit_bytes=VMEM_BYTES),
        cost_estimate=cost(2 * rows * x.shape[1] * wide, [x, *weights, out]),
        name="spread",
    )(length, x, *weights)


def inner_kernel(x_ref, *refs):
    w_refs, (gate_ref, up_ref, inner_ref) = refs[:-3], refs[-3:]
    both = nt(x_ref[...], joined(w_refs))
    gate, up = both[:, :UNIT_BLOCK], both[:, UNIT_BLOCK:]
    gate_ref[...] = gate
    up_ref[...] = up
    inner_ref[...] = (gate * jax.nn.sigmoid(gate) * up).astype(BF16)


def inner_units(x, weights):
    rows = x.shape[0]
    total = weights[0].shape[0] // 2
    spec = pl.BlockSpec((rows, UNIT_BLOCK), lambda i: (0, i))
    outs = [jax.ShapeDtypeStruct((rows, total), t) for t in (F32, F32, BF16)]
    return pl.pallas_call(
        inner_kernel,
        grid=(total // UNIT_BLOCK,),
        in_specs=[whole(x)]
        + [pl.BlockSpec((2 * UNIT_BLOCK, w.shape[1]), lambda i: (i, 0)) for w in weights],
        out_specs=[spec] * 3,
        out_shape=outs,
        compiler_params=pltpu.CompilerParams(vmem_limit_bytes=VMEM_BYTES),
        cost_estimate=cost(4 * rows * x.shape[1] * total, [x, *weights, *outs]),
        name="inner_units",
    )(x, *weights)


def inner_back_kernel(core_ref, x_ref, gate_ref, up_ref, *refs):
    pieces_here = (len(refs) - 4) // 2
    down_refs, two_refs = refs[:pieces_here], refs[pieces_here : 2 * pieces_here]
    pre_ref, give_ref, keep_ref, total = refs[2 * pieces_here :]
    step = pl.program_id(0)
    grad = nt(x_ref[...], joined(down_refs))
    gate, up = gate_ref[...], up_ref[...]
    sig = jax.nn.sigmoid(gate)
    grad_gate = (grad * up * (sig * (1.0 + gate * (1.0 - sig)))).astype(BF16)
    grad_up = (grad * (gate * sig)).astype(BF16)
    pre = jnp.concatenate([grad_gate, grad_up], axis=1)
    pre_ref[...] = pre
    wide = two_refs[0].shape[1]
    for n, w in enumerate(two_refs):
        cols = slice(n * wide, (n + 1) * wide)
        part = nn(pre, w[...])

        @pl.when(step == 0)
        def _():
            total[:, cols] = part

        @pl.when(step > 0)
        def _():
            total[:, cols] += part

    @pl.when(step == pl.num_programs(0) - 1)
    def _():
        half = give_ref.shape[0]
        core = core_ref[0]
        give_ref[...] = total[pl.ds(pl.multiple_of((1 - core) * half, half), half), :].astype(BF16)
        keep_ref[...] = total[pl.ds(pl.multiple_of(core * half, half), half), :]


def inner_back(core, x, gate, up, down, two):
    rows, cols = x.shape
    total = gate.shape[1]
    spec = pl.BlockSpec((rows, UNIT_BLOCK), lambda i: (0, i))
    outs = [
        jax.ShapeDtypeStruct((rows, 2 * total), BF16),
        jax.ShapeDtypeStruct((rows // 2, cols), BF16),
        jax.ShapeDtypeStruct((rows // 2, cols), F32),
    ]
    return pl.pallas_call(
        inner_back_kernel,
        grid=(total // UNIT_BLOCK,),
        in_specs=[pl.BlockSpec(memory_space=pltpu.SMEM), whole(x), spec, spec]
        + [pl.BlockSpec((UNIT_BLOCK, w.shape[1]), lambda i: (i, 0)) for w in down]
        + [pl.BlockSpec((2 * UNIT_BLOCK, w.shape[1]), lambda i: (i, 0)) for w in two],
        out_specs=[
            pl.BlockSpec((rows, 2 * UNIT_BLOCK), lambda i: (0, i)),
            whole(outs[1]),
            whole(outs[2]),
        ],
        out_shape=outs,
        scratch_shapes=[pltpu.VMEM((rows, cols), F32)],
        compiler_params=pltpu.CompilerParams(vmem_limit_bytes=VMEM_BYTES),
        cost_estimate=cost(6 * rows * cols * total, [x, gate, up, *down, *two, *outs]),
        name="inner_back",
    )(core.reshape(1), x, gate, up, *down, *two)


class Plan:
    def __init__(self, ways_dp, ways_tensor):
        self.ways_dp = ways_dp
        self.ways_tensor = ways_tensor
        self.chips = ways_dp // 2
        self.bits = self.chips.bit_length() - 1
        assert self.chips == 1 << self.bits and ways_tensor == 4
        dp = lax.axis_index("dp")
        self.chip = dp // 2
        self.core = dp % 2
        self.place = lax.axis_index("tensor")
        self.core_perm = [(i, i ^ 1) for i in range(ways_dp)]

    def swap_core(self, array):
        return lax.ppermute(array, "dp", self.core_perm)

    def swap_chip(self, array, bit):
        perm = [(i, i ^ (2 << bit)) for i in range(self.ways_dp)]
        return lax.ppermute(array, "dp", perm)

    def route(self, turn):
        pairs = []
        for chip in range(self.chips):
            for core in range(2):
                for z in range(4):
                    micro = (z + turn) % 2
                    source = (2 * chip + core) * 4 + z
                    target = (2 * chip + z // 2) * 4 + 2 * micro + core
                    pairs.append((source, target))
        return pairs

    def by_chip(self, array):
        lead = array.shape[:-1]
        wide = array.shape[-1] // self.chips
        parts = [
            lax.dynamic_slice_in_dim(array, (self.chip ^ r) * wide, wide, axis=-1)
            for r in range(self.chips)
        ]
        return jnp.concatenate(parts, axis=-1).reshape(*lead, -1)

    def to_chip(self, array):
        got = []
        for turn in range(2):
            micro = (self.place + turn) % 2
            part = lax.dynamic_index_in_dim(array, micro, 0, keepdims=False)
            got.append(lax.ppermute(self.by_chip(part), ("dp", "tensor"), self.route(turn)))
        first = self.place // 2 == 0
        return jnp.concatenate(
            [jnp.where(first, got[0], got[1]), jnp.where(first, got[1], got[0])], axis=0
        )

    def from_chip(self, array):
        rows = array.shape[0] // 2
        got = []
        for turn in range(2):
            block = (self.place // 2 + turn) % 2
            part = lax.dynamic_slice_in_dim(array, block * rows, rows, axis=0)
            back = [(b, a) for a, b in self.route(turn)]
            got.append(lax.ppermute(self.by_chip(part), ("dp", "tensor"), back))
        first = self.place % 2 == 0
        return jnp.stack([jnp.where(first, got[0], got[1]), jnp.where(first, got[1], got[0])])

    def both_rows(self, half):
        other = self.swap_core(half)
        first = self.core == 0
        return jnp.concatenate(
            [jnp.where(first, half, other), jnp.where(first, other, half)], axis=0
        )

    def sum_rows(self, give, keep):
        return keep + self.swap_core(give).astype(F32)

    def line_gather(self, shard):
        mine = lax.dynamic_index_in_dim(shard, self.core, 0, keepdims=False)
        theirs = lax.dynamic_index_in_dim(shard, 1 - self.core, 0, keepdims=False)
        other = self.swap_core(theirs)
        first = self.core == 0
        pair = jnp.concatenate(
            [jnp.where(first, mine, other), jnp.where(first, other, mine)], axis=1
        )
        return lax.all_gather(pair, "tensor", axis=0, tiled=True)

    def chip_gather(self, own):
        half = own.shape[0] // 2
        if self.bits == 2:
            by_x = self.swap_chip(own, 0)
            by_y = self.swap_chip(own, 1)
            far_top = self.swap_chip(by_x[:half], 1)
            far_low = self.swap_chip(by_y[half:], 0)
            return [own, by_x, by_y, jnp.concatenate([far_top, far_low], axis=0)]
        parts = [own]
        for bit in range(self.bits):
            parts = parts + [self.swap_chip(p, bit) for p in parts]
        return [jnp.concatenate(parts, axis=1)]

    def reduce_weight(self, left, right):
        wide = right.shape[1] // self.chips
        rows = left.shape[1]
        half = rows // 2

        def term(r, lo=0, hi=rows):
            return dot_first(left[:, lo:hi], right[:, r * wide : (r + 1) * wide])

        if self.bits == 2:
            far_top = self.swap_chip(term(3, 0, half).astype(BF16), 1)
            far_low = self.swap_chip(term(3, half, rows).astype(BF16), 0)
            send_x = jnp.concatenate(
                [
                    (term(1, 0, half) + far_top.astype(F32)).astype(BF16),
                    term(1, half, rows).astype(BF16),
                ],
                axis=0,
            )
            send_y = jnp.concatenate(
                [
                    term(2, 0, half).astype(BF16),
                    (term(2, half, rows) + far_low.astype(F32)).astype(BF16),
                ],
                axis=0,
            )
            by_x = self.swap_chip(send_x, 0)
            by_y = self.swap_chip(send_y, 1)
            total = term(0) + by_x.astype(F32) + by_y.astype(F32)
        else:
            parts = [term(r) for r in range(self.chips)]
            for bit in reversed(range(self.bits)):
                keep, give = parts[: 1 << bit], parts[1 << bit :]
                parts = [
                    k + self.swap_chip(g.astype(BF16), bit).astype(F32) for k, g in zip(keep, give)
                ]
            total = parts[0]
        pair = lax.psum_scatter(total.astype(BF16), "tensor", scatter_dimension=0, tiled=True)
        narrow = wide // 2
        mine = lax.dynamic_slice_in_dim(pair, self.core * narrow, narrow, axis=1)
        theirs = lax.dynamic_slice_in_dim(pair, (1 - self.core) * narrow, narrow, axis=1)
        other = self.swap_core(theirs)
        first = self.core == 0
        return jnp.stack([jnp.where(first, mine, other), jnp.where(first, other, mine)]).astype(F32)

    def sum_all(self, vector):
        vector = vector + self.swap_core(vector)
        for bit in range(self.bits):
            vector = vector + self.swap_chip(vector, bit)
        for bit in range(2):
            perm = [(z, z ^ (1 << bit)) for z in range(4)]
            vector = vector + lax.ppermute(vector, "tensor", perm)
        return vector


def split_columns(matrix):
    return matrix.T.reshape(2, matrix.shape[1] // 2, matrix.shape[0])


def split_rows(matrix):
    return matrix.reshape(2, matrix.shape[0] // 2, matrix.shape[1])


def body(
    inputs,
    seq_lengths,
    seq_assign,
    norm1_gain,
    w_query,
    w_key,
    w_value,
    w_forget,
    forget_bias,
    w_out,
    norm2_gain,
    w_gate,
    w_up,
    w_down,
    out_grad,
):
    plan = Plan(lax.axis_size("dp"), lax.axis_size("tensor"))
    core, place = plan.core, plan.place
    part_rows = inputs.shape[1]
    seq_rows = part_rows * 4
    half_rows = seq_rows // 2
    heads_shard = w_forget.shape[1] // 2
    heads_here = heads_shard * 4
    shard_cols = w_query.shape[1] // 2
    blocks = w_gate.shape[1] // 2 // UNIT_BLOCK

    def by_block(matrix):
        return split_columns(matrix).reshape(2, blocks, 1, UNIT_BLOCK, matrix.shape[0])

    forget_part = jnp.pad(
        split_columns(w_forget), ((0, 0), (0, FORGET_PAD - heads_shard), (0, 0))
    )
    line_one = plan.line_gather(
        jnp.concatenate(
            [split_columns(w_query), split_columns(w_key), split_columns(w_value), forget_part],
            axis=1,
        )
    )
    full_one = plan.chip_gather(line_one)
    rows_in = plan.to_chip(inputs).astype(F32)
    two_part = jnp.concatenate([by_block(w_gate), by_block(w_up)], axis=2)
    line_mid = plan.line_gather(
        jnp.concatenate(
            [split_rows(w_out), two_part.reshape(2, -1, two_part.shape[-1])], axis=1
        )
    )
    line_mid = line_mid.reshape(4, -1, line_mid.shape[-1])
    full_out = plan.chip_gather(line_mid[:, :shard_cols].reshape(4 * shard_cols, -1))
    full_two = plan.chip_gather(
        line_mid[:, shard_cols:].reshape(-1, line_mid.shape[-1])
    )
    full_down = plan.chip_gather(plan.line_gather(split_rows(w_down)))
    cotangent = plan.to_chip(out_grad).astype(F32)

    other_assign = plan.swap_core(seq_assign)
    assign_both = jnp.where(
        core == 0,
        jnp.concatenate([seq_assign, other_assign], axis=1),
        jnp.concatenate([other_assign, seq_assign], axis=1),
    ).reshape(4)
    seq_id = jnp.sum(jnp.where(jnp.arange(4) == place, assign_both, 0))
    length = jnp.sum(jnp.where(jnp.arange(seq_lengths.shape[0]) == seq_id, seq_lengths, 0))
    count = length.reshape(1)
    valid_here = (core * half_rows + jnp.arange(half_rows) < length).astype(F32)[:, None]

    gain_one = plan.by_chip(norm1_gain)
    gain_two = plan.by_chip(norm2_gain)
    bias_here = lax.dynamic_index_in_dim(
        forget_bias.reshape(4, 2, heads_shard), core, 1, keepdims=False
    ).reshape(-1)

    scale_one = row_scale(rows_in)
    normed_one = plan.both_rows((rows_in * scale_one * gain_one).astype(BF16))
    queries, key_rows, value_rows, logits = project(normed_one, full_one, shard_cols, heads_shard)
    forget_logit = logits + bias_here
    cumul_gate = jnp.cumsum(jax.nn.log_sigmoid(forget_logit), axis=0)
    gate_pairs = cumul_gate.reshape(seq_rows, heads_here // 2, 2).transpose(1, 0, 2)
    mixed_low, log_total = attn_fwd(count, queries, key_rows, value_rows, gate_pairs)
    hidden_in = rows_in + plan.sum_rows(*combine(core, mixed_low, full_out))

    scale_two = row_scale(hidden_in)
    normed_two = plan.both_rows((hidden_in * scale_two * gain_two).astype(BF16))
    gate_pre, up_pre, inner_low = inner_units(normed_two, full_two)
    grad_ffn = plan.both_rows((valid_here * cotangent).astype(BF16))
    down_shard = plan.reduce_weight(inner_low, grad_ffn)
    ffn_rows = plan.sum_rows(*combine(core, inner_low, full_down))
    outputs = plan.from_chip((valid_here * (hidden_in + ffn_rows)).astype(BF16))

    grad_pre, give_two, keep_two = inner_back(
        core, grad_ffn, gate_pre, up_pre, full_down, full_two
    )
    two_shard = plan.reduce_weight(grad_pre, normed_two)
    grad_normed_two = plan.sum_rows(give_two, keep_two)
    gain_two_term = jnp.sum(grad_normed_two * hidden_in * scale_two, axis=0)
    grad_hidden = valid_here * cotangent + norm_back(
        hidden_in, scale_two, gain_two, grad_normed_two
    )

    grad_attn = plan.both_rows(grad_hidden.astype(BF16))
    out_shard = plan.reduce_weight(mixed_low, grad_attn)
    grad_mixed = spread(count, grad_attn, full_out)
    query_low, key_low, value_low, grad_cumul = attn_bwd(
        count, queries, key_rows, value_rows, gate_pairs, log_total, mixed_low, grad_mixed
    )
    grad_logf = jnp.flip(jnp.cumsum(jnp.flip(grad_cumul, 0), axis=0), 0)
    grad_logit = grad_logf * jax.nn.sigmoid(-forget_logit)
    bias_term = jnp.sum(grad_logit, axis=0)
    grad_one = jnp.concatenate(
        [
            query_low.reshape(seq_rows, 4, shard_cols),
            key_low.reshape(seq_rows, 4, shard_cols),
            value_low.reshape(seq_rows, 4, shard_cols),
            jnp.pad(
                grad_logit.astype(BF16).reshape(seq_rows, 4, heads_shard),
                ((0, 0), (0, 0), (0, FORGET_PAD - heads_shard)),
            ),
        ],
        axis=2,
    ).reshape(seq_rows, -1)
    one_shard = plan.reduce_weight(grad_one, normed_one)
    grad_normed_one = plan.sum_rows(*combine(core, grad_one, full_one))
    gain_one_term = jnp.sum(grad_normed_one * rows_in * scale_one, axis=0)
    input_grad = plan.from_chip(
        (grad_hidden + norm_back(rows_in, scale_one, gain_one, grad_normed_one)).astype(BF16)
    )

    bias_full = jnp.where(
        (jnp.arange(2) == core)[None, :, None], bias_term.reshape(4, 1, heads_shard), 0.0
    ).reshape(-1)
    wide = norm1_gain.shape[0]
    small = plan.sum_all(
        jnp.concatenate([plan.by_chip(gain_one_term), plan.by_chip(gain_two_term), bias_full])
    )

    two_shard = two_shard.reshape(2, blocks, 2, UNIT_BLOCK, -1)

    def columns(shard):
        return shard.reshape(-1, shard.shape[-1]).T

    def rows(shard):
        return shard.reshape(-1, shard.shape[-1])

    return (
        outputs,
        input_grad,
        small[:wide],
        columns(one_shard[:, :shard_cols]),
        columns(one_shard[:, shard_cols : 2 * shard_cols]),
        columns(one_shard[:, 2 * shard_cols : 3 * shard_cols]),
        columns(one_shard[:, 3 * shard_cols : 3 * shard_cols + heads_shard]),
        small[2 * wide :],
        rows(out_shard),
        small[wide : 2 * wide],
        columns(two_shard[:, :, 0]),
        columns(two_shard[:, :, 1]),
        rows(down_shard),
    )


def solution(mesh):
    return jax.shard_map(
        body,
        mesh=mesh,
        in_specs=(
            P(None, ("dp", "tensor"), None),
            P(),
            P(None, "dp"),
            P(),
            P("dp", "tensor"),
            P("dp", "tensor"),
            P("dp", "tensor"),
            P("dp", "tensor"),
            P(),
            P("tensor", "dp"),
            P(),
            P("dp", "tensor"),
            P("dp", "tensor"),
            P("tensor", "dp"),
            P(None, ("dp", "tensor"), None),
        ),
        out_specs=(
            P(None, ("dp", "tensor"), None),
            P(None, ("dp", "tensor"), None),
            P(),
            P("dp", "tensor"),
            P("dp", "tensor"),
            P("dp", "tensor"),
            P("dp", "tensor"),
            P(),
            P("tensor", "dp"),
            P(),
            P("dp", "tensor"),
            P("dp", "tensor"),
            P("tensor", "dp"),
        ),
        check_vma=False,
    )
```

```python
import functools

import jax
import jax.numpy as jnp
from jax import lax
from jax.experimental import pallas as pl
from jax.experimental.pallas import tpu as pltpu
from jax.sharding import PartitionSpec as P

EPS = 1e-06
NEG_BIG = -1e30
F32 = jnp.float32
BF16 = jnp.bfloat16
FORGET_PAD = 16
UNIT_BLOCK = 256
VMEM_BYTES = 60 << 20


def row_scale(tokens):
    return lax.rsqrt(jnp.mean(tokens * tokens, axis=-1, keepdims=True) + EPS)


def norm_back(tokens, scaling, gain, grad_out):
    weighted = grad_out * gain
    cubed = scaling * scaling * scaling
    return scaling * weighted - tokens * cubed * jnp.mean(weighted * tokens, axis=-1, keepdims=True)


def dot_first(left, right):
    return lax.dot_general(left, right, (((0,), (0,)), ((), ())), preferred_element_type=F32)

def nt(a, b):
    return lax.dot_general(a, b, (((1,), (1,)), ((), ())), preferred_element_type=F32)

def nn(a, b):
    return lax.dot_general(a, b, (((1,), (0,)), ((), ())), preferred_element_type=F32)

def pieces(x):
    top = x.astype(BF16).astype(F32)
    rest = x - top
    mid = rest.astype(BF16).astype(F32)
    return top, mid, rest - mid

def side(lane, base, values, rest):
    for n, value in enumerate(values):
        rest = jnp.where(lane == base + n, value, rest)
    return rest

def gate_column(c_ref, which, length, rows):
    col = c_ref[0, :, which : which + 1]
    pos = lax.broadcasted_iota(jnp.int32, (rows, 1), 0)
    return jnp.where(pos < length, -col, NEG_BIG)

def attn_fwd_kernel(len_ref, q_ref, k_ref, v_ref, c_ref, o_ref, l_ref, *, blk):
    rows, wide = q_ref.shape
    hd = wide // 2
    length = len_ref[0]
    lane = lax.broadcasted_iota(jnp.int32, (rows, wide), 1)
    lane_b = lax.broadcasted_iota(jnp.int32, (blk, wide), 1)
    q = q_ref[...].astype(F32) * 0.125
    k = k_ref[...].astype(F32)
    v = v_ref[...].astype(F32)
    heads = []
    for h in range(2):
        inside = (lane < hd) if h == 0 else (lane >= hd)
        base = hd if h == 0 else 0
        bias = jnp.broadcast_to(gate_column(c_ref, h, length, rows), (rows, wide))
        kx = jnp.where(inside, k, side(lane, base, pieces(bias), 0.0)).astype(BF16)
        qx = jnp.where(inside, q, side(lane, base, (1.0, 1.0, 1.0), 0.0)).astype(BF16)
        vx = jnp.where(inside, v, 1.0).astype(BF16)
        heads.append((qx, kx, vx))
    tri = lax.broadcasted_iota(jnp.int32, (blk, blk), 1) <= lax.broadcasted_iota(jnp.int32, (blk, blk), 0)
    for i in range(rows // blk):
        lo, hi = i * blk, (i + 1) * blk
        got = []
        for h in range(2):
            qx, kx, vx = heads[h]
            s_d = jnp.where(tri, nt(qx[lo:hi], kx[lo:hi]), NEG_BIG)
            m = jnp.max(s_d, axis=1, keepdims=True)
            if i:
                s_o = nt(qx[lo:hi], kx[:lo])
                m = jnp.maximum(m, jnp.max(s_o, axis=1, keepdims=True))
            r = nn(jnp.exp(s_d - m).astype(BF16), vx[lo:hi])
            if i:
                r = r + nn(jnp.exp(s_o - m).astype(BF16), vx[:lo])
            total = pltpu.roll(r, hd, 1)
            got.append((r / total, m + jnp.log(total)))
        pos = lo + lax.broadcasted_iota(jnp.int32, (blk, wide), 0)
        o = jnp.where(lane_b < hd, got[0][0], got[1][0])
        o_ref[lo:hi, :] = jnp.where(pos < length, o, 0.0).astype(BF16)
        l_ref[lo:hi, :] = jnp.where(lane_b < hd, got[0][1], got[1][1])

def attn_fwd(length, q, k, v, c, blk=256):
    rows, cols = q.shape
    pairs = cols // 128
    spec = pl.BlockSpec((rows, 128), lambda p: (0, p))
    return pl.pallas_call(
        functools.partial(attn_fwd_kernel, blk=blk),
        grid=(pairs,),
        in_specs=[pl.BlockSpec(memory_space=pltpu.SMEM), spec, spec, spec,
                  pl.BlockSpec((1, rows, 2), lambda p: (p, 0, 0))],
        out_specs=[spec, spec],
        out_shape=[jax.ShapeDtypeStruct((rows, cols), BF16), jax.ShapeDtypeStruct((rows, cols), F32)],
        compiler_params=pltpu.CompilerParams(vmem_limit_bytes=VMEM_BYTES),
        cost_estimate=pl.CostEstimate(flops=rows*rows*128*4*pairs*2, bytes_accessed=rows*cols*12, transcendentals=rows*rows*pairs),
    )(length, q, k, v, c)

def attn_bwd_kernel(len_ref, q_ref, k_ref, v_ref, c_ref, l_ref, o_ref, g_ref, dq_ref, dk_ref, dv_ref, dc_ref, acc_k, acc_v, *, blk):
    rows, wide = q_ref.shape
    hd = wide // 2
    length = len_ref[0]
    lane = lax.broadcasted_iota(jnp.int32, (rows, wide), 1)
    q = q_ref[...].astype(F32) * 0.125
    k = k_ref[...].astype(F32)
    v = v_ref[...].astype(F32)
    g = g_ref[...].astype(F32)
    go = g * o_ref[...].astype(F32)
    tri = lax.broadcasted_iota(jnp.int32, (blk, blk), 0) <= lax.broadcasted_iota(jnp.int32, (blk, blk), 1)
    res = []
    for h in range(2):
        inside = (lane < hd) if h == 0 else (lane >= hd)
        base = hd if h == 0 else 0
        bias = jnp.broadcast_to(gate_column(c_ref, h, length, rows), (rows, wide))
        logt = l_ref[...]
        logt = jnp.where(inside, pltpu.roll(logt, hd, 1), logt)
        other = pltpu.roll(l_ref[...], hd, 1)
        logt = jnp.where(inside, l_ref[...], other)
        dot_o = jnp.broadcast_to(jnp.sum(jnp.where(inside, go, 0.0), axis=1, keepdims=True), (rows, wide))
        kx = jnp.where(inside, k, side(lane, base, pieces(bias) + (1.0, 1.0, 1.0), 0.0)).astype(BF16)
        qx = jnp.where(inside, q, side(lane, base, (1.0, 1.0, 1.0) + pieces(-logt), 0.0)).astype(BF16)
        vx = jnp.where(inside, v, side(lane, base, (1.0, 1.0, 1.0), 0.0)).astype(BF16)
        gx = jnp.where(inside, g, side(lane, base, pieces(-dot_o), 0.0)).astype(BF16)
        kt = kx.T
        dq_parts = []
        for i in range(rows // blk):
            lo, hi = i * blk, (i + 1) * blk
            dqt = None
            for a, b, diag in ((lo, hi, True),) + (((0, lo, False),) if i else ()):
                s = nt(kx[a:b], qx[lo:hi])
                if diag:
                    s = jnp.where(tri, s, NEG_BIG)
                p = jnp.exp(s)
                ds = (p * nt(vx[a:b], gx[lo:hi])).astype(BF16)
                dv = nn(p.astype(BF16), g_ref[lo:hi, :])
                dk = nn(ds, qx[lo:hi])
                t = nn(kt[:, a:b], ds)
                dqt = t if dqt is None else dqt + t
                if diag:
                    acc_v[a:b, :] = dv
                    acc_k[a:b, :] = dk
                else:
                    acc_v[a:b, :] += dv
                    acc_k[a:b, :] += dk
            dq_parts.append(dqt.T)
        dq = jnp.concatenate(dq_parts, axis=0)
        dk = acc_k[...]
        res.append((dq, dk, acc_v[...], dq - pltpu.roll(dk, 3, 1)))
    first = lane < hd
    dq_ref[...] = jnp.where(first, res[0][0] * 0.125, res[1][0] * 0.125).astype(BF16)
    dk_ref[...] = jnp.where(first, res[0][1], res[1][1]).astype(BF16)
    dv_ref[...] = jnp.where(first, res[0][2], res[1][2]).astype(BF16)
    dc_ref[...] = jnp.where(first, res[1][3], res[0][3])

def attn_bwd(length, q, k, v, c, l, o, g, blk=256):
    rows, cols = q.shape
    pairs = cols // 128
    spec = pl.BlockSpec((rows, 128), lambda p: (0, p))
    low = jax.ShapeDtypeStruct((rows, cols), BF16)
    dq, dk, dv, dc = pl.pallas_call(
        functools.partial(attn_bwd_kernel, blk=blk),
        grid=(pairs,),
        in_specs=[pl.BlockSpec(memory_space=pltpu.SMEM), spec, spec, spec,
                  pl.BlockSpec((1, rows, 2), lambda p: (p, 0, 0)), spec, spec, spec],
        out_specs=[spec]*4,
        out_shape=[low, low, low, jax.ShapeDtypeStruct((rows, cols), F32)],
        scratch_shapes=[pltpu.VMEM((rows, 128), F32)]*2,
        compiler_params=pltpu.CompilerParams(vmem_limit_bytes=VMEM_BYTES),
        cost_estimate=pl.CostEstimate(flops=rows*rows*128*10*pairs*2, bytes_accessed=rows*cols*24, transcendentals=rows*rows*pairs),
    )(length, q, k, v, c, l, o, g)
    d3 = dc.reshape(rows, pairs, 128)
    grad_cumul = jnp.stack([d3[:, :, 67], d3[:, :, 3]], axis=2).reshape(rows, 2 * pairs)
    return dq, dk, dv, grad_cumul


def whole(array):
    return pl.BlockSpec(array.shape, lambda *_: (0,) * array.ndim, pipeline_mode=pl.Buffered(1))


def cost(flops, arrays, more=0):
    size = sum(a.size * a.dtype.itemsize for a in arrays)
    return pl.CostEstimate(flops=flops, bytes_accessed=size + more, transcendentals=0)


def joined(refs, lo=None, hi=None):
    if lo is None:
        return jnp.concatenate([r[...] for r in refs], axis=1)
    return jnp.concatenate([r[lo:hi, :] for r in refs], axis=1)


def project_kernel(x_ref, *refs, shard):
    w_refs, (q_ref, k_ref, v_ref, f_ref) = refs[:-4], refs[-4:]
    step = w_refs[0].shape[0] // 2
    x = x_ref[...]
    for kind, out in enumerate((q_ref, k_ref, v_ref)):
        rows = [joined(w_refs, t * step + kind * shard, t * step + (kind + 1) * shard) for t in range(2)]
        out[...] = nt(x, jnp.concatenate(rows, axis=0)).astype(BF16)
    rows = [joined(w_refs, t * step + 3 * shard, (t + 1) * step) for t in range(2)]
    f_ref[0] = nt(x, jnp.concatenate(rows, axis=0))


def project(x, weights, shard, few):
    rows = x.shape[0]
    step = weights[0].shape[0] // 2
    low = jax.ShapeDtypeStruct((rows, 4 * shard), BF16)
    spec = pl.BlockSpec((rows, 2 * shard), lambda i: (0, i))
    pad = step // 2 - 3 * shard
    q, k, v, f = pl.pallas_call(
        functools.partial(project_kernel, shard=shard),
        grid=(2,),
        in_specs=[whole(x)]
        + [pl.BlockSpec((step, w.shape[1]), lambda i: (i, 0)) for w in weights],
        out_specs=[spec, spec, spec, pl.BlockSpec((1, rows, 2 * pad), lambda i: (i, 0, 0))],
        out_shape=[low, low, low, jax.ShapeDtypeStruct((2, rows, 2 * pad), F32)],
        compiler_params=pltpu.CompilerParams(vmem_limit_bytes=VMEM_BYTES),
        cost_estimate=cost(2 * rows * x.shape[1] * 4 * step // 2, [x, *weights, low, low, low]),
        name="project",
    )(x, *weights)
    logits = f.reshape(2, rows, 2, pad)[..., :few].transpose(1, 0, 2, 3).reshape(rows, 4 * few)
    return q, k, v, logits


def combine_kernel(core_ref, left_ref, *refs):
    w_refs, (give_ref, keep_ref) = refs[:-2], refs[-2:]
    step = pl.program_id(0)
    wide = w_refs[0].shape[1]
    for out, cond in ((give_ref, step < 2), (keep_ref, step >= 2)):

        @pl.when(cond)
        def _():
            for n, w in enumerate(w_refs):
                out[:, n * wide : (n + 1) * wide] = nn(left_ref[...], w[...]).astype(out.dtype)


def combine(core, left, weights):
    rows = left.shape[0]
    wide = weights[0].shape[1] * len(weights)
    block = rows // 4

    def place(i, core_ref):
        mine = core_ref[0]
        return (jnp.where(i < 2, (1 - mine) * 2 + i, mine * 2 + i - 2), 0)

    outs = [
        jax.ShapeDtypeStruct((rows // 2, wide), BF16),
        jax.ShapeDtypeStruct((rows // 2, wide), F32),
    ]
    return pl.pallas_call(
        combine_kernel,
        grid_spec=pltpu.PrefetchScalarGridSpec(
            num_scalar_prefetch=1,
            grid=(4,),
            in_specs=[pl.BlockSpec((block, left.shape[1]), place)] + [whole(w) for w in weights],
            out_specs=[
                pl.BlockSpec((block, wide), lambda i, c: (jnp.minimum(i, 1), 0)),
                pl.BlockSpec((block, wide), lambda i, c: (jnp.maximum(i - 2, 0), 0)),
            ],
        ),
        out_shape=outs,
        compiler_params=pltpu.CompilerParams(vmem_limit_bytes=VMEM_BYTES),
        cost_estimate=cost(2 * rows * left.shape[1] * wide, [left, *weights, *outs]),
        name="combine",
    )(core.reshape(1), left, *weights)


def spread_kernel(len_ref, x_ref, *refs):
    w_refs, out_ref = refs[:-1], refs[-1]
    rows = x_ref.shape[0]
    got = nt(x_ref[...], joined(w_refs))
    pos = pl.program_id(0) * rows + lax.broadcasted_iota(jnp.int32, got.shape, 0)
    out_ref[...] = jnp.where(pos < len_ref[0], got, 0.0).astype(BF16)


def spread(length, x, weights):
    rows, wide = x.shape[0], weights[0].shape[0]
    block = rows // 4
    out = jax.ShapeDtypeStruct((rows, wide), BF16)
    return pl.pallas_call(
        spread_kernel,
        grid=(4,),
        in_specs=[
            pl.BlockSpec(memory_space=pltpu.SMEM),
            pl.BlockSpec((block, x.shape[1]), lambda i: (i, 0)),
        ]
        + [whole(w) for w in weights],
        out_specs=pl.BlockSpec((block, wide), lambda i: (i, 0)),
        out_shape=out,
        compiler_params=pltpu.CompilerParams(vmem_limit_bytes=VMEM_BYTES),
        cost_estimate=cost(2 * rows * x.shape[1] * wide, [x, *weights, out]),
        name="spread",
    )(length, x, *weights)


def inner_kernel(x_ref, *refs):
    w_refs, (gate_ref, up_ref, inner_ref) = refs[:-3], refs[-3:]
    both = nt(x_ref[...], joined(w_refs))
    gate, up = both[:, :UNIT_BLOCK], both[:, UNIT_BLOCK:]
    gate_ref[...] = gate
    up_ref[...] = up
    inner_ref[...] = (gate * jax.nn.sigmoid(gate) * up).astype(BF16)


def inner_units(x, weights):
    rows = x.shape[0]
    total = weights[0].shape[0] // 2
    spec = pl.BlockSpec((rows, UNIT_BLOCK), lambda i: (0, i))
    outs = [jax.ShapeDtypeStruct((rows, total), t) for t in (F32, F32, BF16)]
    return pl.pallas_call(
        inner_kernel,
        grid=(total // UNIT_BLOCK,),
        in_specs=[whole(x)]
        + [pl.BlockSpec((2 * UNIT_BLOCK, w.shape[1]), lambda i: (i, 0)) for w in weights],
        out_specs=[spec] * 3,
        out_shape=outs,
        compiler_params=pltpu.CompilerParams(vmem_limit_bytes=VMEM_BYTES),
        cost_estimate=cost(4 * rows * x.shape[1] * total, [x, *weights, *outs]),
        name="inner_units",
    )(x, *weights)


def inner_back_kernel(core_ref, x_ref, gate_ref, up_ref, *refs):
    pieces_here = (len(refs) - 4) // 2
    down_refs, two_refs = refs[:pieces_here], refs[pieces_here : 2 * pieces_here]
    pre_ref, give_ref, keep_ref, total = refs[2 * pieces_here :]
    step = pl.program_id(0)
    grad = nt(x_ref[...], joined(down_refs))
    gate, up = gate_ref[...], up_ref[...]
    sig = jax.nn.sigmoid(gate)
    grad_gate = (grad * up * (sig * (1.0 + gate * (1.0 - sig)))).astype(BF16)
    grad_up = (grad * (gate * sig)).astype(BF16)
    pre = jnp.concatenate([grad_gate, grad_up], axis=1)
    pre_ref[...] = pre
    wide = two_refs[0].shape[1]
    for n, w in enumerate(two_refs):
        cols = slice(n * wide, (n + 1) * wide)
        part = nn(pre, w[...])

        @pl.when(step == 0)
        def _():
            total[:, cols] = part

        @pl.when(step > 0)
        def _():
            total[:, cols] += part

    @pl.when(step == pl.num_programs(0) - 1)
    def _():
        half = give_ref.shape[0]
        core = core_ref[0]
        give_ref[...] = total[pl.ds(pl.multiple_of((1 - core) * half, half), half), :].astype(BF16)
        keep_ref[...] = total[pl.ds(pl.multiple_of(core * half, half), half), :]


def inner_back(core, x, gate, up, down, two):
    rows, cols = x.shape
    total = gate.shape[1]
    spec = pl.BlockSpec((rows, UNIT_BLOCK), lambda i: (0, i))
    outs = [
        jax.ShapeDtypeStruct((rows, 2 * total), BF16),
        jax.ShapeDtypeStruct((rows // 2, cols), BF16),
        jax.ShapeDtypeStruct((rows // 2, cols), F32),
    ]
    return pl.pallas_call(
        inner_back_kernel,
        grid=(total // UNIT_BLOCK,),
        in_specs=[pl.BlockSpec(memory_space=pltpu.SMEM), whole(x), spec, spec]
        + [pl.BlockSpec((UNIT_BLOCK, w.shape[1]), lambda i: (i, 0)) for w in down]
        + [pl.BlockSpec((2 * UNIT_BLOCK, w.shape[1]), lambda i: (i, 0)) for w in two],
        out_specs=[
            pl.BlockSpec((rows, 2 * UNIT_BLOCK), lambda i: (0, i)),
            whole(outs[1]),
            whole(outs[2]),
        ],
        out_shape=outs,
        scratch_shapes=[pltpu.VMEM((rows, cols), F32)],
        compiler_params=pltpu.CompilerParams(vmem_limit_bytes=VMEM_BYTES),
        cost_estimate=cost(6 * rows * cols * total, [x, gate, up, *down, *two, *outs]),
        name="inner_back",
    )(core.reshape(1), x, gate, up, *down, *two)


class Plan:
    def __init__(self, ways_dp, ways_tensor):
        self.ways_dp = ways_dp
        self.ways_tensor = ways_tensor
        self.chips = ways_dp // 2
        self.bits = self.chips.bit_length() - 1
        assert self.chips == 1 << self.bits and ways_tensor == 4
        dp = lax.axis_index("dp")
        self.chip = dp // 2
        self.core = dp % 2
        self.place = lax.axis_index("tensor")
        self.core_perm = [(i, i ^ 1) for i in range(ways_dp)]

    def swap_core(self, array):
        return lax.ppermute(array, "dp", self.core_perm)

    def swap_chip(self, array, bit):
        perm = [(i, i ^ (2 << bit)) for i in range(self.ways_dp)]
        return lax.ppermute(array, "dp", perm)

    def route(self, turn):
        pairs = []
        for chip in range(self.chips):
            for core in range(2):
                for z in range(4):
                    micro = (z + turn) % 2
                    source = (2 * chip + core) * 4 + z
                    target = (2 * chip + z // 2) * 4 + 2 * micro + core
                    pairs.append((source, target))
        return pairs

    def by_chip(self, array):
        lead = array.shape[:-1]
        wide = array.shape[-1] // self.chips
        parts = [
            lax.dynamic_slice_in_dim(array, (self.chip ^ r) * wide, wide, axis=-1)
            for r in range(self.chips)
        ]
        return jnp.concatenate(parts, axis=-1).reshape(*lead, -1)

    def to_chip(self, array):
        got = []
        for turn in range(2):
            micro = (self.place + turn) % 2
            part = lax.dynamic_index_in_dim(array, micro, 0, keepdims=False)
            got.append(lax.ppermute(self.by_chip(part), ("dp", "tensor"), self.route(turn)))
        first = self.place // 2 == 0
        return jnp.concatenate(
            [jnp.where(first, got[0], got[1]), jnp.where(first, got[1], got[0])], axis=0
        )

    def from_chip(self, array):
        rows = array.shape[0] // 2
        got = []
        for turn in range(2):
            block = (self.place // 2 + turn) % 2
            part = lax.dynamic_slice_in_dim(array, block * rows, rows, axis=0)
            back = [(b, a) for a, b in self.route(turn)]
            got.append(lax.ppermute(self.by_chip(part), ("dp", "tensor"), back))
        first = self.place % 2 == 0
        return jnp.stack([jnp.where(first, got[0], got[1]), jnp.where(first, got[1], got[0])])

    def both_rows(self, half):
        other = self.swap_core(half)
        first = self.core == 0
        return jnp.concatenate(
            [jnp.where(first, half, other), jnp.where(first, other, half)], axis=0
        )

    def sum_rows(self, give, keep):
        return keep + self.swap_core(give).astype(F32)

    def line_gather(self, shard):
        mine = lax.dynamic_index_in_dim(shard, self.core, 0, keepdims=False)
        theirs = lax.dynamic_index_in_dim(shard, 1 - self.core, 0, keepdims=False)
        other = self.swap_core(theirs)
        first = self.core == 0
        pair = jnp.concatenate(
            [jnp.where(first, mine, other), jnp.where(first, other, mine)], axis=1
        )
        return lax.all_gather(pair, "tensor", axis=0, tiled=True)

    def chip_gather(self, own):
        half = own.shape[0] // 2
        if self.bits == 2:
            by_x = self.swap_chip(own, 0)
            by_y = self.swap_chip(own, 1)
            far_top = self.swap_chip(by_x[:half], 1)
            far_low = self.swap_chip(by_y[half:], 0)
            return [own, by_x, by_y, jnp.concatenate([far_top, far_low], axis=0)]
        parts = [own]
        for bit in range(self.bits):
            parts = parts + [self.swap_chip(p, bit) for p in parts]
        return [jnp.concatenate(parts, axis=1)]

    def scatter(self, total):
        return lax.psum_scatter(total, "tensor", scatter_dimension=0, tiled=True)

    def share(self, pair):
        narrow = pair.shape[1] // 2
        mine = lax.dynamic_slice_in_dim(pair, self.core * narrow, narrow, axis=1)
        theirs = lax.dynamic_slice_in_dim(pair, (1 - self.core) * narrow, narrow, axis=1)
        other = self.swap_core(theirs)
        first = self.core == 0
        return jnp.stack([jnp.where(first, mine, other), jnp.where(first, other, mine)]).astype(F32)

    def sum_all(self, vector):
        vector = vector + self.swap_core(vector)
        for bit in range(self.bits):
            vector = vector + self.swap_chip(vector, bit)
        for bit in range(2):
            perm = [(z, z ^ (1 << bit)) for z in range(4)]
            vector = vector + lax.ppermute(vector, "tensor", perm)
        return vector


class Reduction:
    def __init__(self, plan, left, right):
        self.plan, self.left, self.right = plan, left, right
        self.wide = right.shape[1] // plan.chips
        self.rows = left.shape[1]
        self.half = self.rows // 2
        self.staged = plan.bits == 2
        if self.staged:
            self.first = [
                self.top(3).astype(BF16),
                self.low(3).astype(BF16),
                self.low(1).astype(BF16),
                self.top(2).astype(BF16),
            ]
        else:
            self.first = [self.term(r, 0, self.rows) for r in range(plan.chips)]

    def term(self, r, lo, hi):
        return dot_first(self.left[:, lo:hi], self.right[:, r * self.wide : (r + 1) * self.wide])

    def top(self, r):
        return self.term(r, 0, self.half)

    def low(self, r):
        return self.term(r, self.half, self.rows)

    def send_first(self):
        if self.staged:
            a, b, c, d = self.first
            swap = self.plan.swap_chip
            self.got = [swap(a, 1), swap(b, 0), swap(c, 0), swap(d, 1)]
        else:
            self.got = list(self.first)

    def prepare_second(self):
        if self.staged:
            far_top, far_low = self.got[:2]
            self.second = [
                (self.top(1) + far_top.astype(F32)).astype(BF16),
                (self.low(2) + far_low.astype(F32)).astype(BF16),
            ]
        else:
            self.second = []

    def send_second(self):
        if self.staged:
            self.last = [self.plan.swap_chip(self.second[0], 0), self.plan.swap_chip(self.second[1], 1)]
        else:
            self.last = []

    def finish(self):
        if self.staged:
            x_top, y_low = self.last
            x_low, y_top = self.got[2:]
            top = self.top(0) + x_top.astype(F32) + y_top.astype(F32)
            low = self.low(0) + x_low.astype(F32) + y_low.astype(F32)
            total = jnp.concatenate([top, low], axis=0)
        else:
            parts = self.got
            for bit in reversed(range(self.plan.bits)):
                keep, give = parts[: 1 << bit], parts[1 << bit :]
                parts = [
                    k + self.plan.swap_chip(g.astype(BF16), bit).astype(F32)
                    for k, g in zip(keep, give)
                ]
            total = parts[0]
        return total.astype(BF16)


def together(*groups):
    return lax.optimization_barrier(groups)


def split_columns(matrix):
    return matrix.T.reshape(2, matrix.shape[1] // 2, matrix.shape[0])


def split_rows(matrix):
    return matrix.reshape(2, matrix.shape[0] // 2, matrix.shape[1])


def body(
    inputs,
    seq_lengths,
    seq_assign,
    norm1_gain,
    w_query,
    w_key,
    w_value,
    w_forget,
    forget_bias,
    w_out,
    norm2_gain,
    w_gate,
    w_up,
    w_down,
    out_grad,
):
    plan = Plan(lax.axis_size("dp"), lax.axis_size("tensor"))
    core, place = plan.core, plan.place
    part_rows = inputs.shape[1]
    seq_rows = part_rows * 4
    half_rows = seq_rows // 2
    heads_shard = w_forget.shape[1] // 2
    heads_here = heads_shard * 4
    shard_cols = w_query.shape[1] // 2
    blocks = w_gate.shape[1] // 2 // UNIT_BLOCK

    def by_block(matrix):
        return split_columns(matrix).reshape(2, blocks, 1, UNIT_BLOCK, matrix.shape[0])

    forget_part = jnp.pad(
        split_columns(w_forget), ((0, 0), (0, FORGET_PAD - heads_shard), (0, 0))
    )
    line_one = plan.line_gather(
        jnp.concatenate(
            [split_columns(w_query), split_columns(w_key), split_columns(w_value), forget_part],
            axis=1,
        )
    )
    inputs, line_one = together(inputs, line_one)
    full_one = plan.chip_gather(line_one)
    rows_in = plan.to_chip(inputs).astype(F32)
    line_mid = plan.line_gather(
        jnp.concatenate([split_rows(w_out), split_rows(w_down)], axis=1)
    )
    line_mid = line_mid.reshape(4, -1, line_mid.shape[-1])
    full_out = plan.chip_gather(line_mid[:, :shard_cols].reshape(4 * shard_cols, -1))
    full_down = plan.chip_gather(line_mid[:, shard_cols:].reshape(-1, line_mid.shape[-1]))
    two_part = jnp.concatenate([by_block(w_gate), by_block(w_up)], axis=2)
    line_two = plan.line_gather(two_part.reshape(2, -1, two_part.shape[-1]))
    full_two = plan.chip_gather(line_two)

    other_assign = plan.swap_core(seq_assign)
    assign_both = jnp.where(
        core == 0,
        jnp.concatenate([seq_assign, other_assign], axis=1),
        jnp.concatenate([other_assign, seq_assign], axis=1),
    ).reshape(4)
    seq_id = jnp.sum(jnp.where(jnp.arange(4) == place, assign_both, 0))
    length = jnp.sum(jnp.where(jnp.arange(seq_lengths.shape[0]) == seq_id, seq_lengths, 0))
    count = length.reshape(1)
    valid_here = (core * half_rows + jnp.arange(half_rows) < length).astype(F32)[:, None]

    gain_one = plan.by_chip(norm1_gain)
    gain_two = plan.by_chip(norm2_gain)
    bias_here = lax.dynamic_index_in_dim(
        forget_bias.reshape(4, 2, heads_shard), core, 1, keepdims=False
    ).reshape(-1)

    scale_one = row_scale(rows_in)
    normed_one = plan.both_rows((rows_in * scale_one * gain_one).astype(BF16))
    queries, key_rows, value_rows, logits = project(normed_one, full_one, shard_cols, heads_shard)
    forget_logit = logits + bias_here
    cumul_gate = jnp.cumsum(jax.nn.log_sigmoid(forget_logit), axis=0)
    gate_pairs = cumul_gate.reshape(seq_rows, heads_here // 2, 2).transpose(1, 0, 2)
    mixed_low, log_total = attn_fwd(count, queries, key_rows, value_rows, gate_pairs)
    mixed_low, out_grad = together(mixed_low, out_grad)
    cotangent = plan.to_chip(out_grad).astype(F32)
    hidden_in = rows_in + plan.sum_rows(*combine(core, mixed_low, full_out))

    scale_two = row_scale(hidden_in)
    normed_two = plan.both_rows((hidden_in * scale_two * gain_two).astype(BF16))
    gate_pre, up_pre, inner_low = inner_units(normed_two, full_two)
    grad_ffn = plan.both_rows((valid_here * cotangent).astype(BF16))
    down_sum = Reduction(plan, inner_low, grad_ffn)
    down_sum.first, gate_pre = together(down_sum.first, gate_pre)
    down_sum.send_first()
    ffn_rows = plan.sum_rows(*combine(core, inner_low, full_down))
    outputs = plan.from_chip((valid_here * (hidden_in + ffn_rows)).astype(BF16))

    grad_pre, give_two, keep_two = inner_back(
        core, grad_ffn, gate_pre, up_pre, full_down, full_two
    )
    down_sum.got, grad_pre = together(down_sum.got, grad_pre)
    down_sum.prepare_second()
    two_sum = Reduction(plan, grad_pre, normed_two)
    two_sum.first, down_sum.second = together(two_sum.first, down_sum.second)
    down_sum.send_second()
    two_sum.send_first()
    down_pair = plan.scatter(down_sum.finish())
    grad_normed_two = plan.sum_rows(give_two, keep_two)
    gain_two_term = jnp.sum(grad_normed_two * hidden_in * scale_two, axis=0)
    grad_hidden = valid_here * cotangent + norm_back(
        hidden_in, scale_two, gain_two, grad_normed_two
    )

    grad_attn = plan.both_rows(grad_hidden.astype(BF16))
    grad_mixed = spread(count, grad_attn, full_out)
    query_low, key_low, value_low, grad_cumul = attn_bwd(
        count, queries, key_rows, value_rows, gate_pairs, log_total, mixed_low, grad_mixed
    )
    two_sum.got, query_low = together(two_sum.got, query_low)
    two_sum.prepare_second()
    two_sum.second, query_low, key_low, value_low, grad_cumul = together(
        two_sum.second, query_low, key_low, value_low, grad_cumul
    )
    two_sum.send_second()
    grad_logf = jnp.flip(jnp.cumsum(jnp.flip(grad_cumul, 0), axis=0), 0)
    grad_logit = grad_logf * jax.nn.sigmoid(-forget_logit)
    bias_term = jnp.sum(grad_logit, axis=0)
    grad_one = jnp.concatenate(
        [
            query_low.reshape(seq_rows, 4, shard_cols),
            key_low.reshape(seq_rows, 4, shard_cols),
            value_low.reshape(seq_rows, 4, shard_cols),
            jnp.pad(
                grad_logit.astype(BF16).reshape(seq_rows, 4, heads_shard),
                ((0, 0), (0, 0), (0, FORGET_PAD - heads_shard)),
            ),
        ],
        axis=2,
    ).reshape(seq_rows, -1)
    grad_attn, grad_one = together(grad_attn, grad_one)
    out_sum = Reduction(plan, mixed_low, grad_attn)
    one_sum = Reduction(plan, grad_one, normed_one)
    out_sum.first, one_sum.first, two_sum.last = together(
        out_sum.first, one_sum.first, two_sum.last
    )
    out_sum.send_first()
    one_sum.send_first()
    two_total, down_pair = together(two_sum.finish(), down_pair)
    two_pair = plan.scatter(two_total)
    out_sum.got, one_sum.got, two_total, grad_one = together(
        out_sum.got, one_sum.got, two_total, grad_one
    )
    out_sum.prepare_second()
    one_sum.prepare_second()
    out_sum.second, one_sum.second = together(out_sum.second, one_sum.second)
    out_sum.send_second()
    one_sum.send_second()
    out_total, two_pair = together(out_sum.finish(), two_pair)
    out_pair = plan.scatter(out_total)
    one_total, out_pair = together(one_sum.finish(), out_pair)
    one_pair = plan.scatter(one_total)
    down_shard, two_shard = plan.share(down_pair), plan.share(two_pair)
    out_shard, one_shard = plan.share(out_pair), plan.share(one_pair)
    grad_normed_one = plan.sum_rows(*combine(core, grad_one, full_one))
    gain_one_term = jnp.sum(grad_normed_one * rows_in * scale_one, axis=0)
    input_grad = plan.from_chip(
        (grad_hidden + norm_back(rows_in, scale_one, gain_one, grad_normed_one)).astype(BF16)
    )

    bias_full = jnp.where(
        (jnp.arange(2) == core)[None, :, None], bias_term.reshape(4, 1, heads_shard), 0.0
    ).reshape(-1)
    wide = norm1_gain.shape[0]
    small = plan.sum_all(
        jnp.concatenate([plan.by_chip(gain_one_term), plan.by_chip(gain_two_term), bias_full])
    )

    two_shard = two_shard.reshape(2, blocks, 2, UNIT_BLOCK, -1)

    def columns(shard):
        return shard.reshape(-1, shard.shape[-1]).T

    def rows(shard):
        return shard.reshape(-1, shard.shape[-1])

    return (
        outputs,
        input_grad,
        small[:wide],
        columns(one_shard[:, :shard_cols]),
        columns(one_shard[:, shard_cols : 2 * shard_cols]),
        columns(one_shard[:, 2 * shard_cols : 3 * shard_cols]),
        columns(one_shard[:, 3 * shard_cols : 3 * shard_cols + heads_shard]),
        small[2 * wide :],
        rows(out_shard),
        small[wide : 2 * wide],
        columns(two_shard[:, :, 0]),
        columns(two_shard[:, :, 1]),
        rows(down_shard),
    )


def solution(mesh):
    return jax.shard_map(
        body,
        mesh=mesh,
        in_specs=(
            P(None, ("dp", "tensor"), None),
            P(),
            P(None, "dp"),
            P(),
            P("dp", "tensor"),
            P("dp", "tensor"),
            P("dp", "tensor"),
            P("dp", "tensor"),
            P(),
            P("tensor", "dp"),
            P(),
            P("dp", "tensor"),
            P("dp", "tensor"),
            P("tensor", "dp"),
            P(None, ("dp", "tensor"), None),
        ),
        out_specs=(
            P(None, ("dp", "tensor"), None),
            P(None, ("dp", "tensor"), None),
            P(),
            P("dp", "tensor"),
            P("dp", "tensor"),
            P("dp", "tensor"),
            P("dp", "tensor"),
            P(),
            P("tensor", "dp"),
            P(),
            P("dp", "tensor"),
            P("dp", "tensor"),
            P("tensor", "dp"),
        ),
        check_vma=False,
    )
```

```python
import functools

import jax
import jax.numpy as jnp
from jax import lax
from jax.experimental import pallas as pl
from jax.experimental.pallas import tpu as pltpu
from jax.sharding import PartitionSpec as P

EPS = 1e-06
NEG_BIG = -1e30
F32 = jnp.float32
BF16 = jnp.bfloat16
FORGET_PAD = 16
UNIT_BLOCK = 256
VMEM_BYTES = 60 << 20


def row_scale(tokens):
    return lax.rsqrt(jnp.mean(tokens * tokens, axis=-1, keepdims=True) + EPS)


def norm_back(tokens, scaling, gain, grad_out):
    weighted = grad_out * gain
    cubed = scaling * scaling * scaling
    return scaling * weighted - tokens * cubed * jnp.mean(weighted * tokens, axis=-1, keepdims=True)


def dot_first(left, right):
    return lax.dot_general(left, right, (((0,), (0,)), ((), ())), preferred_element_type=F32)

def nt(a, b):
    return lax.dot_general(a, b, (((1,), (1,)), ((), ())), preferred_element_type=F32)

def nn(a, b):
    return lax.dot_general(a, b, (((1,), (0,)), ((), ())), preferred_element_type=F32)

def pieces(x):
    top = x.astype(BF16).astype(F32)
    rest = x - top
    mid = rest.astype(BF16).astype(F32)
    return top, mid, rest - mid

def side(lane, base, values, rest):
    for n, value in enumerate(values):
        rest = jnp.where(lane == base + n, value, rest)
    return rest

def gate_column(c_ref, which, length, rows):
    col = c_ref[0, :, which : which + 1]
    pos = lax.broadcasted_iota(jnp.int32, (rows, 1), 0)
    return jnp.where(pos < length, -col, NEG_BIG)

def attn_fwd_kernel(len_ref, q_ref, k_ref, v_ref, c_ref, o_ref, l_ref, *, blk):
    rows, wide = q_ref.shape
    hd = wide // 2
    length = len_ref[0]
    lane = lax.broadcasted_iota(jnp.int32, (rows, wide), 1)
    lane_b = lax.broadcasted_iota(jnp.int32, (blk, wide), 1)
    q = q_ref[...].astype(F32) * 0.125
    k = k_ref[...].astype(F32)
    v = v_ref[...].astype(F32)
    heads = []
    for h in range(2):
        inside = (lane < hd) if h == 0 else (lane >= hd)
        base = hd if h == 0 else 0
        bias = jnp.broadcast_to(gate_column(c_ref, h, length, rows), (rows, wide))
        kx = jnp.where(inside, k, side(lane, base, pieces(bias), 0.0)).astype(BF16)
        qx = jnp.where(inside, q, side(lane, base, (1.0, 1.0, 1.0), 0.0)).astype(BF16)
        vx = jnp.where(inside, v, 1.0).astype(BF16)
        heads.append((qx, kx, vx))
    tri = lax.broadcasted_iota(jnp.int32, (blk, blk), 1) <= lax.broadcasted_iota(jnp.int32, (blk, blk), 0)
    for i in range(rows // blk):
        lo, hi = i * blk, (i + 1) * blk
        got = []
        for h in range(2):
            qx, kx, vx = heads[h]
            s_d = jnp.where(tri, nt(qx[lo:hi], kx[lo:hi]), NEG_BIG)
            m = jnp.max(s_d, axis=1, keepdims=True)
            if i:
                s_o = nt(qx[lo:hi], kx[:lo])
                m = jnp.maximum(m, jnp.max(s_o, axis=1, keepdims=True))
            r = nn(jnp.exp(s_d - m).astype(BF16), vx[lo:hi])
            if i:
                r = r + nn(jnp.exp(s_o - m).astype(BF16), vx[:lo])
            total = pltpu.roll(r, hd, 1)
            got.append((r / total, m + jnp.log(total)))
        pos = lo + lax.broadcasted_iota(jnp.int32, (blk, wide), 0)
        o = jnp.where(lane_b < hd, got[0][0], got[1][0])
        o_ref[lo:hi, :] = jnp.where(pos < length, o, 0.0).astype(BF16)
        l_ref[lo:hi, :] = jnp.where(lane_b < hd, got[0][1], got[1][1])

def third(rows, pairs, n):
    return pl.BlockSpec((rows, 128), lambda p: (0, n * pairs + p))


def attn_fwd(length, qkv, c, blk=256):
    rows, cols = qkv.shape[0], qkv.shape[1] // 3
    pairs = cols // 128
    spec = pl.BlockSpec((rows, 128), lambda p: (0, p))
    return pl.pallas_call(
        functools.partial(attn_fwd_kernel, blk=blk),
        grid=(pairs,),
        in_specs=[pl.BlockSpec(memory_space=pltpu.SMEM)]
        + [third(rows, pairs, n) for n in range(3)]
        + [pl.BlockSpec((1, rows, 2), lambda p: (p, 0, 0))],
        out_specs=[spec, spec],
        out_shape=[jax.ShapeDtypeStruct((rows, cols), BF16), jax.ShapeDtypeStruct((rows, cols), F32)],
        compiler_params=pltpu.CompilerParams(vmem_limit_bytes=VMEM_BYTES),
        cost_estimate=pl.CostEstimate(flops=rows*rows*128*4*pairs*2, bytes_accessed=rows*cols*12, transcendentals=rows*rows*pairs),
    )(length, qkv, qkv, qkv, c)

def attn_bwd_kernel(len_ref, q_ref, k_ref, v_ref, c_ref, l_ref, o_ref, g_ref, dq_ref, dk_ref, dv_ref, dc_ref, acc_k, acc_v, *, blk):
    rows, wide = q_ref.shape
    hd = wide // 2
    length = len_ref[0]
    lane = lax.broadcasted_iota(jnp.int32, (rows, wide), 1)
    q = q_ref[...].astype(F32) * 0.125
    k = k_ref[...].astype(F32)
    v = v_ref[...].astype(F32)
    g = g_ref[...].astype(F32)
    go = g * o_ref[...].astype(F32)
    tri = lax.broadcasted_iota(jnp.int32, (blk, blk), 0) <= lax.broadcasted_iota(jnp.int32, (blk, blk), 1)
    res = []
    for h in range(2):
        inside = (lane < hd) if h == 0 else (lane >= hd)
        base = hd if h == 0 else 0
        bias = jnp.broadcast_to(gate_column(c_ref, h, length, rows), (rows, wide))
        logt = l_ref[...]
        logt = jnp.where(inside, pltpu.roll(logt, hd, 1), logt)
        other = pltpu.roll(l_ref[...], hd, 1)
        logt = jnp.where(inside, l_ref[...], other)
        dot_o = jnp.broadcast_to(jnp.sum(jnp.where(inside, go, 0.0), axis=1, keepdims=True), (rows, wide))
        kx = jnp.where(inside, k, side(lane, base, pieces(bias) + (1.0, 1.0, 1.0), 0.0)).astype(BF16)
        qx = jnp.where(inside, q, side(lane, base, (1.0, 1.0, 1.0) + pieces(-logt), 0.0)).astype(BF16)
        vx = jnp.where(inside, v, side(lane, base, (1.0, 1.0, 1.0), 0.0)).astype(BF16)
        gx = jnp.where(inside, g, side(lane, base, pieces(-dot_o), 0.0)).astype(BF16)
        kt = kx.T
        dq_parts = []
        for i in range(rows // blk):
            lo, hi = i * blk, (i + 1) * blk
            dqt = None
            for a, b, diag in ((lo, hi, True),) + (((0, lo, False),) if i else ()):
                s = nt(kx[a:b], qx[lo:hi])
                if diag:
                    s = jnp.where(tri, s, NEG_BIG)
                p = jnp.exp(s)
                ds = (p * nt(vx[a:b], gx[lo:hi])).astype(BF16)
                dv = nn(p.astype(BF16), g_ref[lo:hi, :])
                dk = nn(ds, qx[lo:hi])
                t = nn(kt[:, a:b], ds)
                dqt = t if dqt is None else dqt + t
                if diag:
                    acc_v[a:b, :] = dv
                    acc_k[a:b, :] = dk
                else:
                    acc_v[a:b, :] += dv
                    acc_k[a:b, :] += dk
            dq_parts.append(dqt.T)
        dq = jnp.concatenate(dq_parts, axis=0)
        dk = acc_k[...]
        res.append((dq, dk, acc_v[...], dq - pltpu.roll(dk, 3, 1)))
    first = lane < hd
    dq_ref[...] = jnp.where(first, res[0][0] * 0.125, res[1][0] * 0.125).astype(BF16)
    dk_ref[...] = jnp.where(first, res[0][1], res[1][1]).astype(BF16)
    dv_ref[...] = jnp.where(first, res[0][2], res[1][2]).astype(BF16)
    dc_ref[...] = jnp.where(first, res[1][3], res[0][3])

def attn_bwd(length, qkv, c, l, o, g, blk=256):
    rows, cols = o.shape
    pairs = cols // 128
    spec = pl.BlockSpec((rows, 128), lambda p: (0, p))
    low = jax.ShapeDtypeStruct((rows, cols), BF16)
    dq, dk, dv, dc = pl.pallas_call(
        functools.partial(attn_bwd_kernel, blk=blk),
        grid=(pairs,),
        in_specs=[pl.BlockSpec(memory_space=pltpu.SMEM)]
        + [third(rows, pairs, n) for n in range(3)]
        + [pl.BlockSpec((1, rows, 2), lambda p: (p, 0, 0)), spec, spec, spec],
        out_specs=[spec]*4,
        out_shape=[low, low, low, jax.ShapeDtypeStruct((rows, cols), F32)],
        scratch_shapes=[pltpu.VMEM((rows, 128), F32)]*2,
        compiler_params=pltpu.CompilerParams(vmem_limit_bytes=VMEM_BYTES),
        cost_estimate=pl.CostEstimate(flops=rows*rows*128*10*pairs*2, bytes_accessed=rows*cols*24, transcendentals=rows*rows*pairs),
    )(length, qkv, qkv, qkv, c, l, o, g)
    d3 = dc.reshape(rows, pairs, 128)
    grad_cumul = jnp.stack([d3[:, :, 67], d3[:, :, 3]], axis=2).reshape(rows, 2 * pairs)
    return dq, dk, dv, grad_cumul


def whole(array):
    return pl.BlockSpec(array.shape, lambda *_: (0,) * array.ndim, pipeline_mode=pl.Buffered(1))


def cost(flops, arrays, more=0):
    size = sum(a.size * a.dtype.itemsize for a in arrays)
    return pl.CostEstimate(flops=flops, bytes_accessed=size + more, transcendentals=0)


def joined(refs, lo=None, hi=None):
    if lo is None:
        return jnp.concatenate([r[...] for r in refs], axis=1)
    return jnp.concatenate([r[lo:hi, :] for r in refs], axis=1)


def project_kernel(x_ref, *refs):
    pieces_here = (len(refs) - 2) // 2
    w_refs, f_refs, (out_ref, f_ref) = refs[:pieces_here], refs[pieces_here:-2], refs[-2:]
    out_ref[...] = nt(x_ref[...], joined(w_refs)).astype(BF16)

    @pl.when(pl.program_id(0) == 0)
    def _():
        f_ref[...] = nt(x_ref[...], joined(f_refs))


def project(x, weights, few):
    rows = x.shape[0]
    extra = 4 * FORGET_PAD
    cols = (weights[0].shape[0] - extra) // 3
    outs = [
        jax.ShapeDtypeStruct((rows, 3 * cols), BF16),
        jax.ShapeDtypeStruct((rows, extra), F32),
    ]
    last = 3 * cols // extra
    qkv, f = pl.pallas_call(
        project_kernel,
        grid=(3,),
        in_specs=[whole(x)]
        + [pl.BlockSpec((cols, w.shape[1]), lambda i: (i, 0)) for w in weights]
        + [pl.BlockSpec((extra, w.shape[1]), lambda i: (last, 0)) for w in weights],
        out_specs=[pl.BlockSpec((rows, cols), lambda i: (0, i)), whole(outs[1])],
        out_shape=outs,
        compiler_params=pltpu.CompilerParams(vmem_limit_bytes=VMEM_BYTES),
        cost_estimate=cost(2 * rows * x.shape[1] * 3 * cols, [x, *weights, *outs]),
        name="project",
    )(x, *weights, *weights)
    logits = f.reshape(rows, 4, FORGET_PAD)[..., :few].reshape(rows, 4 * few)
    return qkv, logits


def combine_kernel(core_ref, *refs, lefts):
    left_refs, w_refs, (give_ref, keep_ref) = refs[:lefts], refs[lefts:-2], refs[-2:]
    step = pl.program_id(0)
    wide = w_refs[0].shape[1]
    for out, cond in ((give_ref, step < 2), (keep_ref, step >= 2)):

        @pl.when(cond)
        def _():
            for n, w in enumerate(w_refs):
                got, at = None, 0
                for left in left_refs:
                    deep = left.shape[1]
                    part = nn(left[...], w[at : at + deep, :])
                    got = part if got is None else got + part
                    at += deep
                out[:, n * wide : (n + 1) * wide] = got.astype(out.dtype)


def combine(core, lefts, weights):
    rows = lefts[0].shape[0]
    wide = weights[0].shape[1] * len(weights)
    block = rows // 4

    def place(i, core_ref):
        mine = core_ref[0]
        return (jnp.where(i < 2, (1 - mine) * 2 + i, mine * 2 + i - 2), 0)

    outs = [
        jax.ShapeDtypeStruct((rows // 2, wide), BF16),
        jax.ShapeDtypeStruct((rows // 2, wide), F32),
    ]
    return pl.pallas_call(
        functools.partial(combine_kernel, lefts=len(lefts)),
        grid_spec=pltpu.PrefetchScalarGridSpec(
            num_scalar_prefetch=1,
            grid=(4,),
            in_specs=[pl.BlockSpec((block, left.shape[1]), place) for left in lefts]
            + [whole(w) for w in weights],
            out_specs=[
                pl.BlockSpec((block, wide), lambda i, c: (jnp.minimum(i, 1), 0)),
                pl.BlockSpec((block, wide), lambda i, c: (jnp.maximum(i - 2, 0), 0)),
            ],
        ),
        out_shape=outs,
        compiler_params=pltpu.CompilerParams(vmem_limit_bytes=VMEM_BYTES),
        cost_estimate=cost(
            2 * rows * weights[0].shape[0] * wide, [*lefts, *weights, *outs]
        ),
        name="combine",
    )(core.reshape(1), *lefts, *weights)


def spread_kernel(len_ref, x_ref, *refs):
    w_refs, out_ref = refs[:-1], refs[-1]
    rows = x_ref.shape[0]
    got = nt(x_ref[...], joined(w_refs))
    pos = pl.program_id(0) * rows + lax.broadcasted_iota(jnp.int32, got.shape, 0)
    out_ref[...] = jnp.where(pos < len_ref[0], got, 0.0).astype(BF16)


def spread(length, x, weights):
    rows, wide = x.shape[0], weights[0].shape[0]
    block = rows // 4
    out = jax.ShapeDtypeStruct((rows, wide), BF16)
    return pl.pallas_call(
        spread_kernel,
        grid=(4,),
        in_specs=[
            pl.BlockSpec(memory_space=pltpu.SMEM),
            pl.BlockSpec((block, x.shape[1]), lambda i: (i, 0)),
        ]
        + [whole(w) for w in weights],
        out_specs=pl.BlockSpec((block, wide), lambda i: (i, 0)),
        out_shape=out,
        compiler_params=pltpu.CompilerParams(vmem_limit_bytes=VMEM_BYTES),
        cost_estimate=cost(2 * rows * x.shape[1] * wide, [x, *weights, out]),
        name="spread",
    )(length, x, *weights)


def inner_kernel(x_ref, *refs):
    w_refs, (gate_ref, up_ref, inner_ref) = refs[:-3], refs[-3:]
    both = nt(x_ref[...], joined(w_refs))
    gate, up = both[:, :UNIT_BLOCK], both[:, UNIT_BLOCK:]
    gate_ref[...] = gate
    up_ref[...] = up
    inner_ref[...] = (gate * jax.nn.sigmoid(gate) * up).astype(BF16)


def inner_units(x, weights):
    rows = x.shape[0]
    total = weights[0].shape[0] // 2
    spec = pl.BlockSpec((rows, UNIT_BLOCK), lambda i: (0, i))
    outs = [jax.ShapeDtypeStruct((rows, total), t) for t in (F32, F32, BF16)]
    return pl.pallas_call(
        inner_kernel,
        grid=(total // UNIT_BLOCK,),
        in_specs=[whole(x)]
        + [pl.BlockSpec((2 * UNIT_BLOCK, w.shape[1]), lambda i: (i, 0)) for w in weights],
        out_specs=[spec] * 3,
        out_shape=outs,
        compiler_params=pltpu.CompilerParams(vmem_limit_bytes=VMEM_BYTES),
        cost_estimate=cost(4 * rows * x.shape[1] * total, [x, *weights, *outs]),
        name="inner_units",
    )(x, *weights)


def inner_grads_kernel(x_ref, gate_ref, up_ref, *refs):
    down_refs, pre_ref = refs[:-1], refs[-1]
    grad = nt(x_ref[...], joined(down_refs))
    gate, up = gate_ref[...], up_ref[...]
    sig = jax.nn.sigmoid(gate)
    pre_ref[:, :UNIT_BLOCK] = (grad * up * (sig * (1.0 + gate * (1.0 - sig)))).astype(BF16)
    pre_ref[:, UNIT_BLOCK:] = (grad * (gate * sig)).astype(BF16)


def inner_grads(x, gate, up, down):
    rows, cols = x.shape
    total = gate.shape[1]
    spec = pl.BlockSpec((rows, UNIT_BLOCK), lambda i: (0, i))
    out = jax.ShapeDtypeStruct((rows, 2 * total), BF16)
    return pl.pallas_call(
        inner_grads_kernel,
        grid=(total // UNIT_BLOCK,),
        in_specs=[whole(x), spec, spec]
        + [pl.BlockSpec((UNIT_BLOCK, w.shape[1]), lambda i: (i, 0)) for w in down],
        out_specs=pl.BlockSpec((rows, 2 * UNIT_BLOCK), lambda i: (0, i)),
        out_shape=out,
        compiler_params=pltpu.CompilerParams(vmem_limit_bytes=VMEM_BYTES),
        cost_estimate=cost(2 * rows * cols * total, [x, gate, up, *down, out]),
        name="inner_grads",
    )(x, gate, up, *down)


class Plan:
    def __init__(self, ways_dp, ways_tensor):
        self.ways_dp = ways_dp
        self.ways_tensor = ways_tensor
        self.chips = ways_dp // 2
        self.bits = self.chips.bit_length() - 1
        assert self.chips == 1 << self.bits and ways_tensor == 4
        dp = lax.axis_index("dp")
        self.chip = dp // 2
        self.core = dp % 2
        self.place = lax.axis_index("tensor")
        self.core_perm = [(i, i ^ 1) for i in range(ways_dp)]

    def swap_core(self, array):
        return lax.ppermute(array, "dp", self.core_perm)

    def swap_chip(self, array, bit):
        perm = [(i, i ^ (2 << bit)) for i in range(self.ways_dp)]
        return lax.ppermute(array, "dp", perm)

    def route(self, turn):
        pairs = []
        for chip in range(self.chips):
            for core in range(2):
                for z in range(4):
                    micro = (z + turn) % 2
                    source = (2 * chip + core) * 4 + z
                    target = (2 * chip + z // 2) * 4 + 2 * micro + core
                    pairs.append((source, target))
        return pairs

    def by_chip(self, array):
        lead = array.shape[:-1]
        wide = array.shape[-1] // self.chips
        parts = [
            lax.dynamic_slice_in_dim(array, (self.chip ^ r) * wide, wide, axis=-1)
            for r in range(self.chips)
        ]
        return jnp.concatenate(parts, axis=-1).reshape(*lead, -1)

    def to_chip(self, array):
        got = []
        for turn in range(2):
            micro = (self.place + turn) % 2
            part = lax.dynamic_index_in_dim(array, micro, 0, keepdims=False)
            got.append(lax.ppermute(self.by_chip(part), ("dp", "tensor"), self.route(turn)))
        first = self.place // 2 == 0
        return jnp.concatenate(
            [jnp.where(first, got[0], got[1]), jnp.where(first, got[1], got[0])], axis=0
        )

    def from_chip(self, array):
        rows = array.shape[0] // 2
        got = []
        for turn in range(2):
            block = (self.place // 2 + turn) % 2
            part = lax.dynamic_slice_in_dim(array, block * rows, rows, axis=0)
            back = [(b, a) for a, b in self.route(turn)]
            got.append(lax.ppermute(self.by_chip(part), ("dp", "tensor"), back))
        first = self.place % 2 == 0
        return jnp.stack([jnp.where(first, got[0], got[1]), jnp.where(first, got[1], got[0])])

    def both_rows(self, half):
        other = self.swap_core(half)
        first = self.core == 0
        return jnp.concatenate(
            [jnp.where(first, half, other), jnp.where(first, other, half)], axis=0
        )

    def sum_rows(self, give, keep):
        return keep + self.swap_core(give).astype(F32)

    def line_gather(self, shard):
        mine = lax.dynamic_index_in_dim(shard, self.core, 0, keepdims=False)
        theirs = lax.dynamic_index_in_dim(shard, 1 - self.core, 0, keepdims=False)
        other = self.swap_core(theirs)
        first = self.core == 0
        pair = jnp.concatenate(
            [jnp.where(first, mine, other), jnp.where(first, other, mine)], axis=1
        )
        return lax.all_gather(pair, "tensor", axis=0, tiled=True)

    def near_gather(self, own):
        if self.bits == 2:
            return [own, self.swap_chip(own, 0), self.swap_chip(own, 1)]
        parts = [own]
        for bit in range(self.bits):
            parts = parts + [self.swap_chip(p, bit) for p in parts]
        return [jnp.concatenate(parts, axis=1)]

    def far_gather(self, near):
        if self.bits != 2:
            return near
        own, by_x, by_y = near
        half = own.shape[0] // 2
        far_top = self.swap_chip(by_x[:half], 1)
        far_low = self.swap_chip(by_y[half:], 0)
        return [own, by_x, by_y, jnp.concatenate([far_top, far_low], axis=0)]

    def scatter(self, total):
        return lax.psum_scatter(total, "tensor", scatter_dimension=0, tiled=True)

    def share(self, pair):
        narrow = pair.shape[1] // 2
        mine = lax.dynamic_slice_in_dim(pair, self.core * narrow, narrow, axis=1)
        theirs = lax.dynamic_slice_in_dim(pair, (1 - self.core) * narrow, narrow, axis=1)
        other = self.swap_core(theirs)
        first = self.core == 0
        return jnp.stack([jnp.where(first, mine, other), jnp.where(first, other, mine)]).astype(F32)

    def sum_all(self, vector):
        vector = vector + self.swap_core(vector)
        for bit in range(self.bits):
            vector = vector + self.swap_chip(vector, bit)
        for bit in range(2):
            perm = [(z, z ^ (1 << bit)) for z in range(4)]
            vector = vector + lax.ppermute(vector, "tensor", perm)
        return vector


class Reduction:
    def __init__(self, plan, lefts, right):
        self.plan, self.lefts, self.right = plan, lefts, right
        self.wide = right.shape[1] // plan.chips
        self.staged = plan.bits == 2
        if self.staged:
            self.first = [
                self.top(3).astype(BF16),
                self.low(3).astype(BF16),
                self.low(1).astype(BF16),
                self.top(2).astype(BF16),
            ]
        else:
            self.first = [
                jnp.concatenate([self.top(r), self.low(r)], axis=0) for r in range(plan.chips)
            ]

    def term(self, r, side):
        right = self.right[:, r * self.wide : (r + 1) * self.wide]
        parts = []
        for left in self.lefts:
            half = left.shape[1] // 2
            parts.append(dot_first(left[:, side * half : (side + 1) * half], right))
        return parts[0] if len(parts) == 1 else jnp.concatenate(parts, axis=0)

    def top(self, r):
        return self.term(r, 0)

    def low(self, r):
        return self.term(r, 1)

    def by_place(self, half):
        if len(self.lefts) == 1:
            return half
        parts, at = [], 0
        for left in self.lefts:
            parts.append((at, left.shape[1] // 4))
            at += left.shape[1] // 2
        return jnp.concatenate(
            [half[at + n * few : at + (n + 1) * few] for n in range(2) for at, few in parts], axis=0
        )

    def send_first(self):
        if self.staged:
            a, b, c, d = self.first
            swap = self.plan.swap_chip
            self.got = [swap(a, 1), swap(b, 0), swap(c, 0), swap(d, 1)]
        else:
            self.got = list(self.first)

    def prepare_second(self):
        if self.staged:
            far_top, far_low = self.got[:2]
            self.second = [
                (self.top(1) + far_top.astype(F32)).astype(BF16),
                (self.low(2) + far_low.astype(F32)).astype(BF16),
            ]
        else:
            self.second = []

    def send_second(self):
        if self.staged:
            self.last = [self.plan.swap_chip(self.second[0], 0), self.plan.swap_chip(self.second[1], 1)]
        else:
            self.last = []

    def finish(self):
        if self.staged:
            x_top, y_low = self.last
            x_low, y_top = self.got[2:]
            top = self.top(0) + x_top.astype(F32) + y_top.astype(F32)
            low = self.low(0) + x_low.astype(F32) + y_low.astype(F32)
            total = jnp.concatenate([self.by_place(top.astype(BF16)), self.by_place(low.astype(BF16))], axis=0)
        else:
            parts = self.got
            for bit in reversed(range(self.plan.bits)):
                keep, give = parts[: 1 << bit], parts[1 << bit :]
                parts = [
                    k + self.plan.swap_chip(g.astype(BF16), bit).astype(F32)
                    for k, g in zip(keep, give)
                ]
            half = parts[0].shape[0] // 2
            total = jnp.concatenate(
                [self.by_place(parts[0][:half]), self.by_place(parts[0][half:])], axis=0
            )
        return total.astype(BF16)


def together(*groups):
    return lax.optimization_barrier(groups)


def split_columns(matrix):
    return matrix.T.reshape(2, matrix.shape[1] // 2, matrix.shape[0])


def split_rows(matrix):
    return matrix.reshape(2, matrix.shape[0] // 2, matrix.shape[1])


def body(
    inputs,
    seq_lengths,
    seq_assign,
    norm1_gain,
    w_query,
    w_key,
    w_value,
    w_forget,
    forget_bias,
    w_out,
    norm2_gain,
    w_gate,
    w_up,
    w_down,
    out_grad,
):
    plan = Plan(lax.axis_size("dp"), lax.axis_size("tensor"))
    core, place = plan.core, plan.place
    part_rows = inputs.shape[1]
    seq_rows = part_rows * 4
    half_rows = seq_rows // 2
    heads_shard = w_forget.shape[1] // 2
    heads_here = heads_shard * 4
    shard_cols = w_query.shape[1] // 2
    blocks = w_gate.shape[1] // 2 // UNIT_BLOCK

    def by_block(matrix):
        return split_columns(matrix).reshape(2, blocks, 1, UNIT_BLOCK, matrix.shape[0])

    forget_part = jnp.pad(
        split_columns(w_forget), ((0, 0), (0, FORGET_PAD - heads_shard), (0, 0))
    )
    line_one = plan.line_gather(
        jnp.concatenate(
            [split_columns(w_query), split_columns(w_key), split_columns(w_value), forget_part],
            axis=1,
        )
    )
    inputs, line_one = together(inputs, line_one)
    rows_one = line_one.shape[0] // 4

    def by_kind(piece):
        piece = piece.reshape(4, rows_one, -1)
        edges = [0, shard_cols, 2 * shard_cols, 3 * shard_cols, rows_one]
        parts = [piece[:, a:b].reshape(-1, piece.shape[-1]) for a, b in zip(edges, edges[1:])]
        return jnp.concatenate(parts, axis=0)

    full_one = [by_kind(piece) for piece in plan.far_gather(plan.near_gather(line_one))]
    rows_in = plan.to_chip(inputs).astype(F32)
    line_mid = plan.line_gather(
        jnp.concatenate([split_rows(w_out), split_rows(w_down)], axis=1)
    )
    line_mid, full_one = together(line_mid, full_one)
    line_mid = line_mid.reshape(4, -1, line_mid.shape[-1])
    near_out = plan.near_gather(line_mid[:, :shard_cols].reshape(4 * shard_cols, -1))
    near_down = plan.near_gather(line_mid[:, shard_cols:].reshape(-1, line_mid.shape[-1]))
    two_part = jnp.concatenate([by_block(w_gate), by_block(w_up)], axis=2)
    line_two = plan.line_gather(two_part.reshape(2, -1, two_part.shape[-1]))

    other_assign = plan.swap_core(seq_assign)
    assign_both = jnp.where(
        core == 0,
        jnp.concatenate([seq_assign, other_assign], axis=1),
        jnp.concatenate([other_assign, seq_assign], axis=1),
    ).reshape(4)
    seq_id = jnp.sum(jnp.where(jnp.arange(4) == place, assign_both, 0))
    length = jnp.sum(jnp.where(jnp.arange(seq_lengths.shape[0]) == seq_id, seq_lengths, 0))
    count = length.reshape(1)
    valid_here = (core * half_rows + jnp.arange(half_rows) < length).astype(F32)[:, None]

    gain_one = plan.by_chip(norm1_gain)
    gain_two = plan.by_chip(norm2_gain)
    bias_here = lax.dynamic_index_in_dim(
        forget_bias.reshape(4, 2, heads_shard), core, 1, keepdims=False
    ).reshape(-1)

    scale_one = row_scale(rows_in)
    normed_one = plan.both_rows((rows_in * scale_one * gain_one).astype(BF16))
    qkv, logits = project(normed_one, full_one, heads_shard)
    forget_logit = logits + bias_here
    cumul_gate = jnp.cumsum(jax.nn.log_sigmoid(forget_logit), axis=0)
    gate_pairs = cumul_gate.reshape(seq_rows, heads_here // 2, 2).transpose(1, 0, 2)
    near_out, gate_pairs = together(near_out, gate_pairs)
    full_out = plan.far_gather(near_out)
    mixed_low, log_total = attn_fwd(count, qkv, gate_pairs)
    mixed_low, out_grad, near_down, full_out = together(mixed_low, out_grad, near_down, full_out)
    full_down = plan.far_gather(near_down)
    full_two = plan.far_gather(plan.near_gather(line_two))
    cotangent = plan.to_chip(out_grad).astype(F32)
    hidden_in = rows_in + plan.sum_rows(*combine(core, [mixed_low], full_out))

    scale_two = row_scale(hidden_in)
    normed_two = plan.both_rows((hidden_in * scale_two * gain_two).astype(BF16))
    normed_two, full_down = together(normed_two, full_down)
    gate_pre, up_pre, inner_low = inner_units(normed_two, full_two)
    grad_ffn = plan.both_rows((valid_here * cotangent).astype(BF16))
    down_sum = Reduction(plan, [inner_low], grad_ffn)
    down_sum.first, gate_pre = together(down_sum.first, gate_pre)
    down_sum.send_first()

    grad_pre = inner_grads(grad_ffn, gate_pre, up_pre, full_down)
    down_far, grad_pre = together(down_sum.got[:2], grad_pre)
    down_sum.got = [*down_far, *down_sum.got[2:]]
    two_sum = Reduction(plan, [grad_pre], normed_two)
    two_sum.first, down_sum.got, grad_pre = together(two_sum.first, down_sum.got, grad_pre)
    two_sum.send_first()
    down_sum.prepare_second()
    give_two, keep_two = combine(core, [grad_pre], full_two)
    two_far, down_sum.second, give_two = together(two_sum.got[:2], down_sum.second, give_two)
    two_sum.got = [*two_far, *two_sum.got[2:]]
    down_sum.send_second()
    grad_normed_two = plan.sum_rows(give_two, keep_two)
    gain_two_term = jnp.sum(grad_normed_two * hidden_in * scale_two, axis=0)
    grad_hidden = valid_here * cotangent + norm_back(
        hidden_in, scale_two, gain_two, grad_normed_two
    )

    grad_attn = plan.both_rows(grad_hidden.astype(BF16))
    out_sum = Reduction(plan, [mixed_low], grad_attn)
    out_sum.first, down_sum.last, grad_attn = together(out_sum.first, down_sum.last, grad_attn)
    out_sum.send_first()
    grad_mixed = spread(count, grad_attn, full_out)
    query_low, key_low, value_low, grad_cumul = attn_bwd(
        count, qkv, gate_pairs, log_total, mixed_low, grad_mixed
    )
    two_sum.got, out_sum.got, query_low = together(two_sum.got, out_sum.got, query_low)
    two_sum.prepare_second()
    out_sum.prepare_second()
    two_sum.second, out_sum.second, query_low, key_low, value_low, grad_cumul = together(
        two_sum.second, out_sum.second, query_low, key_low, value_low, grad_cumul
    )
    two_sum.send_second()
    out_sum.send_second()
    down_pair = plan.scatter(down_sum.finish())
    grad_logf = jnp.flip(jnp.cumsum(jnp.flip(grad_cumul, 0), axis=0), 0)
    grad_logit = grad_logf * jax.nn.sigmoid(-forget_logit)
    bias_term = jnp.sum(grad_logit, axis=0)
    logit_low = jnp.pad(
        grad_logit.astype(BF16).reshape(seq_rows, 4, heads_shard),
        ((0, 0), (0, 0), (0, FORGET_PAD - heads_shard)),
    ).reshape(seq_rows, -1)
    grad_one = [query_low, key_low, value_low, logit_low]
    grad_one, two_sum.last, out_sum.last = together(grad_one, two_sum.last, out_sum.last)
    one_sum = Reduction(plan, grad_one, normed_one)
    one_sum.send_first()
    one_far, two_sum.last, out_sum.last, inner_low = together(
        one_sum.got[:2], two_sum.last, out_sum.last, inner_low
    )
    ffn_rows = plan.sum_rows(*combine(core, [inner_low], full_down))
    outputs = plan.from_chip((valid_here * (hidden_in + ffn_rows)).astype(BF16))
    one_sum.got = [*one_far, *one_sum.got[2:]]
    two_total, down_pair = together(two_sum.finish(), down_pair)
    two_pair = plan.scatter(two_total)
    one_sum.got, two_total = together(one_sum.got, two_total)
    one_sum.prepare_second()
    one_sum.second, grad_one = together(one_sum.second, grad_one)
    one_sum.send_second()
    out_total, two_pair = together(out_sum.finish(), two_pair)
    out_pair = plan.scatter(out_total)
    one_total, out_pair = together(one_sum.finish(), out_pair)
    one_pair = plan.scatter(one_total)
    down_shard, two_shard = plan.share(down_pair), plan.share(two_pair)
    out_shard, one_shard = plan.share(out_pair), plan.share(one_pair)
    grad_normed_one = plan.sum_rows(*combine(core, grad_one, full_one))
    gain_one_term = jnp.sum(grad_normed_one * rows_in * scale_one, axis=0)
    input_grad = plan.from_chip(
        (grad_hidden + norm_back(rows_in, scale_one, gain_one, grad_normed_one)).astype(BF16)
    )

    bias_full = jnp.where(
        (jnp.arange(2) == core)[None, :, None], bias_term.reshape(4, 1, heads_shard), 0.0
    ).reshape(-1)
    wide = norm1_gain.shape[0]
    small = plan.sum_all(
        jnp.concatenate([plan.by_chip(gain_one_term), plan.by_chip(gain_two_term), bias_full])
    )

    two_shard = two_shard.reshape(2, blocks, 2, UNIT_BLOCK, -1)

    def columns(shard):
        return shard.reshape(-1, shard.shape[-1]).T

    def rows(shard):
        return shard.reshape(-1, shard.shape[-1])

    return (
        outputs,
        input_grad,
        small[:wide],
        columns(one_shard[:, :shard_cols]),
        columns(one_shard[:, shard_cols : 2 * shard_cols]),
        columns(one_shard[:, 2 * shard_cols : 3 * shard_cols]),
        columns(one_shard[:, 3 * shard_cols : 3 * shard_cols + heads_shard]),
        small[2 * wide :],
        rows(out_shard),
        small[wide : 2 * wide],
        columns(two_shard[:, :, 0]),
        columns(two_shard[:, :, 1]),
        rows(down_shard),
    )


def solution(mesh):
    return jax.shard_map(
        body,
        mesh=mesh,
        in_specs=(
            P(None, ("dp", "tensor"), None),
            P(),
            P(None, "dp"),
            P(),
            P("dp", "tensor"),
            P("dp", "tensor"),
            P("dp", "tensor"),
            P("dp", "tensor"),
            P(),
            P("tensor", "dp"),
            P(),
            P("dp", "tensor"),
            P("dp", "tensor"),
            P("tensor", "dp"),
            P(None, ("dp", "tensor"), None),
        ),
        out_specs=(
            P(None, ("dp", "tensor"), None),
            P(None, ("dp", "tensor"), None),
            P(),
            P("dp", "tensor"),
            P("dp", "tensor"),
            P("dp", "tensor"),
            P("dp", "tensor"),
            P(),
            P("tensor", "dp"),
            P(),
            P("dp", "tensor"),
            P("dp", "tensor"),
            P("tensor", "dp"),
        ),
        check_vma=False,
    )
```

```python
import functools

import jax
import jax.numpy as jnp
from jax import lax
from jax.experimental import pallas as pl
from jax.experimental.pallas import tpu as pltpu
from jax.sharding import PartitionSpec as P

EPS = 1e-06
NEG_BIG = -1e30
F32 = jnp.float32
BF16 = jnp.bfloat16
FORGET_PAD = 16
UNIT_BLOCK = 256
VMEM_BYTES = 60 << 20


def row_scale(tokens):
    return lax.rsqrt(jnp.mean(tokens * tokens, axis=-1, keepdims=True) + EPS)


def norm_back(tokens, scaling, gain, grad_out):
    weighted = grad_out * gain
    cubed = scaling * scaling * scaling
    return scaling * weighted - tokens * cubed * jnp.mean(weighted * tokens, axis=-1, keepdims=True)


def dot_first(left, right):
    return lax.dot_general(left, right, (((0,), (0,)), ((), ())), preferred_element_type=F32)

def nt(a, b):
    return lax.dot_general(a, b, (((1,), (1,)), ((), ())), preferred_element_type=F32)

def nn(a, b):
    return lax.dot_general(a, b, (((1,), (0,)), ((), ())), preferred_element_type=F32)

def pieces(x):
    top = x.astype(BF16).astype(F32)
    rest = x - top
    mid = rest.astype(BF16).astype(F32)
    return top, mid, rest - mid

def side(lane, base, values, rest):
    for n, value in enumerate(values):
        rest = jnp.where(lane == base + n, value, rest)
    return rest

def gate_column(c_ref, which, length, rows):
    col = c_ref[0, :, which : which + 1]
    pos = lax.broadcasted_iota(jnp.int32, (rows, 1), 0)
    return jnp.where(pos < length, -col, NEG_BIG)

def attn_fwd_kernel(len_ref, q_ref, k_ref, v_ref, c_ref, o_ref, l_ref, *, blk):
    rows, wide = q_ref.shape
    hd = wide // 2
    length = len_ref[0]
    lane = lax.broadcasted_iota(jnp.int32, (rows, wide), 1)
    lane_b = lax.broadcasted_iota(jnp.int32, (blk, wide), 1)
    q = q_ref[...].astype(F32) * 0.125
    k = k_ref[...].astype(F32)
    v = v_ref[...].astype(F32)
    heads = []
    for h in range(2):
        inside = (lane < hd) if h == 0 else (lane >= hd)
        base = hd if h == 0 else 0
        bias = jnp.broadcast_to(gate_column(c_ref, h, length, rows), (rows, wide))
        kx = jnp.where(inside, k, side(lane, base, pieces(bias), 0.0)).astype(BF16)
        qx = jnp.where(inside, q, side(lane, base, (1.0, 1.0, 1.0), 0.0)).astype(BF16)
        vx = jnp.where(inside, v, 1.0).astype(BF16)
        heads.append((qx, kx, vx))
    tri = lax.broadcasted_iota(jnp.int32, (blk, blk), 1) <= lax.broadcasted_iota(jnp.int32, (blk, blk), 0)
    for i in range(rows // blk):
        lo, hi = i * blk, (i + 1) * blk
        got = []
        for h in range(2):
            qx, kx, vx = heads[h]
            s_d = jnp.where(tri, nt(qx[lo:hi], kx[lo:hi]), NEG_BIG)
            m = jnp.max(s_d, axis=1, keepdims=True)
            if i:
                s_o = nt(qx[lo:hi], kx[:lo])
                m = jnp.maximum(m, jnp.max(s_o, axis=1, keepdims=True))
            r = nn(jnp.exp(s_d - m).astype(BF16), vx[lo:hi])
            if i:
                r = r + nn(jnp.exp(s_o - m).astype(BF16), vx[:lo])
            total = pltpu.roll(r, hd, 1)
            got.append((r / total, m + jnp.log(total)))
        pos = lo + lax.broadcasted_iota(jnp.int32, (blk, wide), 0)
        o = jnp.where(lane_b < hd, got[0][0], got[1][0])
        o_ref[lo:hi, :] = jnp.where(pos < length, o, 0.0).astype(BF16)
        l_ref[lo:hi, :] = jnp.where(lane_b < hd, got[0][1], got[1][1])

def attn_fwd(length, q, k, v, c, blk=256):
    rows, cols = q.shape
    pairs = cols // 128
    spec = pl.BlockSpec((rows, 128), lambda p: (0, p))
    return pl.pallas_call(
        functools.partial(attn_fwd_kernel, blk=blk),
        grid=(pairs,),
        in_specs=[pl.BlockSpec(memory_space=pltpu.SMEM), spec, spec, spec,
                  pl.BlockSpec((1, rows, 2), lambda p: (p, 0, 0))],
        out_specs=[spec, spec],
        out_shape=[jax.ShapeDtypeStruct((rows, cols), BF16), jax.ShapeDtypeStruct((rows, cols), F32)],
        compiler_params=pltpu.CompilerParams(vmem_limit_bytes=VMEM_BYTES),
        cost_estimate=pl.CostEstimate(flops=rows*rows*128*4*pairs*2, bytes_accessed=rows*cols*12, transcendentals=rows*rows*pairs),
    )(length, q, k, v, c)

def attn_bwd_kernel(len_ref, q_ref, k_ref, v_ref, c_ref, l_ref, o_ref, g_ref, dq_ref, dk_ref, dv_ref, dc_ref, acc_k, acc_v, *, blk):
    rows, wide = q_ref.shape
    hd = wide // 2
    length = len_ref[0]
    lane = lax.broadcasted_iota(jnp.int32, (rows, wide), 1)
    q = q_ref[...].astype(F32) * 0.125
    k = k_ref[...].astype(F32)
    v = v_ref[...].astype(F32)
    g = g_ref[...].astype(F32)
    go = g * o_ref[...].astype(F32)
    tri = lax.broadcasted_iota(jnp.int32, (blk, blk), 0) <= lax.broadcasted_iota(jnp.int32, (blk, blk), 1)
    res = []
    for h in range(2):
        inside = (lane < hd) if h == 0 else (lane >= hd)
        base = hd if h == 0 else 0
        bias = jnp.broadcast_to(gate_column(c_ref, h, length, rows), (rows, wide))
        logt = l_ref[...]
        logt = jnp.where(inside, pltpu.roll(logt, hd, 1), logt)
        other = pltpu.roll(l_ref[...], hd, 1)
        logt = jnp.where(inside, l_ref[...], other)
        dot_o = jnp.broadcast_to(jnp.sum(jnp.where(inside, go, 0.0), axis=1, keepdims=True), (rows, wide))
        kx = jnp.where(inside, k, side(lane, base, pieces(bias) + (1.0, 1.0, 1.0), 0.0)).astype(BF16)
        qx = jnp.where(inside, q, side(lane, base, (1.0, 1.0, 1.0) + pieces(-logt), 0.0)).astype(BF16)
        vx = jnp.where(inside, v, side(lane, base, (1.0, 1.0, 1.0), 0.0)).astype(BF16)
        gx = jnp.where(inside, g, side(lane, base, pieces(-dot_o), 0.0)).astype(BF16)
        kt = kx.T
        dq_parts = []
        for i in range(rows // blk):
            lo, hi = i * blk, (i + 1) * blk
            dqt = None
            for a, b, diag in ((lo, hi, True),) + (((0, lo, False),) if i else ()):
                s = nt(kx[a:b], qx[lo:hi])
                if diag:
                    s = jnp.where(tri, s, NEG_BIG)
                p = jnp.exp(s)
                ds = (p * nt(vx[a:b], gx[lo:hi])).astype(BF16)
                dv = nn(p.astype(BF16), g_ref[lo:hi, :])
                dk = nn(ds, qx[lo:hi])
                t = nn(kt[:, a:b], ds)
                dqt = t if dqt is None else dqt + t
                if diag:
                    acc_v[a:b, :] = dv
                    acc_k[a:b, :] = dk
                else:
                    acc_v[a:b, :] += dv
                    acc_k[a:b, :] += dk
            dq_parts.append(dqt.T)
        dq = jnp.concatenate(dq_parts, axis=0)
        dk = acc_k[...]
        res.append((dq, dk, acc_v[...], dq - pltpu.roll(dk, 3, 1)))
    first = lane < hd
    dq_ref[...] = jnp.where(first, res[0][0] * 0.125, res[1][0] * 0.125).astype(BF16)
    dk_ref[...] = jnp.where(first, res[0][1], res[1][1]).astype(BF16)
    dv_ref[...] = jnp.where(first, res[0][2], res[1][2]).astype(BF16)
    dc_ref[...] = jnp.where(first, res[1][3], res[0][3])

def attn_bwd(length, q, k, v, c, l, o, g, blk=256):
    rows, cols = q.shape
    pairs = cols // 128
    spec = pl.BlockSpec((rows, 128), lambda p: (0, p))
    low = jax.ShapeDtypeStruct((rows, cols), BF16)
    dq, dk, dv, dc = pl.pallas_call(
        functools.partial(attn_bwd_kernel, blk=blk),
        grid=(pairs,),
        in_specs=[pl.BlockSpec(memory_space=pltpu.SMEM), spec, spec, spec,
                  pl.BlockSpec((1, rows, 2), lambda p: (p, 0, 0)), spec, spec, spec],
        out_specs=[spec]*4,
        out_shape=[low, low, low, jax.ShapeDtypeStruct((rows, cols), F32)],
        scratch_shapes=[pltpu.VMEM((rows, 128), F32)]*2,
        compiler_params=pltpu.CompilerParams(vmem_limit_bytes=VMEM_BYTES),
        cost_estimate=pl.CostEstimate(flops=rows*rows*128*10*pairs*2, bytes_accessed=rows*cols*24, transcendentals=rows*rows*pairs),
    )(length, q, k, v, c, l, o, g)
    d3 = dc.reshape(rows, pairs, 128)
    grad_cumul = jnp.stack([d3[:, :, 67], d3[:, :, 3]], axis=2).reshape(rows, 2 * pairs)
    return dq, dk, dv, grad_cumul


def whole(array):
    return pl.BlockSpec(array.shape, lambda *_: (0,) * array.ndim, pipeline_mode=pl.Buffered(1))


def cost(flops, arrays, more=0):
    size = sum(a.size * a.dtype.itemsize for a in arrays)
    return pl.CostEstimate(flops=flops, bytes_accessed=size + more, transcendentals=0)


def joined(refs, lo=None, hi=None):
    if lo is None:
        return jnp.concatenate([r[...] for r in refs], axis=1)
    return jnp.concatenate([r[lo:hi, :] for r in refs], axis=1)


def project_kernel(x_ref, *refs, shard):
    w_refs, (q_ref, k_ref, v_ref, f_ref) = refs[:-4], refs[-4:]
    step = w_refs[0].shape[0] // 2
    x = x_ref[...]
    for kind, out in enumerate((q_ref, k_ref, v_ref)):
        rows = [joined(w_refs, t * step + kind * shard, t * step + (kind + 1) * shard) for t in range(2)]
        out[...] = nt(x, jnp.concatenate(rows, axis=0)).astype(BF16)
    rows = [joined(w_refs, t * step + 3 * shard, (t + 1) * step) for t in range(2)]
    f_ref[0] = nt(x, jnp.concatenate(rows, axis=0))


def project(x, weights, shard, few):
    rows = x.shape[0]
    step = weights[0].shape[0] // 2
    low = jax.ShapeDtypeStruct((rows, 4 * shard), BF16)
    spec = pl.BlockSpec((rows, 2 * shard), lambda i: (0, i))
    pad = step // 2 - 3 * shard
    q, k, v, f = pl.pallas_call(
        functools.partial(project_kernel, shard=shard),
        grid=(2,),
        in_specs=[whole(x)]
        + [pl.BlockSpec((step, w.shape[1]), lambda i: (i, 0)) for w in weights],
        out_specs=[spec, spec, spec, pl.BlockSpec((1, rows, 2 * pad), lambda i: (i, 0, 0))],
        out_shape=[low, low, low, jax.ShapeDtypeStruct((2, rows, 2 * pad), F32)],
        compiler_params=pltpu.CompilerParams(vmem_limit_bytes=VMEM_BYTES),
        cost_estimate=cost(2 * rows * x.shape[1] * 4 * step // 2, [x, *weights, low, low, low]),
        name="project",
    )(x, *weights)
    logits = f.reshape(2, rows, 2, pad)[..., :few].transpose(1, 0, 2, 3).reshape(rows, 4 * few)
    return q, k, v, logits


def combine_kernel(core_ref, *refs, lefts):
    left_refs, w_refs, (give_ref, keep_ref) = refs[:lefts], refs[lefts:-2], refs[-2:]
    step = pl.program_id(0)
    wide = w_refs[0].shape[1]
    for out, cond in ((give_ref, step < 2), (keep_ref, step >= 2)):

        @pl.when(cond)
        def _():
            for n, w in enumerate(w_refs):
                got, at = None, 0
                for left in left_refs:
                    deep = left.shape[1]
                    part = nn(left[...], w[at : at + deep, :])
                    got = part if got is None else got + part
                    at += deep
                out[:, n * wide : (n + 1) * wide] = got.astype(out.dtype)


def combine(core, lefts, weights):
    rows = lefts[0].shape[0]
    wide = weights[0].shape[1] * len(weights)
    block = rows // 4

    def place(i, core_ref):
        mine = core_ref[0]
        return (jnp.where(i < 2, (1 - mine) * 2 + i, mine * 2 + i - 2), 0)

    outs = [
        jax.ShapeDtypeStruct((rows // 2, wide), BF16),
        jax.ShapeDtypeStruct((rows // 2, wide), F32),
    ]
    return pl.pallas_call(
        functools.partial(combine_kernel, lefts=len(lefts)),
        grid_spec=pltpu.PrefetchScalarGridSpec(
            num_scalar_prefetch=1,
            grid=(4,),
            in_specs=[pl.BlockSpec((block, left.shape[1]), place) for left in lefts]
            + [whole(w) for w in weights],
            out_specs=[
                pl.BlockSpec((block, wide), lambda i, c: (jnp.minimum(i, 1), 0)),
                pl.BlockSpec((block, wide), lambda i, c: (jnp.maximum(i - 2, 0), 0)),
            ],
        ),
        out_shape=outs,
        compiler_params=pltpu.CompilerParams(vmem_limit_bytes=VMEM_BYTES),
        cost_estimate=cost(
            2 * rows * weights[0].shape[0] * wide, [*lefts, *weights, *outs]
        ),
        name="combine",
    )(core.reshape(1), *lefts, *weights)


def spread_kernel(len_ref, x_ref, *refs):
    w_refs, out_ref = refs[:-1], refs[-1]
    rows = x_ref.shape[0]
    got = nt(x_ref[...], joined(w_refs))
    pos = pl.program_id(0) * rows + lax.broadcasted_iota(jnp.int32, got.shape, 0)
    out_ref[...] = jnp.where(pos < len_ref[0], got, 0.0).astype(BF16)


def spread(length, x, weights):
    rows, wide = x.shape[0], weights[0].shape[0]
    block = rows // 4
    out = jax.ShapeDtypeStruct((rows, wide), BF16)
    return pl.pallas_call(
        spread_kernel,
        grid=(4,),
        in_specs=[
            pl.BlockSpec(memory_space=pltpu.SMEM),
            pl.BlockSpec((block, x.shape[1]), lambda i: (i, 0)),
        ]
        + [whole(w) for w in weights],
        out_specs=pl.BlockSpec((block, wide), lambda i: (i, 0)),
        out_shape=out,
        compiler_params=pltpu.CompilerParams(vmem_limit_bytes=VMEM_BYTES),
        cost_estimate=cost(2 * rows * x.shape[1] * wide, [x, *weights, out]),
        name="spread",
    )(length, x, *weights)


def inner_kernel(x_ref, *refs):
    w_refs, (gate_ref, up_ref, inner_ref) = refs[:-3], refs[-3:]
    both = nt(x_ref[...], joined(w_refs))
    gate, up = both[:, :UNIT_BLOCK], both[:, UNIT_BLOCK:]
    gate_ref[...] = gate
    up_ref[...] = up
    inner_ref[...] = (gate * jax.nn.sigmoid(gate) * up).astype(BF16)


def inner_units(x, weights):
    rows = x.shape[0]
    total = weights[0].shape[0] // 2
    spec = pl.BlockSpec((rows, UNIT_BLOCK), lambda i: (0, i))
    outs = [jax.ShapeDtypeStruct((rows, total), t) for t in (F32, F32, BF16)]
    return pl.pallas_call(
        inner_kernel,
        grid=(total // UNIT_BLOCK,),
        in_specs=[whole(x)]
        + [pl.BlockSpec((2 * UNIT_BLOCK, w.shape[1]), lambda i: (i, 0)) for w in weights],
        out_specs=[spec] * 3,
        out_shape=outs,
        compiler_params=pltpu.CompilerParams(vmem_limit_bytes=VMEM_BYTES),
        cost_estimate=cost(4 * rows * x.shape[1] * total, [x, *weights, *outs]),
        name="inner_units",
    )(x, *weights)


def inner_grads_kernel(x_ref, gate_ref, up_ref, *refs):
    down_refs, pre_ref = refs[:-1], refs[-1]
    grad = nt(x_ref[...], joined(down_refs))
    gate, up = gate_ref[...], up_ref[...]
    sig = jax.nn.sigmoid(gate)
    pre_ref[:, :UNIT_BLOCK] = (grad * up * (sig * (1.0 + gate * (1.0 - sig)))).astype(BF16)
    pre_ref[:, UNIT_BLOCK:] = (grad * (gate * sig)).astype(BF16)


def inner_grads(x, gate, up, down):
    rows, cols = x.shape
    total = gate.shape[1]
    spec = pl.BlockSpec((rows, UNIT_BLOCK), lambda i: (0, i))
    out = jax.ShapeDtypeStruct((rows, 2 * total), BF16)
    return pl.pallas_call(
        inner_grads_kernel,
        grid=(total // UNIT_BLOCK,),
        in_specs=[whole(x), spec, spec]
        + [pl.BlockSpec((UNIT_BLOCK, w.shape[1]), lambda i: (i, 0)) for w in down],
        out_specs=pl.BlockSpec((rows, 2 * UNIT_BLOCK), lambda i: (0, i)),
        out_shape=out,
        compiler_params=pltpu.CompilerParams(vmem_limit_bytes=VMEM_BYTES),
        cost_estimate=cost(2 * rows * cols * total, [x, gate, up, *down, out]),
        name="inner_grads",
    )(x, gate, up, *down)


class Plan:
    def __init__(self, ways_dp, ways_tensor):
        self.ways_dp = ways_dp
        self.ways_tensor = ways_tensor
        self.chips = ways_dp // 2
        self.bits = self.chips.bit_length() - 1
        assert self.chips == 1 << self.bits and ways_tensor == 4
        dp = lax.axis_index("dp")
        self.chip = dp // 2
        self.core = dp % 2
        self.place = lax.axis_index("tensor")
        self.core_perm = [(i, i ^ 1) for i in range(ways_dp)]

    def swap_core(self, array):
        return lax.ppermute(array, "dp", self.core_perm)

    def swap_chip(self, array, bit):
        perm = [(i, i ^ (2 << bit)) for i in range(self.ways_dp)]
        return lax.ppermute(array, "dp", perm)

    def route(self, turn):
        pairs = []
        for chip in range(self.chips):
            for core in range(2):
                for z in range(4):
                    micro = (z + turn) % 2
                    source = (2 * chip + core) * 4 + z
                    target = (2 * chip + z // 2) * 4 + 2 * micro + core
                    pairs.append((source, target))
        return pairs

    def by_chip(self, array):
        lead = array.shape[:-1]
        wide = array.shape[-1] // self.chips
        parts = [
            lax.dynamic_slice_in_dim(array, (self.chip ^ r) * wide, wide, axis=-1)
            for r in range(self.chips)
        ]
        return jnp.concatenate(parts, axis=-1).reshape(*lead, -1)

    def to_chip(self, array):
        got = []
        for turn in range(2):
            micro = (self.place + turn) % 2
            part = lax.dynamic_index_in_dim(array, micro, 0, keepdims=False)
            got.append(lax.ppermute(self.by_chip(part), ("dp", "tensor"), self.route(turn)))
        first = self.place // 2 == 0
        return jnp.concatenate(
            [jnp.where(first, got[0], got[1]), jnp.where(first, got[1], got[0])], axis=0
        )

    def from_chip(self, array):
        rows = array.shape[0] // 2
        got = []
        for turn in range(2):
            block = (self.place // 2 + turn) % 2
            part = lax.dynamic_slice_in_dim(array, block * rows, rows, axis=0)
            back = [(b, a) for a, b in self.route(turn)]
            got.append(lax.ppermute(self.by_chip(part), ("dp", "tensor"), back))
        first = self.place % 2 == 0
        return jnp.stack([jnp.where(first, got[0], got[1]), jnp.where(first, got[1], got[0])])

    def both_rows(self, half):
        other = self.swap_core(half)
        first = self.core == 0
        return jnp.concatenate(
            [jnp.where(first, half, other), jnp.where(first, other, half)], axis=0
        )

    def sum_rows(self, give, keep):
        return keep + self.swap_core(give).astype(F32)

    def line_gather(self, shard):
        mine = lax.dynamic_index_in_dim(shard, self.core, 0, keepdims=False)
        theirs = lax.dynamic_index_in_dim(shard, 1 - self.core, 0, keepdims=False)
        other = self.swap_core(theirs)
        first = self.core == 0
        pair = jnp.concatenate(
            [jnp.where(first, mine, other), jnp.where(first, other, mine)], axis=1
        )
        return lax.all_gather(pair, "tensor", axis=0, tiled=True)

    def near_gather(self, own):
        if self.bits == 2:
            return [own, self.swap_chip(own, 0), self.swap_chip(own, 1)]
        parts = [own]
        for bit in range(self.bits):
            parts = parts + [self.swap_chip(p, bit) for p in parts]
        return [jnp.concatenate(parts, axis=1)]

    def far_gather(self, near):
        if self.bits != 2:
            return near
        own, by_x, by_y = near
        half = own.shape[0] // 2
        far_top = self.swap_chip(by_x[:half], 1)
        far_low = self.swap_chip(by_y[half:], 0)
        return [own, by_x, by_y, jnp.concatenate([far_top, far_low], axis=0)]

    def scatter(self, total):
        return lax.psum_scatter(total, "tensor", scatter_dimension=0, tiled=True)

    def share(self, pair):
        narrow = pair.shape[1] // 2
        mine = lax.dynamic_slice_in_dim(pair, self.core * narrow, narrow, axis=1)
        theirs = lax.dynamic_slice_in_dim(pair, (1 - self.core) * narrow, narrow, axis=1)
        other = self.swap_core(theirs)
        first = self.core == 0
        return jnp.stack([jnp.where(first, mine, other), jnp.where(first, other, mine)]).astype(F32)

    def sum_all(self, vector):
        vector = vector + self.swap_core(vector)
        for bit in range(self.bits):
            vector = vector + self.swap_chip(vector, bit)
        for bit in range(2):
            perm = [(z, z ^ (1 << bit)) for z in range(4)]
            vector = vector + lax.ppermute(vector, "tensor", perm)
        return vector


class Reduction:
    def __init__(self, plan, lefts, right):
        self.plan, self.lefts, self.right = plan, lefts, right
        self.wide = right.shape[1] // plan.chips
        self.staged = plan.bits == 2
        if self.staged:
            self.first = [
                self.top(3).astype(BF16),
                self.low(3).astype(BF16),
                self.low(1).astype(BF16),
                self.top(2).astype(BF16),
            ]
        else:
            self.first = [
                jnp.concatenate([self.top(r), self.low(r)], axis=0) for r in range(plan.chips)
            ]

    def term(self, r, side):
        right = self.right[:, r * self.wide : (r + 1) * self.wide]
        parts = []
        for left in self.lefts:
            half = left.shape[1] // 2
            parts.append(dot_first(left[:, side * half : (side + 1) * half], right))
        return parts[0] if len(parts) == 1 else jnp.concatenate(parts, axis=0)

    def top(self, r):
        return self.term(r, 0)

    def low(self, r):
        return self.term(r, 1)

    def by_place(self, half):
        if len(self.lefts) == 1:
            return half
        parts, at = [], 0
        for left in self.lefts:
            parts.append((at, left.shape[1] // 4))
            at += left.shape[1] // 2
        return jnp.concatenate(
            [half[at + n * few : at + (n + 1) * few] for n in range(2) for at, few in parts], axis=0
        )

    def send_first(self):
        if self.staged:
            a, b, c, d = self.first
            swap = self.plan.swap_chip
            self.got = [swap(a, 1), swap(b, 0), swap(c, 0), swap(d, 1)]
        else:
            self.got = list(self.first)

    def prepare_second(self):
        if self.staged:
            far_top, far_low = self.got[:2]
            self.second = [
                (self.top(1) + far_top.astype(F32)).astype(BF16),
                (self.low(2) + far_low.astype(F32)).astype(BF16),
            ]
        else:
            self.second = []

    def send_second(self):
        if self.staged:
            self.last = [self.plan.swap_chip(self.second[0], 0), self.plan.swap_chip(self.second[1], 1)]
        else:
            self.last = []

    def finish(self):
        if self.staged:
            x_top, y_low = self.last
            x_low, y_top = self.got[2:]
            top = self.top(0) + x_top.astype(F32) + y_top.astype(F32)
            low = self.low(0) + x_low.astype(F32) + y_low.astype(F32)
            total = jnp.concatenate([self.by_place(top.astype(BF16)), self.by_place(low.astype(BF16))], axis=0)
        else:
            parts = self.got
            for bit in reversed(range(self.plan.bits)):
                keep, give = parts[: 1 << bit], parts[1 << bit :]
                parts = [
                    k + self.plan.swap_chip(g.astype(BF16), bit).astype(F32)
                    for k, g in zip(keep, give)
                ]
            half = parts[0].shape[0] // 2
            total = jnp.concatenate(
                [self.by_place(parts[0][:half]), self.by_place(parts[0][half:])], axis=0
            )
        return total.astype(BF16)


def together(*groups):
    return lax.optimization_barrier(groups)


def split_columns(matrix):
    return matrix.T.reshape(2, matrix.shape[1] // 2, matrix.shape[0])


def split_rows(matrix):
    return matrix.reshape(2, matrix.shape[0] // 2, matrix.shape[1])


def body(
    inputs,
    seq_lengths,
    seq_assign,
    norm1_gain,
    w_query,
    w_key,
    w_value,
    w_forget,
    forget_bias,
    w_out,
    norm2_gain,
    w_gate,
    w_up,
    w_down,
    out_grad,
):
    plan = Plan(lax.axis_size("dp"), lax.axis_size("tensor"))
    core, place = plan.core, plan.place
    part_rows = inputs.shape[1]
    seq_rows = part_rows * 4
    half_rows = seq_rows // 2
    heads_shard = w_forget.shape[1] // 2
    heads_here = heads_shard * 4
    shard_cols = w_query.shape[1] // 2
    blocks = w_gate.shape[1] // 2 // UNIT_BLOCK

    def by_block(matrix):
        return split_columns(matrix).reshape(2, blocks, 1, UNIT_BLOCK, matrix.shape[0])

    forget_part = jnp.pad(
        split_columns(w_forget), ((0, 0), (0, FORGET_PAD - heads_shard), (0, 0))
    )
    line_one = plan.line_gather(
        jnp.concatenate(
            [split_columns(w_query), split_columns(w_key), split_columns(w_value), forget_part],
            axis=1,
        )
    )
    inputs, line_one = together(inputs, line_one)
    rows_one = line_one.shape[0] // 4

    def by_kind(piece):
        piece = piece.reshape(4, rows_one, -1)
        edges = [0, shard_cols, 2 * shard_cols, 3 * shard_cols, rows_one]
        parts = [piece[:, a:b].reshape(-1, piece.shape[-1]) for a, b in zip(edges, edges[1:])]
        return jnp.concatenate(parts, axis=0)

    full_one = plan.far_gather(plan.near_gather(line_one))
    rows_in = plan.to_chip(inputs)
    rows_in, full_one = together(rows_in, full_one)
    rows_in = rows_in.astype(F32)
    line_mid = plan.line_gather(
        jnp.concatenate([split_rows(w_out), split_rows(w_down)], axis=1)
    )
    line_mid, full_one = together(line_mid, full_one)
    line_mid = line_mid.reshape(4, -1, line_mid.shape[-1])
    near_out = plan.near_gather(line_mid[:, :shard_cols].reshape(4 * shard_cols, -1))
    near_down = plan.near_gather(line_mid[:, shard_cols:].reshape(-1, line_mid.shape[-1]))
    two_part = jnp.concatenate([by_block(w_gate), by_block(w_up)], axis=2)
    line_two = plan.line_gather(two_part.reshape(2, -1, two_part.shape[-1]))

    other_assign = plan.swap_core(seq_assign)
    assign_both = jnp.where(
        core == 0,
        jnp.concatenate([seq_assign, other_assign], axis=1),
        jnp.concatenate([other_assign, seq_assign], axis=1),
    ).reshape(4)
    seq_id = jnp.sum(jnp.where(jnp.arange(4) == place, assign_both, 0))
    length = jnp.sum(jnp.where(jnp.arange(seq_lengths.shape[0]) == seq_id, seq_lengths, 0))
    count = length.reshape(1)
    valid_here = (core * half_rows + jnp.arange(half_rows) < length).astype(F32)[:, None]

    gain_one = plan.by_chip(norm1_gain)
    gain_two = plan.by_chip(norm2_gain)
    bias_here = lax.dynamic_index_in_dim(
        forget_bias.reshape(4, 2, heads_shard), core, 1, keepdims=False
    ).reshape(-1)

    scale_one = row_scale(rows_in)
    normed_one = plan.both_rows((rows_in * scale_one * gain_one).astype(BF16))
    queries, key_rows, value_rows, logits = project(
        normed_one, full_one, shard_cols, heads_shard
    )
    forget_logit = logits + bias_here
    cumul_gate = jnp.cumsum(jax.nn.log_sigmoid(forget_logit), axis=0)
    gate_pairs = cumul_gate.reshape(seq_rows, heads_here // 2, 2).transpose(1, 0, 2)
    near_out, gate_pairs = together(near_out, gate_pairs)
    full_out, line_two, gate_pairs = together(plan.far_gather(near_out), line_two, gate_pairs)
    mixed_low, log_total = attn_fwd(count, queries, key_rows, value_rows, gate_pairs)
    mixed_low, near_down, full_one = together(mixed_low, near_down, full_one)
    kinds_one = [by_kind(piece) for piece in full_one]
    full_down = plan.far_gather(near_down)
    near_two, out_grad = together(plan.near_gather(line_two), out_grad)
    full_two = plan.far_gather(near_two)
    cotangent = plan.to_chip(out_grad).astype(F32)
    hidden_in = rows_in + plan.sum_rows(*combine(core, [mixed_low], full_out))

    scale_two = row_scale(hidden_in)
    normed_two = plan.both_rows((hidden_in * scale_two * gain_two).astype(BF16))
    normed_two, full_down, kinds_one = together(normed_two, full_down, kinds_one)
    gate_pre, up_pre, inner_low = inner_units(normed_two, full_two)
    grad_ffn = plan.both_rows((valid_here * cotangent).astype(BF16))
    down_sum = Reduction(plan, [inner_low], grad_ffn)
    down_sum.first, gate_pre = together(down_sum.first, gate_pre)
    down_sum.send_first()

    grad_pre = inner_grads(grad_ffn, gate_pre, up_pre, full_down)
    down_far, grad_pre = together(down_sum.got[:2], grad_pre)
    down_sum.got = [*down_far, *down_sum.got[2:]]
    two_sum = Reduction(plan, [grad_pre], normed_two)
    two_sum.first, down_sum.got, grad_pre = together(two_sum.first, down_sum.got, grad_pre)
    two_sum.send_first()
    down_sum.prepare_second()
    give_two, keep_two = combine(core, [grad_pre], full_two)
    give_ffn, keep_ffn = combine(core, [inner_low], full_down)
    down_sum.send_second()
    two_far, down_sum.last, give_two, give_ffn = together(
        two_sum.got[:2], down_sum.last, give_two, give_ffn
    )
    two_sum.got = [*two_far, *two_sum.got[2:]]
    grad_normed_two = plan.sum_rows(give_two, keep_two)
    gain_two_term = jnp.sum(grad_normed_two * hidden_in * scale_two, axis=0)
    grad_hidden = valid_here * cotangent + norm_back(
        hidden_in, scale_two, gain_two, grad_normed_two
    )

    grad_attn = plan.both_rows(grad_hidden.astype(BF16))
    out_sum = Reduction(plan, [mixed_low], grad_attn)
    two_sum.prepare_second()
    out_sum.first, two_sum.second, grad_attn = together(
        out_sum.first, two_sum.second, grad_attn
    )
    two_sum.send_second()
    out_sum.send_first()
    ffn_rows = plan.sum_rows(give_ffn, keep_ffn)
    outputs = (valid_here * (hidden_in + ffn_rows)).astype(BF16)
    grad_mixed = spread(count, grad_attn, full_out)
    query_low, key_low, value_low, grad_cumul = attn_bwd(
        count, queries, key_rows, value_rows, gate_pairs, log_total, mixed_low, grad_mixed
    )
    two_sum.got, two_sum.last, out_sum.got, query_low, key_low, value_low, grad_cumul = together(
        two_sum.got, two_sum.last, out_sum.got, query_low, key_low, value_low, grad_cumul
    )
    out_sum.prepare_second()
    out_sum.second, outputs, grad_cumul = together(out_sum.second, outputs, grad_cumul)
    outputs = plan.from_chip(outputs)
    out_sum.send_second()
    grad_logf = jnp.flip(jnp.cumsum(jnp.flip(grad_cumul, 0), axis=0), 0)
    grad_logit = grad_logf * jax.nn.sigmoid(-forget_logit)
    bias_term = jnp.sum(grad_logit, axis=0)
    logit_low = jnp.pad(
        grad_logit.astype(BF16).reshape(seq_rows, 4, heads_shard),
        ((0, 0), (0, 0), (0, FORGET_PAD - heads_shard)),
    ).reshape(seq_rows, -1)
    grad_one = [query_low, key_low, value_low, logit_low]
    one_sum = Reduction(plan, grad_one, normed_one)
    one_sum.first, out_sum.last = together(one_sum.first, out_sum.last)
    one_sum.send_first()
    one_far, grad_one = together(one_sum.got[:2], grad_one)
    one_sum.got = [*one_far, *one_sum.got[2:]]
    down_pair = plan.scatter(down_sum.finish())
    two_total, down_pair, outputs = together(two_sum.finish(), down_pair, outputs)
    two_pair = plan.scatter(two_total)
    grad_normed_one = plan.sum_rows(*combine(core, grad_one, kinds_one))
    gain_one_term = jnp.sum(grad_normed_one * rows_in * scale_one, axis=0)
    input_grad = plan.from_chip(
        (grad_hidden + norm_back(rows_in, scale_one, gain_one, grad_normed_one)).astype(BF16)
    )
    one_sum.prepare_second()
    one_sum.send_second()

    bias_full = jnp.where(
        (jnp.arange(2) == core)[None, :, None], bias_term.reshape(4, 1, heads_shard), 0.0
    ).reshape(-1)
    wide = norm1_gain.shape[0]
    small = plan.sum_all(
        jnp.concatenate([plan.by_chip(gain_one_term), plan.by_chip(gain_two_term), bias_full])
    )

    out_total, two_pair = together(out_sum.finish(), two_pair)
    out_pair = plan.scatter(out_total)
    one_total, out_pair, input_grad = together(one_sum.finish(), out_pair, input_grad)
    one_pair = plan.scatter(one_total)
    down_shard, two_shard = plan.share(down_pair), plan.share(two_pair)
    out_shard, one_shard = plan.share(out_pair), plan.share(one_pair)

    two_shard = two_shard.reshape(2, blocks, 2, UNIT_BLOCK, -1)

    def columns(shard):
        return shard.reshape(-1, shard.shape[-1]).T

    def rows(shard):
        return shard.reshape(-1, shard.shape[-1])

    return (
        outputs,
        input_grad,
        small[:wide],
        columns(one_shard[:, :shard_cols]),
        columns(one_shard[:, shard_cols : 2 * shard_cols]),
        columns(one_shard[:, 2 * shard_cols : 3 * shard_cols]),
        columns(one_shard[:, 3 * shard_cols : 3 * shard_cols + heads_shard]),
        small[2 * wide :],
        rows(out_shard),
        small[wide : 2 * wide],
        columns(two_shard[:, :, 0]),
        columns(two_shard[:, :, 1]),
        rows(down_shard),
    )


def solution(mesh):
    return jax.shard_map(
        body,
        mesh=mesh,
        in_specs=(
            P(None, ("dp", "tensor"), None),
            P(),
            P(None, "dp"),
            P(),
            P("dp", "tensor"),
            P("dp", "tensor"),
            P("dp", "tensor"),
            P("dp", "tensor"),
            P(),
            P("tensor", "dp"),
            P(),
            P("dp", "tensor"),
            P("dp", "tensor"),
            P("tensor", "dp"),
            P(None, ("dp", "tensor"), None),
        ),
        out_specs=(
            P(None, ("dp", "tensor"), None),
            P(None, ("dp", "tensor"), None),
            P(),
            P("dp", "tensor"),
            P("dp", "tensor"),
            P("dp", "tensor"),
            P("dp", "tensor"),
            P(),
            P("tensor", "dp"),
            P(),
            P("dp", "tensor"),
            P("dp", "tensor"),
            P("tensor", "dp"),
        ),
        check_vma=False,
    )
```

```python
import functools

import jax
import jax.numpy as jnp
from jax import lax
from jax.experimental import pallas as pl
from jax.experimental.pallas import tpu as pltpu
from jax.sharding import PartitionSpec as P

EPS = 1e-06
NEG_BIG = -1e30
F32 = jnp.float32
BF16 = jnp.bfloat16
FORGET_PAD = 16
UNIT_BLOCK = 256
VMEM_BYTES = 60 << 20


def row_scale(tokens):
    return lax.rsqrt(jnp.mean(tokens * tokens, axis=-1, keepdims=True) + EPS)


def norm_back(tokens, scaling, gain, grad_out):
    weighted = grad_out * gain
    cubed = scaling * scaling * scaling
    return scaling * weighted - tokens * cubed * jnp.mean(weighted * tokens, axis=-1, keepdims=True)


def dot_first(left, right):
    return lax.dot_general(left, right, (((0,), (0,)), ((), ())), preferred_element_type=F32)

def nt(a, b):
    return lax.dot_general(a, b, (((1,), (1,)), ((), ())), preferred_element_type=F32)

def nn(a, b):
    return lax.dot_general(a, b, (((1,), (0,)), ((), ())), preferred_element_type=F32)

def pieces(x):
    top = x.astype(BF16).astype(F32)
    rest = x - top
    mid = rest.astype(BF16).astype(F32)
    return top, mid, rest - mid

def side(lane, base, values, rest):
    for n, value in enumerate(values):
        rest = jnp.where(lane == base + n, value, rest)
    return rest

def gate_column(c_ref, which, length, rows):
    col = c_ref[0, :, which : which + 1]
    pos = lax.broadcasted_iota(jnp.int32, (rows, 1), 0)
    return jnp.where(pos < length, -col, NEG_BIG)

def attn_fwd_kernel(len_ref, q_ref, k_ref, v_ref, c_ref, o_ref, l_ref, *, blk):
    rows, wide = q_ref.shape
    hd = wide // 2
    length = len_ref[0]
    lane = lax.broadcasted_iota(jnp.int32, (rows, wide), 1)
    lane_b = lax.broadcasted_iota(jnp.int32, (blk, wide), 1)
    q = q_ref[...].astype(F32) * 0.125
    k = k_ref[...].astype(F32)
    v = v_ref[...].astype(F32)
    heads = []
    for h in range(2):
        inside = (lane < hd) if h == 0 else (lane >= hd)
        base = hd if h == 0 else 0
        bias = jnp.broadcast_to(gate_column(c_ref, h, length, rows), (rows, wide))
        kx = jnp.where(inside, k, side(lane, base, pieces(bias), 0.0)).astype(BF16)
        qx = jnp.where(inside, q, side(lane, base, (1.0, 1.0, 1.0), 0.0)).astype(BF16)
        vx = jnp.where(inside, v, 1.0).astype(BF16)
        heads.append((qx, kx, vx))
    tri = lax.broadcasted_iota(jnp.int32, (blk, blk), 1) <= lax.broadcasted_iota(jnp.int32, (blk, blk), 0)
    for i in range(rows // blk):
        lo, hi = i * blk, (i + 1) * blk
        got = []
        for h in range(2):
            qx, kx, vx = heads[h]
            s_d = jnp.where(tri, nt(qx[lo:hi], kx[lo:hi]), NEG_BIG)
            m = jnp.max(s_d, axis=1, keepdims=True)
            if i:
                s_o = nt(qx[lo:hi], kx[:lo])
                m = jnp.maximum(m, jnp.max(s_o, axis=1, keepdims=True))
            r = nn(jnp.exp(s_d - m).astype(BF16), vx[lo:hi])
            if i:
                r = r + nn(jnp.exp(s_o - m).astype(BF16), vx[:lo])
            total = pltpu.roll(r, hd, 1)
            got.append((r / total, m + jnp.log(total)))
        pos = lo + lax.broadcasted_iota(jnp.int32, (blk, wide), 0)
        o = jnp.where(lane_b < hd, got[0][0], got[1][0])
        o_ref[lo:hi, :] = jnp.where(pos < length, o, 0.0).astype(BF16)
        l_ref[lo:hi, :] = jnp.where(lane_b < hd, got[0][1], got[1][1])

def attn_fwd(length, q, k, v, c, blk=256):
    rows, cols = q.shape
    pairs = cols // 128
    spec = pl.BlockSpec((rows, 128), lambda p: (0, p))
    return pl.pallas_call(
        functools.partial(attn_fwd_kernel, blk=blk),
        grid=(pairs,),
        in_specs=[pl.BlockSpec(memory_space=pltpu.SMEM), spec, spec, spec,
                  pl.BlockSpec((1, rows, 2), lambda p: (p, 0, 0))],
        out_specs=[spec, spec],
        out_shape=[jax.ShapeDtypeStruct((rows, cols), BF16), jax.ShapeDtypeStruct((rows, cols), F32)],
        compiler_params=pltpu.CompilerParams(vmem_limit_bytes=VMEM_BYTES),
        cost_estimate=pl.CostEstimate(flops=rows*rows*128*4*pairs*2, bytes_accessed=rows*cols*12, transcendentals=rows*rows*pairs),
    )(length, q, k, v, c)

def attn_bwd_kernel(len_ref, q_ref, k_ref, v_ref, c_ref, l_ref, o_ref, g_ref, dq_ref, dk_ref, dv_ref, dc_ref, acc_k, acc_v, *, blk):
    rows, wide = q_ref.shape
    hd = wide // 2
    length = len_ref[0]
    lane = lax.broadcasted_iota(jnp.int32, (rows, wide), 1)
    q = q_ref[...].astype(F32) * 0.125
    k = k_ref[...].astype(F32)
    v = v_ref[...].astype(F32)
    g = g_ref[...].astype(F32)
    go = g * o_ref[...].astype(F32)
    tri = lax.broadcasted_iota(jnp.int32, (blk, blk), 0) <= lax.broadcasted_iota(jnp.int32, (blk, blk), 1)
    res = []
    for h in range(2):
        inside = (lane < hd) if h == 0 else (lane >= hd)
        base = hd if h == 0 else 0
        bias = jnp.broadcast_to(gate_column(c_ref, h, length, rows), (rows, wide))
        logt = l_ref[...]
        logt = jnp.where(inside, pltpu.roll(logt, hd, 1), logt)
        other = pltpu.roll(l_ref[...], hd, 1)
        logt = jnp.where(inside, l_ref[...], other)
        dot_o = jnp.broadcast_to(jnp.sum(jnp.where(inside, go, 0.0), axis=1, keepdims=True), (rows, wide))
        kx = jnp.where(inside, k, side(lane, base, pieces(bias) + (1.0, 1.0, 1.0), 0.0)).astype(BF16)
        qx = jnp.where(inside, q, side(lane, base, (1.0, 1.0, 1.0) + pieces(-logt), 0.0)).astype(BF16)
        vx = jnp.where(inside, v, side(lane, base, (1.0, 1.0, 1.0), 0.0)).astype(BF16)
        gx = jnp.where(inside, g, side(lane, base, pieces(-dot_o), 0.0)).astype(BF16)
        kt = kx.T
        dq_parts = []
        for i in range(rows // blk):
            lo, hi = i * blk, (i + 1) * blk
            dqt = None
            for a, b, diag in ((lo, hi, True),) + (((0, lo, False),) if i else ()):
                s = nt(kx[a:b], qx[lo:hi])
                if diag:
                    s = jnp.where(tri, s, NEG_BIG)
                p = jnp.exp(s)
                ds = (p * nt(vx[a:b], gx[lo:hi])).astype(BF16)
                dv = nn(p.astype(BF16), g_ref[lo:hi, :])
                dk = nn(ds, qx[lo:hi])
                t = nn(kt[:, a:b], ds)
                dqt = t if dqt is None else dqt + t
                if diag:
                    acc_v[a:b, :] = dv
                    acc_k[a:b, :] = dk
                else:
                    acc_v[a:b, :] += dv
                    acc_k[a:b, :] += dk
            dq_parts.append(dqt.T)
        dq = jnp.concatenate(dq_parts, axis=0)
        dk = acc_k[...]
        res.append((dq, dk, acc_v[...], dq - pltpu.roll(dk, 3, 1)))
    first = lane < hd
    dq_ref[...] = jnp.where(first, res[0][0] * 0.125, res[1][0] * 0.125).astype(BF16)
    dk_ref[...] = jnp.where(first, res[0][1], res[1][1]).astype(BF16)
    dv_ref[...] = jnp.where(first, res[0][2], res[1][2]).astype(BF16)
    dc_ref[...] = jnp.where(first, res[1][3], res[0][3])

def attn_bwd(length, q, k, v, c, l, o, g, blk=256):
    rows, cols = q.shape
    pairs = cols // 128
    spec = pl.BlockSpec((rows, 128), lambda p: (0, p))
    low = jax.ShapeDtypeStruct((rows, cols), BF16)
    dq, dk, dv, dc = pl.pallas_call(
        functools.partial(attn_bwd_kernel, blk=blk),
        grid=(pairs,),
        in_specs=[pl.BlockSpec(memory_space=pltpu.SMEM), spec, spec, spec,
                  pl.BlockSpec((1, rows, 2), lambda p: (p, 0, 0)), spec, spec, spec],
        out_specs=[spec]*4,
        out_shape=[low, low, low, jax.ShapeDtypeStruct((rows, cols), F32)],
        scratch_shapes=[pltpu.VMEM((rows, 128), F32)]*2,
        compiler_params=pltpu.CompilerParams(vmem_limit_bytes=VMEM_BYTES),
        cost_estimate=pl.CostEstimate(flops=rows*rows*128*10*pairs*2, bytes_accessed=rows*cols*24, transcendentals=rows*rows*pairs),
    )(length, q, k, v, c, l, o, g)
    d3 = dc.reshape(rows, pairs, 128)
    grad_cumul = jnp.stack([d3[:, :, 67], d3[:, :, 3]], axis=2).reshape(rows, 2 * pairs)
    return dq, dk, dv, grad_cumul


def whole(array):
    return pl.BlockSpec(array.shape, lambda *_: (0,) * array.ndim, pipeline_mode=pl.Buffered(1))


def cost(flops, arrays, more=0):
    size = sum(a.size * a.dtype.itemsize for a in arrays)
    return pl.CostEstimate(flops=flops, bytes_accessed=size + more, transcendentals=0)


def joined(refs, lo=None, hi=None):
    if lo is None:
        return jnp.concatenate([r[...] for r in refs], axis=1)
    return jnp.concatenate([r[lo:hi, :] for r in refs], axis=1)


def project_kernel(x_ref, *refs, shard):
    w_refs, (q_ref, k_ref, v_ref, f_ref) = refs[:-4], refs[-4:]
    step = w_refs[0].shape[0] // 2
    x = x_ref[...]
    for kind, out in enumerate((q_ref, k_ref, v_ref)):
        rows = [joined(w_refs, t * step + kind * shard, t * step + (kind + 1) * shard) for t in range(2)]
        out[...] = nt(x, jnp.concatenate(rows, axis=0)).astype(BF16)
    rows = [joined(w_refs, t * step + 3 * shard, (t + 1) * step) for t in range(2)]
    f_ref[0] = nt(x, jnp.concatenate(rows, axis=0))


def project(x, weights, shard, few):
    rows = x.shape[0]
    step = weights[0].shape[0] // 2
    low = jax.ShapeDtypeStruct((rows, 4 * shard), BF16)
    spec = pl.BlockSpec((rows, 2 * shard), lambda i: (0, i))
    pad = step // 2 - 3 * shard
    q, k, v, f = pl.pallas_call(
        functools.partial(project_kernel, shard=shard),
        grid=(2,),
        in_specs=[whole(x)]
        + [pl.BlockSpec((step, w.shape[1]), lambda i: (i, 0)) for w in weights],
        out_specs=[spec, spec, spec, pl.BlockSpec((1, rows, 2 * pad), lambda i: (i, 0, 0))],
        out_shape=[low, low, low, jax.ShapeDtypeStruct((2, rows, 2 * pad), F32)],
        compiler_params=pltpu.CompilerParams(vmem_limit_bytes=VMEM_BYTES),
        cost_estimate=cost(2 * rows * x.shape[1] * 4 * step // 2, [x, *weights, low, low, low]),
        name="project",
    )(x, *weights)
    logits = f.reshape(2, rows, 2, pad)[..., :few].transpose(1, 0, 2, 3).reshape(rows, 4 * few)
    return q, k, v, logits


def combine_kernel(core_ref, *refs, lefts):
    left_refs, w_refs, (give_ref, keep_ref) = refs[:lefts], refs[lefts:-2], refs[-2:]
    step = pl.program_id(0)
    wide = w_refs[0].shape[1]
    for n, w in enumerate(w_refs):
        got, at = None, 0
        for left in left_refs:
            deep = left.shape[1]
            part = nn(left[...], w[at : at + deep, :])
            got = part if got is None else got + part
            at += deep
        cols = slice(n * wide, (n + 1) * wide)

        @pl.when(step < 2)
        def _():
            give_ref[:, cols] = got.astype(BF16)

        @pl.when(step >= 2)
        def _():
            keep_ref[:, cols] = got


def combine(core, lefts, weights):
    rows = lefts[0].shape[0]
    wide = weights[0].shape[1] * len(weights)
    block = rows // 4

    def place(i, core_ref):
        mine = core_ref[0]
        return (jnp.where(i < 2, (1 - mine) * 2 + i, mine * 2 + i - 2), 0)

    outs = [
        jax.ShapeDtypeStruct((rows // 2, wide), BF16),
        jax.ShapeDtypeStruct((rows // 2, wide), F32),
    ]
    return pl.pallas_call(
        functools.partial(combine_kernel, lefts=len(lefts)),
        grid_spec=pltpu.PrefetchScalarGridSpec(
            num_scalar_prefetch=1,
            grid=(4,),
            in_specs=[pl.BlockSpec((block, left.shape[1]), place) for left in lefts]
            + [whole(w) for w in weights],
            out_specs=[
                pl.BlockSpec((block, wide), lambda i, c: (jnp.minimum(i, 1), 0)),
                pl.BlockSpec((block, wide), lambda i, c: (jnp.maximum(i - 2, 0), 0)),
            ],
        ),
        out_shape=outs,
        compiler_params=pltpu.CompilerParams(vmem_limit_bytes=VMEM_BYTES),
        cost_estimate=cost(
            2 * rows * weights[0].shape[0] * wide, [*lefts, *weights, *outs]
        ),
        name="combine",
    )(core.reshape(1), *lefts, *weights)


def spread_kernel(len_ref, x_ref, *refs):
    w_refs, out_ref = refs[:-1], refs[-1]
    rows = x_ref.shape[0]
    got = nt(x_ref[...], joined(w_refs))
    pos = pl.program_id(0) * rows + lax.broadcasted_iota(jnp.int32, got.shape, 0)
    out_ref[...] = jnp.where(pos < len_ref[0], got, 0.0).astype(BF16)


def spread(length, x, weights):
    rows, wide = x.shape[0], weights[0].shape[0]
    block = rows // 4
    out = jax.ShapeDtypeStruct((rows, wide), BF16)
    return pl.pallas_call(
        spread_kernel,
        grid=(4,),
        in_specs=[
            pl.BlockSpec(memory_space=pltpu.SMEM),
            pl.BlockSpec((block, x.shape[1]), lambda i: (i, 0)),
        ]
        + [whole(w) for w in weights],
        out_specs=pl.BlockSpec((block, wide), lambda i: (i, 0)),
        out_shape=out,
        compiler_params=pltpu.CompilerParams(vmem_limit_bytes=VMEM_BYTES),
        cost_estimate=cost(2 * rows * x.shape[1] * wide, [x, *weights, out]),
        name="spread",
    )(length, x, *weights)


def inner_kernel(x_ref, *refs):
    w_refs, (gate_ref, up_ref, inner_ref) = refs[:-3], refs[-3:]
    both = nt(x_ref[...], joined(w_refs))
    gate, up = both[:, :UNIT_BLOCK], both[:, UNIT_BLOCK:]
    gate_ref[...] = gate
    up_ref[...] = up
    inner_ref[...] = (gate * jax.nn.sigmoid(gate) * up).astype(BF16)


def inner_units(x, weights):
    rows = x.shape[0]
    total = weights[0].shape[0] // 2
    spec = pl.BlockSpec((rows, UNIT_BLOCK), lambda i: (0, i))
    outs = [jax.ShapeDtypeStruct((rows, total), t) for t in (F32, F32, BF16)]
    return pl.pallas_call(
        inner_kernel,
        grid=(total // UNIT_BLOCK,),
        in_specs=[whole(x)]
        + [pl.BlockSpec((2 * UNIT_BLOCK, w.shape[1]), lambda i: (i, 0)) for w in weights],
        out_specs=[spec] * 3,
        out_shape=outs,
        compiler_params=pltpu.CompilerParams(vmem_limit_bytes=VMEM_BYTES),
        cost_estimate=cost(4 * rows * x.shape[1] * total, [x, *weights, *outs]),
        name="inner_units",
    )(x, *weights)


def inner_grads_kernel(x_ref, gate_ref, up_ref, *refs):
    down_refs, pre_ref = refs[:-1], refs[-1]
    grad = nt(x_ref[...], joined(down_refs))
    gate, up = gate_ref[...], up_ref[...]
    sig = jax.nn.sigmoid(gate)
    pre_ref[:, :UNIT_BLOCK] = (grad * up * (sig * (1.0 + gate * (1.0 - sig)))).astype(BF16)
    pre_ref[:, UNIT_BLOCK:] = (grad * (gate * sig)).astype(BF16)


def inner_grads(x, gate, up, down):
    rows, cols = x.shape
    total = gate.shape[1]
    spec = pl.BlockSpec((rows, UNIT_BLOCK), lambda i: (0, i))
    out = jax.ShapeDtypeStruct((rows, 2 * total), BF16)
    return pl.pallas_call(
        inner_grads_kernel,
        grid=(total // UNIT_BLOCK,),
        in_specs=[whole(x), spec, spec]
        + [pl.BlockSpec((UNIT_BLOCK, w.shape[1]), lambda i: (i, 0)) for w in down],
        out_specs=pl.BlockSpec((rows, 2 * UNIT_BLOCK), lambda i: (0, i)),
        out_shape=out,
        compiler_params=pltpu.CompilerParams(vmem_limit_bytes=VMEM_BYTES),
        cost_estimate=cost(2 * rows * cols * total, [x, gate, up, *down, out]),
        name="inner_grads",
    )(x, gate, up, *down)


def half_products(left_refs, right, side):
    parts = []
    for ref, narrow in left_refs:
        got = dot_first(ref[...], right)
        if narrow:
            few = got.shape[0] // 2
            got = jnp.where(side == 0, got[:few], got[few:])
        parts.append(got)
    return parts


def term_kernel(*refs, narrow, side):
    count = len(narrow)
    right_ref, add_refs, out_ref = refs[count], refs[count + 1 : -1], refs[-1]
    at = 0
    for part in half_products(list(zip(refs[:count], narrow)), right_ref[...], side):
        rows = slice(at, at + part.shape[0])
        for add in add_refs:
            part = part + add[rows, :].astype(F32)
        out_ref[rows, :] = part.astype(BF16)
        at += part.shape[0]


def left_specs(lefts, steps, block):
    specs, narrow = [], []
    for left in lefts:
        rows, cols = left.shape
        wide = cols // (2 * steps)
        narrow.append(wide % 128 != 0)
        if wide % 128:
            specs.append(pl.BlockSpec((rows, cols), lambda i: (0, 0)))
        else:
            specs.append(pl.BlockSpec((rows, wide), lambda i: (0, block(i))))
    return specs, tuple(narrow)


def chunks_of(lefts):
    half = lefts[0].shape[1] // 2
    return max(1, half // 512) if len(lefts) == 1 else 1


def term_sum(lefts, right, side, r, wide, adds=()):
    steps = chunks_of(lefts)
    half = sum(left.shape[1] for left in lefts) // 2
    specs, narrow = left_specs(lefts, steps, lambda i: side * steps + i)
    part = pl.BlockSpec((half // steps, wide), lambda i: (i, 0))
    out = jax.ShapeDtypeStruct((half, wide), BF16)
    return pl.pallas_call(
        functools.partial(term_kernel, narrow=narrow, side=side),
        grid=(steps,),
        in_specs=specs
        + [pl.BlockSpec((right.shape[0], wide), lambda i: (0, r))]
        + [part] * len(adds),
        out_specs=part,
        out_shape=out,
        compiler_params=pltpu.CompilerParams(vmem_limit_bytes=VMEM_BYTES),
        cost_estimate=cost(2 * right.shape[0] * half * wide, [*adds, out, out]),
        name="term_sum",
    )(*lefts, right, *adds)


def total_kernel(*refs, narrow, steps):
    count = len(narrow)
    right_ref, tops, lows, out_ref = refs[count], refs[count + 1 : -3], refs[-3:-1], refs[-1]
    step = pl.program_id(0)
    side = step // steps
    parts = half_products(list(zip(refs[:count], narrow)), right_ref[...], side)
    if count == 1:
        places = [parts]
    else:
        places = [
            [part[n * (part.shape[0] // 2) : (n + 1) * (part.shape[0] // 2)] for part in parts]
            for n in range(2)
        ]
    for this, adds in ((0, tops), (1, lows)):

        @pl.when(side == this)
        def _():
            at = 0
            for n, place in enumerate(places):
                off = 0
                for part, whole_part in zip(place, parts):
                    few = part.shape[0]
                    start = off + n * few if count > 1 else 0
                    got = part
                    for add in adds:
                        got = got + add[start : start + few, :].astype(F32)
                    out_ref[at : at + few, :] = got.astype(BF16)
                    at += few
                    off += whole_part.shape[0]


def total_sum(lefts, right, tops, lows, wide):
    steps = chunks_of(lefts)
    full = sum(left.shape[1] for left in lefts)
    block = full // (2 * steps)
    specs, narrow = left_specs(lefts, steps, lambda i: i)
    out = jax.ShapeDtypeStruct((full, wide), BF16)
    return pl.pallas_call(
        functools.partial(total_kernel, narrow=narrow, steps=steps),
        grid=(2 * steps,),
        in_specs=specs
        + [pl.BlockSpec((right.shape[0], wide), lambda i: (0, 0))]
        + [pl.BlockSpec((block, wide), lambda i: (jnp.minimum(i, steps - 1), 0))] * 2
        + [pl.BlockSpec((block, wide), lambda i: (jnp.maximum(i - steps, 0), 0))] * 2,
        out_specs=pl.BlockSpec((block, wide), lambda i: (i, 0)),
        out_shape=out,
        compiler_params=pltpu.CompilerParams(vmem_limit_bytes=VMEM_BYTES),
        cost_estimate=cost(2 * right.shape[0] * full * wide, [out, out, out]),
        name="total_sum",
    )(*lefts, right, *tops, *lows)


class Plan:
    def __init__(self, ways_dp, ways_tensor):
        self.ways_dp = ways_dp
        self.ways_tensor = ways_tensor
        self.chips = ways_dp // 2
        self.bits = self.chips.bit_length() - 1
        assert self.chips == 1 << self.bits and ways_tensor == 4
        dp = lax.axis_index("dp")
        self.chip = dp // 2
        self.core = dp % 2
        self.place = lax.axis_index("tensor")
        self.core_perm = [(i, i ^ 1) for i in range(ways_dp)]

    def swap_core(self, array):
        return lax.ppermute(array, "dp", self.core_perm)

    def swap_chip(self, array, bit):
        perm = [(i, i ^ (2 << bit)) for i in range(self.ways_dp)]
        return lax.ppermute(array, "dp", perm)

    def route(self, turn):
        pairs = []
        for chip in range(self.chips):
            for core in range(2):
                for z in range(4):
                    micro = (z + turn) % 2
                    source = (2 * chip + core) * 4 + z
                    target = (2 * chip + z // 2) * 4 + 2 * micro + core
                    pairs.append((source, target))
        return pairs

    def by_chip(self, array):
        lead = array.shape[:-1]
        wide = array.shape[-1] // self.chips
        parts = [
            lax.dynamic_slice_in_dim(array, (self.chip ^ r) * wide, wide, axis=-1)
            for r in range(self.chips)
        ]
        return jnp.concatenate(parts, axis=-1).reshape(*lead, -1)

    def to_chip(self, array):
        got = []
        for turn in range(2):
            micro = (self.place + turn) % 2
            part = lax.dynamic_index_in_dim(array, micro, 0, keepdims=False)
            got.append(lax.ppermute(self.by_chip(part), ("dp", "tensor"), self.route(turn)))
        first = self.place // 2 == 0
        return jnp.concatenate(
            [jnp.where(first, got[0], got[1]), jnp.where(first, got[1], got[0])], axis=0
        )

    def from_chip(self, array):
        rows = array.shape[0] // 2
        got = []
        for turn in range(2):
            block = (self.place // 2 + turn) % 2
            part = lax.dynamic_slice_in_dim(array, block * rows, rows, axis=0)
            back = [(b, a) for a, b in self.route(turn)]
            got.append(lax.ppermute(self.by_chip(part), ("dp", "tensor"), back))
        first = self.place % 2 == 0
        return jnp.stack([jnp.where(first, got[0], got[1]), jnp.where(first, got[1], got[0])])

    def both_rows(self, half):
        other = self.swap_core(half)
        first = self.core == 0
        return jnp.concatenate(
            [jnp.where(first, half, other), jnp.where(first, other, half)], axis=0
        )

    def sum_rows(self, give, keep):
        return keep + self.swap_core(give).astype(F32)

    def line_gather(self, shard):
        mine = lax.dynamic_index_in_dim(shard, self.core, 0, keepdims=False)
        theirs = lax.dynamic_index_in_dim(shard, 1 - self.core, 0, keepdims=False)
        other = self.swap_core(theirs)
        first = self.core == 0
        pair = jnp.concatenate(
            [jnp.where(first, mine, other), jnp.where(first, other, mine)], axis=1
        )
        return lax.all_gather(pair, "tensor", axis=0, tiled=True)

    def near_gather(self, own):
        if self.bits == 2:
            return [own, self.swap_chip(own, 0), self.swap_chip(own, 1)]
        parts = [own]
        for bit in range(self.bits):
            parts = parts + [self.swap_chip(p, bit) for p in parts]
        return [jnp.concatenate(parts, axis=1)]

    def far_gather(self, near):
        if self.bits != 2:
            return near
        own, by_x, by_y = near
        half = own.shape[0] // 2
        far_top = self.swap_chip(by_x[:half], 1)
        far_low = self.swap_chip(by_y[half:], 0)
        return [own, by_x, by_y, jnp.concatenate([far_top, far_low], axis=0)]

    def scatter(self, total):
        return lax.psum_scatter(total, "tensor", scatter_dimension=0, tiled=True)

    def share(self, pair):
        narrow = pair.shape[1] // 2
        mine = lax.dynamic_slice_in_dim(pair, self.core * narrow, narrow, axis=1)
        theirs = lax.dynamic_slice_in_dim(pair, (1 - self.core) * narrow, narrow, axis=1)
        other = self.swap_core(theirs)
        first = self.core == 0
        return jnp.stack([jnp.where(first, mine, other), jnp.where(first, other, mine)]).astype(F32)

    def sum_all(self, vector):
        vector = vector + self.swap_core(vector)
        for bit in range(self.bits):
            vector = vector + self.swap_chip(vector, bit)
        for bit in range(2):
            perm = [(z, z ^ (1 << bit)) for z in range(4)]
            vector = vector + lax.ppermute(vector, "tensor", perm)
        return vector


class Reduction:
    def __init__(self, plan, lefts, right):
        self.plan, self.lefts, self.right = plan, lefts, right
        self.wide = right.shape[1] // plan.chips
        self.staged = plan.bits == 2
        if self.staged:
            if len(lefts) == 1:
                self.first = [
                    self.top(3).astype(BF16),
                    self.low(3).astype(BF16),
                    self.low(1).astype(BF16),
                    self.top(2).astype(BF16),
                ]
            else:
                self.first = [self.sent(0, 3), self.sent(1, 3), self.sent(1, 1), self.sent(0, 2)]
        else:
            self.first = [
                jnp.concatenate([self.top(r), self.low(r)], axis=0) for r in range(plan.chips)
            ]

    def term(self, r, side):
        right = self.right[:, r * self.wide : (r + 1) * self.wide]
        parts = []
        for left in self.lefts:
            half = left.shape[1] // 2
            parts.append(dot_first(left[:, side * half : (side + 1) * half], right))
        return parts[0] if len(parts) == 1 else jnp.concatenate(parts, axis=0)

    def sent(self, side, r, *adds):
        return term_sum(self.lefts, self.right, side, r, self.wide, adds)

    def top(self, r):
        return self.term(r, 0)

    def low(self, r):
        return self.term(r, 1)

    def by_place(self, half):
        if len(self.lefts) == 1:
            return half
        parts, at = [], 0
        for left in self.lefts:
            parts.append((at, left.shape[1] // 4))
            at += left.shape[1] // 2
        return jnp.concatenate(
            [half[at + n * few : at + (n + 1) * few] for n in range(2) for at, few in parts], axis=0
        )

    def send_first(self):
        if self.staged:
            a, b, c, d = self.first
            swap = self.plan.swap_chip
            self.got = [swap(a, 1), swap(b, 0), swap(c, 0), swap(d, 1)]
        else:
            self.got = list(self.first)

    def prepare_second(self):
        if self.staged:
            far_top, far_low = self.got[:2]
            self.second = [self.sent(0, 1, far_top), self.sent(1, 2, far_low)]
        else:
            self.second = []

    def send_second(self):
        if self.staged:
            self.last = [self.plan.swap_chip(self.second[0], 0), self.plan.swap_chip(self.second[1], 1)]
        else:
            self.last = []

    def finish(self):
        if self.staged:
            x_top, y_low = self.last
            x_low, y_top = self.got[2:]
            return total_sum(self.lefts, self.right, (x_top, y_top), (x_low, y_low), self.wide)
        else:
            parts = self.got
            for bit in reversed(range(self.plan.bits)):
                keep, give = parts[: 1 << bit], parts[1 << bit :]
                parts = [
                    k + self.plan.swap_chip(g.astype(BF16), bit).astype(F32)
                    for k, g in zip(keep, give)
                ]
            half = parts[0].shape[0] // 2
            total = jnp.concatenate(
                [self.by_place(parts[0][:half]), self.by_place(parts[0][half:])], axis=0
            )
        return total.astype(BF16)


def together(*groups):
    return lax.optimization_barrier(groups)


def split_columns(matrix):
    return matrix.T.reshape(2, matrix.shape[1] // 2, matrix.shape[0])


def split_rows(matrix):
    return matrix.reshape(2, matrix.shape[0] // 2, matrix.shape[1])


def body(
    inputs,
    seq_lengths,
    seq_assign,
    norm1_gain,
    w_query,
    w_key,
    w_value,
    w_forget,
    forget_bias,
    w_out,
    norm2_gain,
    w_gate,
    w_up,
    w_down,
    out_grad,
):
    plan = Plan(lax.axis_size("dp"), lax.axis_size("tensor"))
    core, place = plan.core, plan.place
    part_rows = inputs.shape[1]
    seq_rows = part_rows * 4
    half_rows = seq_rows // 2
    heads_shard = w_forget.shape[1] // 2
    heads_here = heads_shard * 4
    shard_cols = w_query.shape[1] // 2
    blocks = w_gate.shape[1] // 2 // UNIT_BLOCK

    def by_block(matrix):
        return split_columns(matrix).reshape(2, blocks, 1, UNIT_BLOCK, matrix.shape[0])

    forget_part = jnp.pad(
        split_columns(w_forget), ((0, 0), (0, FORGET_PAD - heads_shard), (0, 0))
    )
    line_one = plan.line_gather(
        jnp.concatenate(
            [split_columns(w_query), split_columns(w_key), split_columns(w_value), forget_part],
            axis=1,
        )
    )
    inputs, line_one = together(inputs, line_one)
    rows_one = line_one.shape[0] // 4

    def by_kind(piece):
        piece = piece.reshape(4, rows_one, -1)
        edges = [0, shard_cols, 2 * shard_cols, 3 * shard_cols, rows_one]
        parts = [piece[:, a:b].reshape(-1, piece.shape[-1]) for a, b in zip(edges, edges[1:])]
        return jnp.concatenate(parts, axis=0)

    full_one = plan.far_gather(plan.near_gather(line_one))
    rows_in = plan.to_chip(inputs)
    rows_in, full_one = together(rows_in, full_one)
    rows_in = rows_in.astype(F32)
    line_mid = plan.line_gather(
        jnp.concatenate([split_rows(w_out), split_rows(w_down)], axis=1)
    )
    line_mid, full_one = together(line_mid, full_one)
    line_mid = line_mid.reshape(4, -1, line_mid.shape[-1])
    near_out = plan.near_gather(line_mid[:, :shard_cols].reshape(4 * shard_cols, -1))
    near_down = plan.near_gather(line_mid[:, shard_cols:].reshape(-1, line_mid.shape[-1]))
    two_part = jnp.concatenate([by_block(w_gate), by_block(w_up)], axis=2)
    line_two = plan.line_gather(two_part.reshape(2, -1, two_part.shape[-1]))

    other_assign = plan.swap_core(seq_assign)
    assign_both = jnp.where(
        core == 0,
        jnp.concatenate([seq_assign, other_assign], axis=1),
        jnp.concatenate([other_assign, seq_assign], axis=1),
    ).reshape(4)
    seq_id = jnp.sum(jnp.where(jnp.arange(4) == place, assign_both, 0))
    length = jnp.sum(jnp.where(jnp.arange(seq_lengths.shape[0]) == seq_id, seq_lengths, 0))
    count = length.reshape(1)
    valid_here = (core * half_rows + jnp.arange(half_rows) < length).astype(F32)[:, None]

    gain_one = plan.by_chip(norm1_gain)
    gain_two = plan.by_chip(norm2_gain)
    bias_here = lax.dynamic_index_in_dim(
        forget_bias.reshape(4, 2, heads_shard), core, 1, keepdims=False
    ).reshape(-1)

    scale_one = row_scale(rows_in)
    normed_one = plan.both_rows((rows_in * scale_one * gain_one).astype(BF16))
    queries, key_rows, value_rows, logits = project(
        normed_one, full_one, shard_cols, heads_shard
    )
    forget_logit = logits + bias_here
    cumul_gate = jnp.cumsum(jax.nn.log_sigmoid(forget_logit), axis=0)
    gate_pairs = cumul_gate.reshape(seq_rows, heads_here // 2, 2).transpose(1, 0, 2)
    near_out, gate_pairs = together(near_out, gate_pairs)
    full_out, line_two, gate_pairs = together(plan.far_gather(near_out), line_two, gate_pairs)
    mixed_low, log_total = attn_fwd(count, queries, key_rows, value_rows, gate_pairs)
    mixed_low, near_down, full_one = together(mixed_low, near_down, full_one)
    kinds_one = [by_kind(piece) for piece in full_one]
    full_down = plan.far_gather(near_down)
    near_two, out_grad = together(plan.near_gather(line_two), out_grad)
    full_two = plan.far_gather(near_two)
    cotangent = plan.to_chip(out_grad).astype(F32)
    hidden_in = rows_in + plan.sum_rows(*combine(core, [mixed_low], full_out))

    scale_two = row_scale(hidden_in)
    normed_two = plan.both_rows((hidden_in * scale_two * gain_two).astype(BF16))
    normed_two, full_down, kinds_one = together(normed_two, full_down, kinds_one)
    gate_pre, up_pre, inner_low = inner_units(normed_two, full_two)
    grad_ffn = plan.both_rows((valid_here * cotangent).astype(BF16))
    down_sum = Reduction(plan, [inner_low], grad_ffn)
    down_sum.first, gate_pre = together(down_sum.first, gate_pre)
    down_sum.send_first()

    grad_pre = inner_grads(grad_ffn, gate_pre, up_pre, full_down)
    down_far, grad_pre = together(down_sum.got[:2], grad_pre)
    down_sum.got = [*down_far, *down_sum.got[2:]]
    two_sum = Reduction(plan, [grad_pre], normed_two)
    two_sum.first, down_sum.got, grad_pre, inner_low = together(
        two_sum.first, down_sum.got, grad_pre, inner_low
    )
    two_sum.send_first()
    down_sum.prepare_second()
    give_two, keep_two = combine(core, [grad_pre], full_two)
    give_ffn, keep_ffn = combine(core, [inner_low], full_down)
    down_sum.send_second()
    two_far, down_sum.last, give_two, give_ffn = together(
        two_sum.got[:2], down_sum.last, give_two, give_ffn
    )
    two_sum.got = [*two_far, *two_sum.got[2:]]
    grad_normed_two = plan.sum_rows(give_two, keep_two)
    gain_two_term = jnp.sum(grad_normed_two * hidden_in * scale_two, axis=0)
    grad_hidden = valid_here * cotangent + norm_back(
        hidden_in, scale_two, gain_two, grad_normed_two
    )

    grad_attn = plan.both_rows(grad_hidden.astype(BF16))
    out_sum = Reduction(plan, [mixed_low], grad_attn)
    two_sum.prepare_second()
    out_sum.first, two_sum.second, grad_attn = together(
        out_sum.first, two_sum.second, grad_attn
    )
    two_sum.send_second()
    out_sum.send_first()
    ffn_rows = plan.sum_rows(give_ffn, keep_ffn)
    outputs = (valid_here * (hidden_in + ffn_rows)).astype(BF16)
    grad_mixed = spread(count, grad_attn, full_out)
    query_low, key_low, value_low, grad_cumul = attn_bwd(
        count, queries, key_rows, value_rows, gate_pairs, log_total, mixed_low, grad_mixed
    )
    two_sum.got, two_sum.last, out_sum.got, query_low, key_low, value_low, grad_cumul = together(
        two_sum.got, two_sum.last, out_sum.got, query_low, key_low, value_low, grad_cumul
    )
    out_sum.prepare_second()
    out_sum.second, grad_cumul = together(out_sum.second, grad_cumul)
    out_sum.send_second()
    grad_logf = jnp.flip(jnp.cumsum(jnp.flip(grad_cumul, 0), axis=0), 0)
    grad_logit = grad_logf * jax.nn.sigmoid(-forget_logit)
    bias_term = jnp.sum(grad_logit, axis=0)
    logit_low = jnp.pad(
        grad_logit.astype(BF16).reshape(seq_rows, 4, heads_shard),
        ((0, 0), (0, 0), (0, FORGET_PAD - heads_shard)),
    ).reshape(seq_rows, -1)
    grad_one = [query_low, key_low, value_low, logit_low]
    one_sum = Reduction(plan, grad_one, normed_one)
    one_sum.first, out_sum.last = together(one_sum.first, out_sum.last)
    one_sum.send_first()
    one_sum.prepare_second()
    one_sum.second, grad_one, two_sum.last, outputs = together(
        one_sum.second, grad_one, two_sum.last, outputs
    )
    one_sum.send_second()
    outputs = plan.from_chip(outputs)
    down_pair = plan.scatter(down_sum.finish())
    two_total, down_pair = together(two_sum.finish(), down_pair)
    two_pair = plan.scatter(two_total)
    grad_normed_one = plan.sum_rows(*combine(core, grad_one, kinds_one))
    gain_one_term = jnp.sum(grad_normed_one * rows_in * scale_one, axis=0)
    input_grad = plan.from_chip(
        (grad_hidden + norm_back(rows_in, scale_one, gain_one, grad_normed_one)).astype(BF16)
    )

    bias_full = jnp.where(
        (jnp.arange(2) == core)[None, :, None], bias_term.reshape(4, 1, heads_shard), 0.0
    ).reshape(-1)
    wide = norm1_gain.shape[0]
    small = plan.sum_all(
        jnp.concatenate([plan.by_chip(gain_one_term), plan.by_chip(gain_two_term), bias_full])
    )

    out_total, two_pair = together(out_sum.finish(), two_pair)
    out_pair = plan.scatter(out_total)
    one_total, out_pair = together(one_sum.finish(), out_pair)
    one_pair = plan.scatter(one_total)
    down_shard, two_shard = plan.share(down_pair), plan.share(two_pair)
    out_shard, one_shard = plan.share(out_pair), plan.share(one_pair)

    two_shard = two_shard.reshape(2, blocks, 2, UNIT_BLOCK, -1)

    def columns(shard):
        return shard.reshape(-1, shard.shape[-1]).T

    def rows(shard):
        return shard.reshape(-1, shard.shape[-1])

    return (
        outputs,
        input_grad,
        small[:wide],
        columns(one_shard[:, :shard_cols]),
        columns(one_shard[:, shard_cols : 2 * shard_cols]),
        columns(one_shard[:, 2 * shard_cols : 3 * shard_cols]),
        columns(one_shard[:, 3 * shard_cols : 3 * shard_cols + heads_shard]),
        small[2 * wide :],
        rows(out_shard),
        small[wide : 2 * wide],
        columns(two_shard[:, :, 0]),
        columns(two_shard[:, :, 1]),
        rows(down_shard),
    )


def solution(mesh):
    return jax.shard_map(
        body,
        mesh=mesh,
        in_specs=(
            P(None, ("dp", "tensor"), None),
            P(),
            P(None, "dp"),
            P(),
            P("dp", "tensor"),
            P("dp", "tensor"),
            P("dp", "tensor"),
            P("dp", "tensor"),
            P(),
            P("tensor", "dp"),
            P(),
            P("dp", "tensor"),
            P("dp", "tensor"),
            P("tensor", "dp"),
            P(None, ("dp", "tensor"), None),
        ),
        out_specs=(
            P(None, ("dp", "tensor"), None),
            P(None, ("dp", "tensor"), None),
            P(),
            P("dp", "tensor"),
            P("dp", "tensor"),
            P("dp", "tensor"),
            P("dp", "tensor"),
            P(),
            P("tensor", "dp"),
            P(),
            P("dp", "tensor"),
            P("dp", "tensor"),
            P("tensor", "dp"),
        ),
        check_vma=False,
    )
```

```python
import functools

import jax
import jax.numpy as jnp
from jax import lax
from jax.experimental import pallas as pl
from jax.experimental.pallas import tpu as pltpu
from jax.sharding import PartitionSpec as P

EPS = 1e-06
NEG_BIG = -1e30
F32 = jnp.float32
BF16 = jnp.bfloat16
FORGET_PAD = 16
UNIT_BLOCK = 256
VMEM_BYTES = 60 << 20


def row_scale(tokens):
    return lax.rsqrt(jnp.mean(tokens * tokens, axis=-1, keepdims=True) + EPS)


def norm_back(tokens, scaling, gain, grad_out):
    weighted = grad_out * gain
    cubed = scaling * scaling * scaling
    return scaling * weighted - tokens * cubed * jnp.mean(weighted * tokens, axis=-1, keepdims=True)


def dot_first(left, right):
    return lax.dot_general(left, right, (((0,), (0,)), ((), ())), preferred_element_type=F32)

def nt(a, b):
    return lax.dot_general(a, b, (((1,), (1,)), ((), ())), preferred_element_type=F32)

def nn(a, b):
    return lax.dot_general(a, b, (((1,), (0,)), ((), ())), preferred_element_type=F32)

def pieces(x):
    top = x.astype(BF16).astype(F32)
    rest = x - top
    mid = rest.astype(BF16).astype(F32)
    return top, mid, rest - mid

def side(lane, base, values, rest):
    for n, value in enumerate(values):
        rest = jnp.where(lane == base + n, value, rest)
    return rest

def gate_column(c_ref, which, length, rows):
    col = c_ref[0, :, which : which + 1]
    pos = lax.broadcasted_iota(jnp.int32, (rows, 1), 0)
    return jnp.where(pos < length, -col, NEG_BIG)

def attn_fwd_kernel(len_ref, q_ref, k_ref, v_ref, c_ref, o_ref, l_ref, *, blk):
    rows, wide = q_ref.shape
    hd = wide // 2
    length = len_ref[0]
    lane = lax.broadcasted_iota(jnp.int32, (rows, wide), 1)
    lane_b = lax.broadcasted_iota(jnp.int32, (blk, wide), 1)
    q = q_ref[...].astype(F32) * 0.125
    k = k_ref[...].astype(F32)
    v = v_ref[...].astype(F32)
    heads = []
    for h in range(2):
        inside = (lane < hd) if h == 0 else (lane >= hd)
        base = hd if h == 0 else 0
        bias = jnp.broadcast_to(gate_column(c_ref, h, length, rows), (rows, wide))
        kx = jnp.where(inside, k, side(lane, base, pieces(bias), 0.0)).astype(BF16)
        qx = jnp.where(inside, q, side(lane, base, (1.0, 1.0, 1.0), 0.0)).astype(BF16)
        vx = jnp.where(inside, v, 1.0).astype(BF16)
        heads.append((qx, kx, vx))
    tri = lax.broadcasted_iota(jnp.int32, (blk, blk), 1) <= lax.broadcasted_iota(jnp.int32, (blk, blk), 0)
    for i in range(rows // blk):
        lo, hi = i * blk, (i + 1) * blk
        got = []
        for h in range(2):
            qx, kx, vx = heads[h]
            s_d = jnp.where(tri, nt(qx[lo:hi], kx[lo:hi]), NEG_BIG)
            m = jnp.max(s_d, axis=1, keepdims=True)
            if i:
                s_o = nt(qx[lo:hi], kx[:lo])
                m = jnp.maximum(m, jnp.max(s_o, axis=1, keepdims=True))
            r = nn(jnp.exp(s_d - m).astype(BF16), vx[lo:hi])
            if i:
                r = r + nn(jnp.exp(s_o - m).astype(BF16), vx[:lo])
            total = pltpu.roll(r, hd, 1)
            got.append((r / total, m + jnp.log(total)))
        pos = lo + lax.broadcasted_iota(jnp.int32, (blk, wide), 0)
        o = jnp.where(lane_b < hd, got[0][0], got[1][0])
        o_ref[lo:hi, :] = jnp.where(pos < length, o, 0.0).astype(BF16)
        l_ref[lo:hi, :] = jnp.where(lane_b < hd, got[0][1], got[1][1])

def attn_fwd(length, q, k, v, c, blk=256):
    rows, cols = q.shape
    pairs = cols // 128
    spec = pl.BlockSpec((rows, 128), lambda p: (0, p))
    return pl.pallas_call(
        functools.partial(attn_fwd_kernel, blk=blk),
        grid=(pairs,),
        in_specs=[pl.BlockSpec(memory_space=pltpu.SMEM), spec, spec, spec,
                  pl.BlockSpec((1, rows, 2), lambda p: (p, 0, 0))],
        out_specs=[spec, spec],
        out_shape=[jax.ShapeDtypeStruct((rows, cols), BF16), jax.ShapeDtypeStruct((rows, cols), F32)],
        compiler_params=pltpu.CompilerParams(vmem_limit_bytes=VMEM_BYTES),
        cost_estimate=pl.CostEstimate(flops=rows*rows*128*4*pairs*2, bytes_accessed=rows*cols*12, transcendentals=rows*rows*pairs),
    )(length, q, k, v, c)

def attn_bwd_kernel(len_ref, q_ref, k_ref, v_ref, c_ref, l_ref, o_ref, g_ref, dq_ref, dk_ref, dv_ref, dc_ref, acc_k, acc_v, *, blk):
    rows, wide = q_ref.shape
    hd = wide // 2
    length = len_ref[0]
    lane = lax.broadcasted_iota(jnp.int32, (rows, wide), 1)
    q = q_ref[...].astype(F32) * 0.125
    k = k_ref[...].astype(F32)
    v = v_ref[...].astype(F32)
    g = g_ref[...].astype(F32)
    go = g * o_ref[...].astype(F32)
    tri = lax.broadcasted_iota(jnp.int32, (blk, blk), 0) <= lax.broadcasted_iota(jnp.int32, (blk, blk), 1)
    res = []
    for h in range(2):
        inside = (lane < hd) if h == 0 else (lane >= hd)
        base = hd if h == 0 else 0
        bias = jnp.broadcast_to(gate_column(c_ref, h, length, rows), (rows, wide))
        logt = l_ref[...]
        logt = jnp.where(inside, pltpu.roll(logt, hd, 1), logt)
        other = pltpu.roll(l_ref[...], hd, 1)
        logt = jnp.where(inside, l_ref[...], other)
        dot_o = jnp.broadcast_to(jnp.sum(jnp.where(inside, go, 0.0), axis=1, keepdims=True), (rows, wide))
        kx = jnp.where(inside, k, side(lane, base, pieces(bias) + (1.0, 1.0, 1.0), 0.0)).astype(BF16)
        qx = jnp.where(inside, q, side(lane, base, (1.0, 1.0, 1.0) + pieces(-logt), 0.0)).astype(BF16)
        vx = jnp.where(inside, v, side(lane, base, (1.0, 1.0, 1.0), 0.0)).astype(BF16)
        gx = jnp.where(inside, g, side(lane, base, pieces(-dot_o), 0.0)).astype(BF16)
        kt = kx.T
        dq_parts = []
        for i in range(rows // blk):
            lo, hi = i * blk, (i + 1) * blk
            dqt = None
            for a, b, diag in ((lo, hi, True),) + (((0, lo, False),) if i else ()):
                s = nt(kx[a:b], qx[lo:hi])
                if diag:
                    s = jnp.where(tri, s, NEG_BIG)
                p = jnp.exp(s)
                ds = (p * nt(vx[a:b], gx[lo:hi])).astype(BF16)
                dv = nn(p.astype(BF16), g_ref[lo:hi, :])
                dk = nn(ds, qx[lo:hi])
                t = nn(kt[:, a:b], ds)
                dqt = t if dqt is None else dqt + t
                if diag:
                    acc_v[a:b, :] = dv
                    acc_k[a:b, :] = dk
                else:
                    acc_v[a:b, :] += dv
                    acc_k[a:b, :] += dk
            dq_parts.append(dqt.T)
        dq = jnp.concatenate(dq_parts, axis=0)
        dk = acc_k[...]
        res.append((dq, dk, acc_v[...], dq - pltpu.roll(dk, 3, 1)))
    first = lane < hd
    dq_ref[...] = jnp.where(first, res[0][0] * 0.125, res[1][0] * 0.125).astype(BF16)
    dk_ref[...] = jnp.where(first, res[0][1], res[1][1]).astype(BF16)
    dv_ref[...] = jnp.where(first, res[0][2], res[1][2]).astype(BF16)
    dc_ref[...] = jnp.where(first, res[1][3], res[0][3])

def attn_bwd(length, q, k, v, c, l, o, g, blk=256):
    rows, cols = q.shape
    pairs = cols // 128
    spec = pl.BlockSpec((rows, 128), lambda p: (0, p))
    low = jax.ShapeDtypeStruct((rows, cols), BF16)
    dq, dk, dv, dc = pl.pallas_call(
        functools.partial(attn_bwd_kernel, blk=blk),
        grid=(pairs,),
        in_specs=[pl.BlockSpec(memory_space=pltpu.SMEM), spec, spec, spec,
                  pl.BlockSpec((1, rows, 2), lambda p: (p, 0, 0)), spec, spec, spec],
        out_specs=[spec]*4,
        out_shape=[low, low, low, jax.ShapeDtypeStruct((rows, cols), F32)],
        scratch_shapes=[pltpu.VMEM((rows, 128), F32)]*2,
        compiler_params=pltpu.CompilerParams(vmem_limit_bytes=VMEM_BYTES),
        cost_estimate=pl.CostEstimate(flops=rows*rows*128*10*pairs*2, bytes_accessed=rows*cols*24, transcendentals=rows*rows*pairs),
    )(length, q, k, v, c, l, o, g)
    d3 = dc.reshape(rows, pairs, 128)
    grad_cumul = jnp.stack([d3[:, :, 67], d3[:, :, 3]], axis=2).reshape(rows, 2 * pairs)
    return dq, dk, dv, grad_cumul


def whole(array):
    return pl.BlockSpec(array.shape, lambda *_: (0,) * array.ndim, pipeline_mode=pl.Buffered(1))


def cost(flops, arrays, more=0):
    size = sum(a.size * a.dtype.itemsize for a in arrays)
    return pl.CostEstimate(flops=flops, bytes_accessed=size + more, transcendentals=0)


def joined(refs, lo=None, hi=None):
    if lo is None:
        return jnp.concatenate([r[...] for r in refs], axis=1)
    return jnp.concatenate([r[lo:hi, :] for r in refs], axis=1)


def project_kernel(x_ref, *refs, shard):
    w_refs, (q_ref, k_ref, v_ref, f_ref) = refs[:-4], refs[-4:]
    step = w_refs[0].shape[0] // 2
    x = x_ref[...]
    for kind, out in enumerate((q_ref, k_ref, v_ref)):
        rows = [joined(w_refs, t * step + kind * shard, t * step + (kind + 1) * shard) for t in range(2)]
        out[...] = nt(x, jnp.concatenate(rows, axis=0)).astype(BF16)
    rows = [joined(w_refs, t * step + 3 * shard, (t + 1) * step) for t in range(2)]
    f_ref[0] = nt(x, jnp.concatenate(rows, axis=0))


def project(x, weights, shard, few):
    rows = x.shape[0]
    step = weights[0].shape[0] // 2
    low = jax.ShapeDtypeStruct((rows, 4 * shard), BF16)
    spec = pl.BlockSpec((rows, 2 * shard), lambda i: (0, i))
    pad = step // 2 - 3 * shard
    q, k, v, f = pl.pallas_call(
        functools.partial(project_kernel, shard=shard),
        grid=(2,),
        in_specs=[whole(x)]
        + [pl.BlockSpec((step, w.shape[1]), lambda i: (i, 0)) for w in weights],
        out_specs=[spec, spec, spec, pl.BlockSpec((1, rows, 2 * pad), lambda i: (i, 0, 0))],
        out_shape=[low, low, low, jax.ShapeDtypeStruct((2, rows, 2 * pad), F32)],
        compiler_params=pltpu.CompilerParams(vmem_limit_bytes=VMEM_BYTES),
        cost_estimate=cost(2 * rows * x.shape[1] * 4 * step // 2, [x, *weights, low, low, low]),
        name="project",
    )(x, *weights)
    logits = f.reshape(2, rows, 2, pad)[..., :few].transpose(1, 0, 2, 3).reshape(rows, 4 * few)
    return q, k, v, logits


def combine_kernel(core_ref, *refs, lefts):
    left_refs, w_refs, (give_ref, keep_ref) = refs[:lefts], refs[lefts:-2], refs[-2:]
    step = pl.program_id(0)
    wide = w_refs[0].shape[1]
    for out, cond in ((give_ref, step < 2), (keep_ref, step >= 2)):

        @pl.when(cond)
        def _():
            for n, w in enumerate(w_refs):
                got, at = None, 0
                for left in left_refs:
                    deep = left.shape[1]
                    part = nn(left[...], w[at : at + deep, :])
                    got = part if got is None else got + part
                    at += deep
                out[:, n * wide : (n + 1) * wide] = got.astype(out.dtype)


def combine(core, lefts, weights):
    rows = lefts[0].shape[0]
    wide = weights[0].shape[1] * len(weights)
    block = rows // 4

    def place(i, core_ref):
        mine = core_ref[0]
        return (jnp.where(i < 2, (1 - mine) * 2 + i, mine * 2 + i - 2), 0)

    outs = [
        jax.ShapeDtypeStruct((rows // 2, wide), BF16),
        jax.ShapeDtypeStruct((rows // 2, wide), F32),
    ]
    return pl.pallas_call(
        functools.partial(combine_kernel, lefts=len(lefts)),
        grid_spec=pltpu.PrefetchScalarGridSpec(
            num_scalar_prefetch=1,
            grid=(4,),
            in_specs=[pl.BlockSpec((block, left.shape[1]), place) for left in lefts]
            + [whole(w) for w in weights],
            out_specs=[
                pl.BlockSpec((block, wide), lambda i, c: (jnp.minimum(i, 1), 0)),
                pl.BlockSpec((block, wide), lambda i, c: (jnp.maximum(i - 2, 0), 0)),
            ],
        ),
        out_shape=outs,
        compiler_params=pltpu.CompilerParams(vmem_limit_bytes=VMEM_BYTES),
        cost_estimate=cost(
            2 * rows * weights[0].shape[0] * wide, [*lefts, *weights, *outs]
        ),
        name="combine",
    )(core.reshape(1), *lefts, *weights)


def spread_kernel(len_ref, x_ref, *refs):
    w_refs, out_ref = refs[:-1], refs[-1]
    rows = x_ref.shape[0]
    got = nt(x_ref[...], joined(w_refs))
    pos = pl.program_id(0) * rows + lax.broadcasted_iota(jnp.int32, got.shape, 0)
    out_ref[...] = jnp.where(pos < len_ref[0], got, 0.0).astype(BF16)


def spread(length, x, weights):
    rows, wide = x.shape[0], weights[0].shape[0]
    block = rows // 4
    out = jax.ShapeDtypeStruct((rows, wide), BF16)
    return pl.pallas_call(
        spread_kernel,
        grid=(4,),
        in_specs=[
            pl.BlockSpec(memory_space=pltpu.SMEM),
            pl.BlockSpec((block, x.shape[1]), lambda i: (i, 0)),
        ]
        + [whole(w) for w in weights],
        out_specs=pl.BlockSpec((block, wide), lambda i: (i, 0)),
        out_shape=out,
        compiler_params=pltpu.CompilerParams(vmem_limit_bytes=VMEM_BYTES),
        cost_estimate=cost(2 * rows * x.shape[1] * wide, [x, *weights, out]),
        name="spread",
    )(length, x, *weights)


def inner_kernel(x_ref, *refs):
    w_refs, (gate_ref, up_ref, inner_ref) = refs[:-3], refs[-3:]
    both = nt(x_ref[...], joined(w_refs))
    gate, up = both[:, :UNIT_BLOCK], both[:, UNIT_BLOCK:]
    gate_ref[...] = gate
    up_ref[...] = up
    inner_ref[...] = (gate * jax.nn.sigmoid(gate) * up).astype(BF16)


def inner_units(x, weights):
    rows = x.shape[0]
    total = weights[0].shape[0] // 2
    spec = pl.BlockSpec((rows, UNIT_BLOCK), lambda i: (0, i))
    outs = [jax.ShapeDtypeStruct((rows, total), t) for t in (F32, F32, BF16)]
    return pl.pallas_call(
        inner_kernel,
        grid=(total // UNIT_BLOCK,),
        in_specs=[whole(x)]
        + [pl.BlockSpec((2 * UNIT_BLOCK, w.shape[1]), lambda i: (i, 0)) for w in weights],
        out_specs=[spec] * 3,
        out_shape=outs,
        compiler_params=pltpu.CompilerParams(vmem_limit_bytes=VMEM_BYTES),
        cost_estimate=cost(4 * rows * x.shape[1] * total, [x, *weights, *outs]),
        name="inner_units",
    )(x, *weights)


def inner_grads_kernel(x_ref, gate_ref, up_ref, *refs):
    down_refs, pre_ref = refs[:-1], refs[-1]
    grad = nt(x_ref[...], joined(down_refs))
    gate, up = gate_ref[...], up_ref[...]
    sig = jax.nn.sigmoid(gate)
    pre_ref[:, :UNIT_BLOCK] = (grad * up * (sig * (1.0 + gate * (1.0 - sig)))).astype(BF16)
    pre_ref[:, UNIT_BLOCK:] = (grad * (gate * sig)).astype(BF16)


def inner_grads(x, gate, up, down):
    rows, cols = x.shape
    total = gate.shape[1]
    spec = pl.BlockSpec((rows, UNIT_BLOCK), lambda i: (0, i))
    out = jax.ShapeDtypeStruct((rows, 2 * total), BF16)
    return pl.pallas_call(
        inner_grads_kernel,
        grid=(total // UNIT_BLOCK,),
        in_specs=[whole(x), spec, spec]
        + [pl.BlockSpec((UNIT_BLOCK, w.shape[1]), lambda i: (i, 0)) for w in down],
        out_specs=pl.BlockSpec((rows, 2 * UNIT_BLOCK), lambda i: (0, i)),
        out_shape=out,
        compiler_params=pltpu.CompilerParams(vmem_limit_bytes=VMEM_BYTES),
        cost_estimate=cost(2 * rows * cols * total, [x, gate, up, *down, out]),
        name="inner_grads",
    )(x, gate, up, *down)


def half_products(left_refs, right, side):
    parts = []
    for ref, narrow in left_refs:
        got = dot_first(ref[...], right)
        if narrow:
            few = got.shape[0] // 2
            got = jnp.where(side == 0, got[:few], got[few:])
        parts.append(got)
    return parts


def term_kernel(*refs, narrow, side):
    count = len(narrow)
    right_ref, add_refs, out_ref = refs[count], refs[count + 1 : -1], refs[-1]
    at = 0
    for part in half_products(list(zip(refs[:count], narrow)), right_ref[...], side):
        rows = slice(at, at + part.shape[0])
        for add in add_refs:
            part = part + add[rows, :].astype(F32)
        out_ref[rows, :] = part.astype(BF16)
        at += part.shape[0]


def left_specs(lefts, steps, block):
    specs, narrow = [], []
    for left in lefts:
        rows, cols = left.shape
        wide = cols // (2 * steps)
        narrow.append(wide % 128 != 0)
        if wide % 128:
            specs.append(pl.BlockSpec((rows, cols), lambda i: (0, 0)))
        else:
            specs.append(pl.BlockSpec((rows, wide), lambda i: (0, block(i))))
    return specs, tuple(narrow)


def chunks_of(lefts):
    half = lefts[0].shape[1] // 2
    return max(1, half // 512) if len(lefts) == 1 else 1


def term_sum(lefts, right, side, r, wide, adds=()):
    steps = chunks_of(lefts)
    half = sum(left.shape[1] for left in lefts) // 2
    specs, narrow = left_specs(lefts, steps, lambda i: side * steps + i)
    part = pl.BlockSpec((half // steps, wide), lambda i: (i, 0))
    out = jax.ShapeDtypeStruct((half, wide), BF16)
    return pl.pallas_call(
        functools.partial(term_kernel, narrow=narrow, side=side),
        grid=(steps,),
        in_specs=specs
        + [pl.BlockSpec((right.shape[0], wide), lambda i: (0, r))]
        + [part] * len(adds),
        out_specs=part,
        out_shape=out,
        compiler_params=pltpu.CompilerParams(vmem_limit_bytes=VMEM_BYTES),
        cost_estimate=cost(2 * right.shape[0] * half * wide, [*adds, out, out]),
        name="term_sum",
    )(*lefts, right, *adds)


def total_kernel(*refs, narrow, steps):
    count = len(narrow)
    right_ref, tops, lows, out_ref = refs[count], refs[count + 1 : -3], refs[-3:-1], refs[-1]
    step = pl.program_id(0)
    side = step // steps
    parts = half_products(list(zip(refs[:count], narrow)), right_ref[...], side)
    if count == 1:
        places = [parts]
    else:
        places = [
            [part[n * (part.shape[0] // 2) : (n + 1) * (part.shape[0] // 2)] for part in parts]
            for n in range(2)
        ]
    for this, adds in ((0, tops), (1, lows)):

        @pl.when(side == this)
        def _():
            at = 0
            for n, place in enumerate(places):
                off = 0
                for part, whole_part in zip(place, parts):
                    few = part.shape[0]
                    start = off + n * few if count > 1 else 0
                    got = part
                    for add in adds:
                        got = got + add[start : start + few, :].astype(F32)
                    out_ref[at : at + few, :] = got.astype(BF16)
                    at += few
                    off += whole_part.shape[0]


def total_sum(lefts, right, tops, lows, wide):
    steps = chunks_of(lefts)
    full = sum(left.shape[1] for left in lefts)
    block = full // (2 * steps)
    specs, narrow = left_specs(lefts, steps, lambda i: i)
    out = jax.ShapeDtypeStruct((full, wide), BF16)
    return pl.pallas_call(
        functools.partial(total_kernel, narrow=narrow, steps=steps),
        grid=(2 * steps,),
        in_specs=specs
        + [pl.BlockSpec((right.shape[0], wide), lambda i: (0, 0))]
        + [pl.BlockSpec((block, wide), lambda i: (jnp.minimum(i, steps - 1), 0))] * 2
        + [pl.BlockSpec((block, wide), lambda i: (jnp.maximum(i - steps, 0), 0))] * 2,
        out_specs=pl.BlockSpec((block, wide), lambda i: (i, 0)),
        out_shape=out,
        compiler_params=pltpu.CompilerParams(vmem_limit_bytes=VMEM_BYTES),
        cost_estimate=cost(2 * right.shape[0] * full * wide, [out, out, out]),
        name="total_sum",
    )(*lefts, right, *tops, *lows)


class Plan:
    def __init__(self, ways_dp, ways_tensor):
        self.ways_dp = ways_dp
        self.ways_tensor = ways_tensor
        self.chips = ways_dp // 2
        self.bits = self.chips.bit_length() - 1
        assert self.chips == 1 << self.bits and ways_tensor == 4
        dp = lax.axis_index("dp")
        self.chip = dp // 2
        self.core = dp % 2
        self.place = lax.axis_index("tensor")
        self.core_perm = [(i, i ^ 1) for i in range(ways_dp)]

    def swap_core(self, array):
        return lax.ppermute(array, "dp", self.core_perm)

    def swap_chip(self, array, bit):
        perm = [(i, i ^ (2 << bit)) for i in range(self.ways_dp)]
        return lax.ppermute(array, "dp", perm)

    def route(self, turn):
        pairs = []
        for chip in range(self.chips):
            for core in range(2):
                for z in range(4):
                    micro = (z + turn) % 2
                    source = (2 * chip + core) * 4 + z
                    target = (2 * chip + z // 2) * 4 + 2 * micro + core
                    pairs.append((source, target))
        return pairs

    def by_chip(self, array):
        lead = array.shape[:-1]
        wide = array.shape[-1] // self.chips
        parts = [
            lax.dynamic_slice_in_dim(array, (self.chip ^ r) * wide, wide, axis=-1)
            for r in range(self.chips)
        ]
        return jnp.concatenate(parts, axis=-1).reshape(*lead, -1)

    def to_chip(self, array):
        got = []
        for turn in range(2):
            micro = (self.place + turn) % 2
            part = lax.dynamic_index_in_dim(array, micro, 0, keepdims=False)
            got.append(lax.ppermute(self.by_chip(part), ("dp", "tensor"), self.route(turn)))
        first = self.place // 2 == 0
        return jnp.concatenate(
            [jnp.where(first, got[0], got[1]), jnp.where(first, got[1], got[0])], axis=0
        )

    def from_chip(self, array):
        rows = array.shape[0] // 2
        got = []
        for turn in range(2):
            block = (self.place // 2 + turn) % 2
            part = lax.dynamic_slice_in_dim(array, block * rows, rows, axis=0)
            back = [(b, a) for a, b in self.route(turn)]
            got.append(lax.ppermute(self.by_chip(part), ("dp", "tensor"), back))
        first = self.place % 2 == 0
        return jnp.stack([jnp.where(first, got[0], got[1]), jnp.where(first, got[1], got[0])])

    def both_rows(self, half):
        other = self.swap_core(half)
        first = self.core == 0
        return jnp.concatenate(
            [jnp.where(first, half, other), jnp.where(first, other, half)], axis=0
        )

    def sum_rows(self, give, keep):
        return keep + self.swap_core(give).astype(F32)

    def line_gather(self, shard):
        mine = lax.dynamic_index_in_dim(shard, self.core, 0, keepdims=False)
        theirs = lax.dynamic_index_in_dim(shard, 1 - self.core, 0, keepdims=False)
        other = self.swap_core(theirs)
        first = self.core == 0
        pair = jnp.concatenate(
            [jnp.where(first, mine, other), jnp.where(first, other, mine)], axis=1
        )
        return lax.all_gather(pair, "tensor", axis=0, tiled=True)

    def near_gather(self, own):
        if self.bits == 2:
            return [own, self.swap_chip(own, 0), self.swap_chip(own, 1)]
        parts = [own]
        for bit in range(self.bits):
            parts = parts + [self.swap_chip(p, bit) for p in parts]
        return [jnp.concatenate(parts, axis=1)]

    def far_gather(self, near):
        if self.bits != 2:
            return near
        own, by_x, by_y = near
        half = own.shape[0] // 2
        far_top = self.swap_chip(by_x[:half], 1)
        far_low = self.swap_chip(by_y[half:], 0)
        return [own, by_x, by_y, jnp.concatenate([far_top, far_low], axis=0)]

    def scatter(self, total):
        return lax.psum_scatter(total, "tensor", scatter_dimension=0, tiled=True)

    def share(self, pair):
        narrow = pair.shape[1] // 2
        mine = lax.dynamic_slice_in_dim(pair, self.core * narrow, narrow, axis=1)
        theirs = lax.dynamic_slice_in_dim(pair, (1 - self.core) * narrow, narrow, axis=1)
        other = self.swap_core(theirs)
        first = self.core == 0
        return jnp.stack([jnp.where(first, mine, other), jnp.where(first, other, mine)]).astype(F32)

    def sum_all(self, vector):
        vector = vector + self.swap_core(vector)
        for bit in range(self.bits):
            vector = vector + self.swap_chip(vector, bit)
        for bit in range(2):
            perm = [(z, z ^ (1 << bit)) for z in range(4)]
            vector = vector + lax.ppermute(vector, "tensor", perm)
        return vector


class Reduction:
    def __init__(self, plan, lefts, right):
        self.plan, self.lefts, self.right = plan, lefts, right
        self.wide = right.shape[1] // plan.chips
        self.staged = plan.bits == 2
        if self.staged:
            if len(lefts) == 1:
                self.first = [
                    self.top(3).astype(BF16),
                    self.low(3).astype(BF16),
                    self.low(1).astype(BF16),
                    self.top(2).astype(BF16),
                ]
            else:
                self.first = [self.sent(0, 3), self.sent(1, 3), self.sent(1, 1), self.sent(0, 2)]
        else:
            self.first = [
                jnp.concatenate([self.top(r), self.low(r)], axis=0) for r in range(plan.chips)
            ]

    def term(self, r, side):
        right = self.right[:, r * self.wide : (r + 1) * self.wide]
        parts = []
        for left in self.lefts:
            half = left.shape[1] // 2
            parts.append(dot_first(left[:, side * half : (side + 1) * half], right))
        return parts[0] if len(parts) == 1 else jnp.concatenate(parts, axis=0)

    def sent(self, side, r, *adds):
        return term_sum(self.lefts, self.right, side, r, self.wide, adds)

    def top(self, r):
        return self.term(r, 0)

    def low(self, r):
        return self.term(r, 1)

    def by_place(self, half):
        if len(self.lefts) == 1:
            return half
        parts, at = [], 0
        for left in self.lefts:
            parts.append((at, left.shape[1] // 4))
            at += left.shape[1] // 2
        return jnp.concatenate(
            [half[at + n * few : at + (n + 1) * few] for n in range(2) for at, few in parts], axis=0
        )

    def send_first(self):
        if self.staged:
            a, b, c, d = self.first
            swap = self.plan.swap_chip
            self.got = [swap(a, 1), swap(b, 0), swap(c, 0), swap(d, 1)]
        else:
            self.got = list(self.first)

    def prepare_second(self):
        if self.staged:
            far_top, far_low = self.got[:2]
            self.second = [self.sent(0, 1, far_top), self.sent(1, 2, far_low)]
        else:
            self.second = []

    def send_second(self):
        if self.staged:
            self.last = [self.plan.swap_chip(self.second[0], 0), self.plan.swap_chip(self.second[1], 1)]
        else:
            self.last = []

    def finish(self):
        if self.staged:
            x_top, y_low = self.last
            x_low, y_top = self.got[2:]
            return total_sum(self.lefts, self.right, (x_top, y_top), (x_low, y_low), self.wide)
        else:
            parts = self.got
            for bit in reversed(range(self.plan.bits)):
                keep, give = parts[: 1 << bit], parts[1 << bit :]
                parts = [
                    k + self.plan.swap_chip(g.astype(BF16), bit).astype(F32)
                    for k, g in zip(keep, give)
                ]
            half = parts[0].shape[0] // 2
            total = jnp.concatenate(
                [self.by_place(parts[0][:half]), self.by_place(parts[0][half:])], axis=0
            )
        return total.astype(BF16)


class Direct:
    def __init__(self, plan, lefts, right):
        self.plan, self.left, self.right = plan, lefts[0], right
        self.wide = right.shape[1] // plan.chips
        self.first = [self.term(r).astype(BF16) for r in range(1, plan.chips)]

    def term(self, r):
        return dot_first(self.left, self.right[:, r * self.wide : (r + 1) * self.wide])

    def send_first(self):
        ways = range(self.plan.ways_dp)
        self.got = [
            lax.ppermute(part, "dp", [(i, i ^ (2 * (n + 1))) for i in ways])
            for n, part in enumerate(self.first)
        ]

    def prepare_second(self):
        self.second = []

    def send_second(self):
        self.last = []

    def finish(self):
        total = self.term(0)
        for part in self.got:
            total = total + part.astype(F32)
        return total.astype(BF16)


def together(*groups):
    return lax.optimization_barrier(groups)


def split_columns(matrix):
    return matrix.T.reshape(2, matrix.shape[1] // 2, matrix.shape[0])


def split_rows(matrix):
    return matrix.reshape(2, matrix.shape[0] // 2, matrix.shape[1])


def body(
    inputs,
    seq_lengths,
    seq_assign,
    norm1_gain,
    w_query,
    w_key,
    w_value,
    w_forget,
    forget_bias,
    w_out,
    norm2_gain,
    w_gate,
    w_up,
    w_down,
    out_grad,
):
    plan = Plan(lax.axis_size("dp"), lax.axis_size("tensor"))
    core, place = plan.core, plan.place
    part_rows = inputs.shape[1]
    seq_rows = part_rows * 4
    half_rows = seq_rows // 2
    heads_shard = w_forget.shape[1] // 2
    heads_here = heads_shard * 4
    shard_cols = w_query.shape[1] // 2
    blocks = w_gate.shape[1] // 2 // UNIT_BLOCK

    def by_block(matrix):
        return split_columns(matrix).reshape(2, blocks, 1, UNIT_BLOCK, matrix.shape[0])

    forget_part = jnp.pad(
        split_columns(w_forget), ((0, 0), (0, FORGET_PAD - heads_shard), (0, 0))
    )
    line_one = plan.line_gather(
        jnp.concatenate(
            [split_columns(w_query), split_columns(w_key), split_columns(w_value), forget_part],
            axis=1,
        )
    )
    inputs, line_one = together(inputs, line_one)
    rows_one = line_one.shape[0] // 4

    def by_kind(piece):
        piece = piece.reshape(4, rows_one, -1)
        edges = [0, shard_cols, 2 * shard_cols, 3 * shard_cols, rows_one]
        parts = [piece[:, a:b].reshape(-1, piece.shape[-1]) for a, b in zip(edges, edges[1:])]
        return jnp.concatenate(parts, axis=0)

    full_one = plan.far_gather(plan.near_gather(line_one))
    rows_in = plan.to_chip(inputs)
    rows_in, full_one = together(rows_in, full_one)
    rows_in = rows_in.astype(F32)
    line_mid = plan.line_gather(
        jnp.concatenate([split_rows(w_out), split_rows(w_down)], axis=1)
    )
    line_mid, full_one = together(line_mid, full_one)
    line_mid = line_mid.reshape(4, -1, line_mid.shape[-1])
    near_out = plan.near_gather(line_mid[:, :shard_cols].reshape(4 * shard_cols, -1))
    near_down = plan.near_gather(line_mid[:, shard_cols:].reshape(-1, line_mid.shape[-1]))
    two_part = jnp.concatenate([by_block(w_gate), by_block(w_up)], axis=2)
    line_two = plan.line_gather(two_part.reshape(2, -1, two_part.shape[-1]))

    other_assign = plan.swap_core(seq_assign)
    assign_both = jnp.where(
        core == 0,
        jnp.concatenate([seq_assign, other_assign], axis=1),
        jnp.concatenate([other_assign, seq_assign], axis=1),
    ).reshape(4)
    seq_id = jnp.sum(jnp.where(jnp.arange(4) == place, assign_both, 0))
    length = jnp.sum(jnp.where(jnp.arange(seq_lengths.shape[0]) == seq_id, seq_lengths, 0))
    count = length.reshape(1)
    valid_here = (core * half_rows + jnp.arange(half_rows) < length).astype(F32)[:, None]

    gain_one = plan.by_chip(norm1_gain)
    gain_two = plan.by_chip(norm2_gain)
    bias_here = lax.dynamic_index_in_dim(
        forget_bias.reshape(4, 2, heads_shard), core, 1, keepdims=False
    ).reshape(-1)

    scale_one = row_scale(rows_in)
    normed_one = plan.both_rows((rows_in * scale_one * gain_one).astype(BF16))
    queries, key_rows, value_rows, logits = project(
        normed_one, full_one, shard_cols, heads_shard
    )
    forget_logit = logits + bias_here
    cumul_gate = jnp.cumsum(jax.nn.log_sigmoid(forget_logit), axis=0)
    gate_pairs = cumul_gate.reshape(seq_rows, heads_here // 2, 2).transpose(1, 0, 2)
    near_out, gate_pairs = together(near_out, gate_pairs)
    full_out, line_two, gate_pairs = together(plan.far_gather(near_out), line_two, gate_pairs)
    mixed_low, log_total = attn_fwd(count, queries, key_rows, value_rows, gate_pairs)
    mixed_low, near_down, full_one = together(mixed_low, near_down, full_one)
    kinds_one = [by_kind(piece) for piece in full_one]
    full_down = plan.far_gather(near_down)
    near_two, out_grad = together(plan.near_gather(line_two), out_grad)
    full_two = plan.far_gather(near_two)
    cotangent = plan.to_chip(out_grad).astype(F32)
    hidden_in = rows_in + plan.sum_rows(*combine(core, [mixed_low], full_out))

    scale_two = row_scale(hidden_in)
    normed_two = plan.both_rows((hidden_in * scale_two * gain_two).astype(BF16))
    normed_two, full_down, kinds_one = together(normed_two, full_down, kinds_one)
    gate_pre, up_pre, inner_low = inner_units(normed_two, full_two)
    grad_ffn = plan.both_rows((valid_here * cotangent).astype(BF16))
    down_sum = Reduction(plan, [inner_low], grad_ffn)
    down_sum.first, gate_pre = together(down_sum.first, gate_pre)
    down_sum.send_first()

    grad_pre = inner_grads(grad_ffn, gate_pre, up_pre, full_down)
    down_far, grad_pre = together(down_sum.got[:2], grad_pre)
    down_sum.got = [*down_far, *down_sum.got[2:]]
    two_sum = Reduction(plan, [grad_pre], normed_two)
    two_sum.first, down_sum.got, grad_pre, inner_low = together(
        two_sum.first, down_sum.got, grad_pre, inner_low
    )
    two_sum.send_first()
    down_sum.prepare_second()
    give_two, keep_two = combine(core, [grad_pre], full_two)
    give_ffn, keep_ffn = combine(core, [inner_low], full_down)
    down_sum.send_second()
    two_far, down_sum.last, give_two, give_ffn = together(
        two_sum.got[:2], down_sum.last, give_two, give_ffn
    )
    two_sum.got = [*two_far, *two_sum.got[2:]]
    grad_normed_two = plan.sum_rows(give_two, keep_two)
    gain_two_term = jnp.sum(grad_normed_two * hidden_in * scale_two, axis=0)
    grad_hidden = valid_here * cotangent + norm_back(
        hidden_in, scale_two, gain_two, grad_normed_two
    )

    grad_attn = plan.both_rows(grad_hidden.astype(BF16))
    out_sum = (Direct if plan.bits == 2 else Reduction)(plan, [mixed_low], grad_attn)
    two_sum.prepare_second()
    out_sum.first, two_sum.second, grad_attn = together(
        out_sum.first, two_sum.second, grad_attn
    )
    two_sum.send_second()
    out_sum.send_first()
    ffn_rows = plan.sum_rows(give_ffn, keep_ffn)
    outputs = (valid_here * (hidden_in + ffn_rows)).astype(BF16)
    grad_mixed = spread(count, grad_attn, full_out)
    query_low, key_low, value_low, grad_cumul = attn_bwd(
        count, queries, key_rows, value_rows, gate_pairs, log_total, mixed_low, grad_mixed
    )
    two_sum.got, two_sum.last, out_sum.got, query_low, key_low, value_low, grad_cumul = together(
        two_sum.got, two_sum.last, out_sum.got, query_low, key_low, value_low, grad_cumul
    )
    out_sum.prepare_second()
    out_sum.second, grad_cumul = together(out_sum.second, grad_cumul)
    out_sum.send_second()
    grad_logf = jnp.flip(jnp.cumsum(jnp.flip(grad_cumul, 0), axis=0), 0)
    grad_logit = grad_logf * jax.nn.sigmoid(-forget_logit)
    bias_term = jnp.sum(grad_logit, axis=0)
    logit_low = jnp.pad(
        grad_logit.astype(BF16).reshape(seq_rows, 4, heads_shard),
        ((0, 0), (0, 0), (0, FORGET_PAD - heads_shard)),
    ).reshape(seq_rows, -1)
    grad_one = [query_low, key_low, value_low, logit_low]
    one_sum = Reduction(plan, grad_one, normed_one)
    one_sum.first, out_sum.last, two_sum.last, outputs = together(
        one_sum.first, out_sum.last, two_sum.last, outputs
    )
    one_sum.send_first()
    outputs = plan.from_chip(outputs)
    one_sum.prepare_second()
    one_sum.second, grad_one = together(one_sum.second, grad_one)
    one_sum.send_second()
    down_pair = plan.scatter(down_sum.finish())
    two_total, down_pair = together(two_sum.finish(), down_pair)
    two_pair = plan.scatter(two_total)
    grad_normed_one = plan.sum_rows(*combine(core, grad_one, kinds_one))
    gain_one_term = jnp.sum(grad_normed_one * rows_in * scale_one, axis=0)
    input_grad = plan.from_chip(
        (grad_hidden + norm_back(rows_in, scale_one, gain_one, grad_normed_one)).astype(BF16)
    )

    bias_full = jnp.where(
        (jnp.arange(2) == core)[None, :, None], bias_term.reshape(4, 1, heads_shard), 0.0
    ).reshape(-1)
    wide = norm1_gain.shape[0]
    small = plan.sum_all(
        jnp.concatenate([plan.by_chip(gain_one_term), plan.by_chip(gain_two_term), bias_full])
    )

    out_total, two_pair = together(out_sum.finish(), two_pair)
    out_pair = plan.scatter(out_total)
    one_total, out_pair = together(one_sum.finish(), out_pair)
    one_pair = plan.scatter(one_total)
    down_shard, two_shard = plan.share(down_pair), plan.share(two_pair)
    out_shard, one_shard = plan.share(out_pair), plan.share(one_pair)

    two_shard = two_shard.reshape(2, blocks, 2, UNIT_BLOCK, -1)

    def columns(shard):
        return shard.reshape(-1, shard.shape[-1]).T

    def rows(shard):
        return shard.reshape(-1, shard.shape[-1])

    return (
        outputs,
        input_grad,
        small[:wide],
        columns(one_shard[:, :shard_cols]),
        columns(one_shard[:, shard_cols : 2 * shard_cols]),
        columns(one_shard[:, 2 * shard_cols : 3 * shard_cols]),
        columns(one_shard[:, 3 * shard_cols : 3 * shard_cols + heads_shard]),
        small[2 * wide :],
        rows(out_shard),
        small[wide : 2 * wide],
        columns(two_shard[:, :, 0]),
        columns(two_shard[:, :, 1]),
        rows(down_shard),
    )


def solution(mesh):
    return jax.shard_map(
        body,
        mesh=mesh,
        in_specs=(
            P(None, ("dp", "tensor"), None),
            P(),
            P(None, "dp"),
            P(),
            P("dp", "tensor"),
            P("dp", "tensor"),
            P("dp", "tensor"),
            P("dp", "tensor"),
            P(),
            P("tensor", "dp"),
            P(),
            P("dp", "tensor"),
            P("dp", "tensor"),
            P("tensor", "dp"),
            P(None, ("dp", "tensor"), None),
        ),
        out_specs=(
            P(None, ("dp", "tensor"), None),
            P(None, ("dp", "tensor"), None),
            P(),
            P("dp", "tensor"),
            P("dp", "tensor"),
            P("dp", "tensor"),
            P("dp", "tensor"),
            P(),
            P("tensor", "dp"),
            P(),
            P("dp", "tensor"),
            P("dp", "tensor"),
            P("tensor", "dp"),
        ),
        check_vma=False,
    )
```

```python
import functools

import jax
import jax.numpy as jnp
from jax import lax
from jax.experimental import pallas as pl
from jax.experimental.pallas import tpu as pltpu
from jax.sharding import PartitionSpec as P

EPS = 1e-06
NEG_BIG = -1e30
F32 = jnp.float32
BF16 = jnp.bfloat16
FORGET_PAD = 16
UNIT_BLOCK = 256
VMEM_BYTES = 60 << 20


def row_scale(tokens):
    return lax.rsqrt(jnp.mean(tokens * tokens, axis=-1, keepdims=True) + EPS)


def norm_back(tokens, scaling, gain, grad_out):
    weighted = grad_out * gain
    cubed = scaling * scaling * scaling
    return scaling * weighted - tokens * cubed * jnp.mean(weighted * tokens, axis=-1, keepdims=True)


def dot_first(left, right):
    return lax.dot_general(left, right, (((0,), (0,)), ((), ())), preferred_element_type=F32)

def nt(a, b):
    return lax.dot_general(a, b, (((1,), (1,)), ((), ())), preferred_element_type=F32)

def nn(a, b):
    return lax.dot_general(a, b, (((1,), (0,)), ((), ())), preferred_element_type=F32)

def pieces(x):
    top = x.astype(BF16).astype(F32)
    rest = x - top
    mid = rest.astype(BF16).astype(F32)
    return top, mid, rest - mid

def side(lane, base, values, rest):
    for n, value in enumerate(values):
        rest = jnp.where(lane == base + n, value, rest)
    return rest

def gate_column(c_ref, which, length, rows):
    col = c_ref[0, :, which : which + 1]
    pos = lax.broadcasted_iota(jnp.int32, (rows, 1), 0)
    return jnp.where(pos < length, -col, NEG_BIG)

def attn_fwd_kernel(len_ref, q_ref, k_ref, v_ref, c_ref, o_ref, l_ref, *, blk):
    rows, wide = q_ref.shape
    hd = wide // 2
    length = len_ref[0]
    lane = lax.broadcasted_iota(jnp.int32, (rows, wide), 1)
    lane_b = lax.broadcasted_iota(jnp.int32, (blk, wide), 1)
    q = q_ref[...].astype(F32) * 0.125
    k = k_ref[...].astype(F32)
    v = v_ref[...].astype(F32)
    heads = []
    for h in range(2):
        inside = (lane < hd) if h == 0 else (lane >= hd)
        base = hd if h == 0 else 0
        bias = jnp.broadcast_to(gate_column(c_ref, h, length, rows), (rows, wide))
        kx = jnp.where(inside, k, side(lane, base, pieces(bias), 0.0)).astype(BF16)
        qx = jnp.where(inside, q, side(lane, base, (1.0, 1.0, 1.0), 0.0)).astype(BF16)
        vx = jnp.where(inside, v, 1.0).astype(BF16)
        heads.append((qx, kx, vx))
    tri = lax.broadcasted_iota(jnp.int32, (blk, blk), 1) <= lax.broadcasted_iota(jnp.int32, (blk, blk), 0)
    for i in range(rows // blk):
        lo, hi = i * blk, (i + 1) * blk
        got = []
        for h in range(2):
            qx, kx, vx = heads[h]
            s_d = jnp.where(tri, nt(qx[lo:hi], kx[lo:hi]), NEG_BIG)
            m = jnp.max(s_d, axis=1, keepdims=True)
            if i:
                s_o = nt(qx[lo:hi], kx[:lo])
                m = jnp.maximum(m, jnp.max(s_o, axis=1, keepdims=True))
            r = nn(jnp.exp(s_d - m).astype(BF16), vx[lo:hi])
            if i:
                r = r + nn(jnp.exp(s_o - m).astype(BF16), vx[:lo])
            total = pltpu.roll(r, hd, 1)
            got.append((r / total, m + jnp.log(total)))
        pos = lo + lax.broadcasted_iota(jnp.int32, (blk, wide), 0)
        o = jnp.where(lane_b < hd, got[0][0], got[1][0])
        o_ref[lo:hi, :] = jnp.where(pos < length, o, 0.0).astype(BF16)
        l_ref[lo:hi, :] = jnp.where(lane_b < hd, got[0][1], got[1][1])

def attn_fwd(length, q, k, v, c, blk=256):
    rows, cols = q.shape
    pairs = cols // 128
    spec = pl.BlockSpec((rows, 128), lambda p: (0, p))
    return pl.pallas_call(
        functools.partial(attn_fwd_kernel, blk=blk),
        grid=(pairs,),
        in_specs=[pl.BlockSpec(memory_space=pltpu.SMEM), spec, spec, spec,
                  pl.BlockSpec((1, rows, 2), lambda p: (p, 0, 0))],
        out_specs=[spec, spec],
        out_shape=[jax.ShapeDtypeStruct((rows, cols), BF16), jax.ShapeDtypeStruct((rows, cols), F32)],
        compiler_params=pltpu.CompilerParams(vmem_limit_bytes=VMEM_BYTES),
        cost_estimate=pl.CostEstimate(flops=rows*rows*128*4*pairs*2, bytes_accessed=rows*cols*12, transcendentals=rows*rows*pairs),
    )(length, q, k, v, c)

def attn_bwd_kernel(len_ref, q_ref, k_ref, v_ref, c_ref, l_ref, o_ref, g_ref, dq_ref, dk_ref, dv_ref, dc_ref, acc_k, acc_v, *, blk):
    rows, wide = q_ref.shape
    hd = wide // 2
    length = len_ref[0]
    lane = lax.broadcasted_iota(jnp.int32, (rows, wide), 1)
    q = q_ref[...].astype(F32) * 0.125
    k = k_ref[...].astype(F32)
    v = v_ref[...].astype(F32)
    g = g_ref[...].astype(F32)
    go = g * o_ref[...].astype(F32)
    tri = lax.broadcasted_iota(jnp.int32, (blk, blk), 0) <= lax.broadcasted_iota(jnp.int32, (blk, blk), 1)
    res = []
    for h in range(2):
        inside = (lane < hd) if h == 0 else (lane >= hd)
        base = hd if h == 0 else 0
        bias = jnp.broadcast_to(gate_column(c_ref, h, length, rows), (rows, wide))
        logt = l_ref[...]
        logt = jnp.where(inside, pltpu.roll(logt, hd, 1), logt)
        other = pltpu.roll(l_ref[...], hd, 1)
        logt = jnp.where(inside, l_ref[...], other)
        dot_o = jnp.broadcast_to(jnp.sum(jnp.where(inside, go, 0.0), axis=1, keepdims=True), (rows, wide))
        kx = jnp.where(inside, k, side(lane, base, pieces(bias) + (1.0, 1.0, 1.0), 0.0)).astype(BF16)
        qx = jnp.where(inside, q, side(lane, base, (1.0, 1.0, 1.0) + pieces(-logt), 0.0)).astype(BF16)
        vx = jnp.where(inside, v, side(lane, base, (1.0, 1.0, 1.0), 0.0)).astype(BF16)
        gx = jnp.where(inside, g, side(lane, base, pieces(-dot_o), 0.0)).astype(BF16)
        kt = kx.T
        dq_parts = []
        for i in range(rows // blk):
            lo, hi = i * blk, (i + 1) * blk
            dqt = None
            for a, b, diag in ((lo, hi, True),) + (((0, lo, False),) if i else ()):
                s = nt(kx[a:b], qx[lo:hi])
                if diag:
                    s = jnp.where(tri, s, NEG_BIG)
                p = jnp.exp(s)
                ds = (p * nt(vx[a:b], gx[lo:hi])).astype(BF16)
                dv = nn(p.astype(BF16), g_ref[lo:hi, :])
                dk = nn(ds, qx[lo:hi])
                t = nn(kt[:, a:b], ds)
                dqt = t if dqt is None else dqt + t
                if diag:
                    acc_v[a:b, :] = dv
                    acc_k[a:b, :] = dk
                else:
                    acc_v[a:b, :] += dv
                    acc_k[a:b, :] += dk
            dq_parts.append(dqt.T)
        dq = jnp.concatenate(dq_parts, axis=0)
        dk = acc_k[...]
        res.append((dq, dk, acc_v[...], dq - pltpu.roll(dk, 3, 1)))
    first = lane < hd
    dq_ref[...] = jnp.where(first, res[0][0] * 0.125, res[1][0] * 0.125).astype(BF16)
    dk_ref[...] = jnp.where(first, res[0][1], res[1][1]).astype(BF16)
    dv_ref[...] = jnp.where(first, res[0][2], res[1][2]).astype(BF16)
    dc_ref[...] = jnp.where(first, res[1][3], res[0][3])

def attn_bwd(length, q, k, v, c, l, o, g, blk=256):
    rows, cols = q.shape
    pairs = cols // 128
    spec = pl.BlockSpec((rows, 128), lambda p: (0, p))
    low = jax.ShapeDtypeStruct((rows, cols), BF16)
    dq, dk, dv, dc = pl.pallas_call(
        functools.partial(attn_bwd_kernel, blk=blk),
        grid=(pairs,),
        in_specs=[pl.BlockSpec(memory_space=pltpu.SMEM), spec, spec, spec,
                  pl.BlockSpec((1, rows, 2), lambda p: (p, 0, 0)), spec, spec, spec],
        out_specs=[spec]*4,
        out_shape=[low, low, low, jax.ShapeDtypeStruct((rows, cols), F32)],
        scratch_shapes=[pltpu.VMEM((rows, 128), F32)]*2,
        compiler_params=pltpu.CompilerParams(vmem_limit_bytes=VMEM_BYTES),
        cost_estimate=pl.CostEstimate(flops=rows*rows*128*10*pairs*2, bytes_accessed=rows*cols*24, transcendentals=rows*rows*pairs),
    )(length, q, k, v, c, l, o, g)
    d3 = dc.reshape(rows, pairs, 128)
    grad_cumul = jnp.stack([d3[:, :, 67], d3[:, :, 3]], axis=2).reshape(rows, 2 * pairs)
    return dq, dk, dv, grad_cumul


def whole(array):
    return pl.BlockSpec(array.shape, lambda *_: (0,) * array.ndim, pipeline_mode=pl.Buffered(1))


def cost(flops, arrays, more=0):
    size = sum(a.size * a.dtype.itemsize for a in arrays)
    return pl.CostEstimate(flops=flops, bytes_accessed=size + more, transcendentals=0)


def joined(refs, lo=None, hi=None):
    if lo is None:
        return jnp.concatenate([r[...] for r in refs], axis=1)
    return jnp.concatenate([r[lo:hi, :] for r in refs], axis=1)


def project_kernel(x_ref, *refs, shard):
    w_refs, (q_ref, k_ref, v_ref, f_ref) = refs[:-4], refs[-4:]
    step = w_refs[0].shape[0] // 2
    x = x_ref[...]
    for kind, out in enumerate((q_ref, k_ref, v_ref)):
        rows = [joined(w_refs, t * step + kind * shard, t * step + (kind + 1) * shard) for t in range(2)]
        out[...] = nt(x, jnp.concatenate(rows, axis=0)).astype(BF16)
    rows = [joined(w_refs, t * step + 3 * shard, (t + 1) * step) for t in range(2)]
    f_ref[0] = nt(x, jnp.concatenate(rows, axis=0))


def project(x, weights, shard, few):
    rows = x.shape[0]
    step = weights[0].shape[0] // 2
    low = jax.ShapeDtypeStruct((rows, 4 * shard), BF16)
    spec = pl.BlockSpec((rows, 2 * shard), lambda i: (0, i))
    pad = step // 2 - 3 * shard
    q, k, v, f = pl.pallas_call(
        functools.partial(project_kernel, shard=shard),
        grid=(2,),
        in_specs=[whole(x)]
        + [pl.BlockSpec((step, w.shape[1]), lambda i: (i, 0)) for w in weights],
        out_specs=[spec, spec, spec, pl.BlockSpec((1, rows, 2 * pad), lambda i: (i, 0, 0))],
        out_shape=[low, low, low, jax.ShapeDtypeStruct((2, rows, 2 * pad), F32)],
        compiler_params=pltpu.CompilerParams(vmem_limit_bytes=VMEM_BYTES),
        cost_estimate=cost(2 * rows * x.shape[1] * 4 * step // 2, [x, *weights, low, low, low]),
        name="project",
    )(x, *weights)
    logits = f.reshape(2, rows, 2, pad)[..., :few].transpose(1, 0, 2, 3).reshape(rows, 4 * few)
    return q, k, v, logits


def combine_kernel(core_ref, *refs, lefts):
    left_refs, w_refs, (give_ref, keep_ref) = refs[:lefts], refs[lefts:-2], refs[-2:]
    step = pl.program_id(0)
    wide = w_refs[0].shape[1]
    for out, cond in ((give_ref, step < 2), (keep_ref, step >= 2)):

        @pl.when(cond)
        def _():
            for n, w in enumerate(w_refs):
                got, at = None, 0
                for left in left_refs:
                    deep = left.shape[1]
                    part = nn(left[...], w[at : at + deep, :])
                    got = part if got is None else got + part
                    at += deep
                out[:, n * wide : (n + 1) * wide] = got.astype(out.dtype)


def combine(core, lefts, weights):
    rows = lefts[0].shape[0]
    wide = weights[0].shape[1] * len(weights)
    block = rows // 4

    def place(i, core_ref):
        mine = core_ref[0]
        return (jnp.where(i < 2, (1 - mine) * 2 + i, mine * 2 + i - 2), 0)

    outs = [
        jax.ShapeDtypeStruct((rows // 2, wide), BF16),
        jax.ShapeDtypeStruct((rows // 2, wide), F32),
    ]
    return pl.pallas_call(
        functools.partial(combine_kernel, lefts=len(lefts)),
        grid_spec=pltpu.PrefetchScalarGridSpec(
            num_scalar_prefetch=1,
            grid=(4,),
            in_specs=[pl.BlockSpec((block, left.shape[1]), place) for left in lefts]
            + [whole(w) for w in weights],
            out_specs=[
                pl.BlockSpec((block, wide), lambda i, c: (jnp.minimum(i, 1), 0)),
                pl.BlockSpec((block, wide), lambda i, c: (jnp.maximum(i - 2, 0), 0)),
            ],
        ),
        out_shape=outs,
        compiler_params=pltpu.CompilerParams(vmem_limit_bytes=VMEM_BYTES),
        cost_estimate=cost(
            2 * rows * weights[0].shape[0] * wide, [*lefts, *weights, *outs]
        ),
        name="combine",
    )(core.reshape(1), *lefts, *weights)


def spread_kernel(len_ref, x_ref, *refs):
    w_refs, out_ref = refs[:-1], refs[-1]
    rows = x_ref.shape[0]
    got = nt(x_ref[...], joined(w_refs))
    pos = pl.program_id(0) * rows + lax.broadcasted_iota(jnp.int32, got.shape, 0)
    out_ref[...] = jnp.where(pos < len_ref[0], got, 0.0).astype(BF16)


def spread(length, x, weights):
    rows, wide = x.shape[0], weights[0].shape[0]
    block = rows // 4
    out = jax.ShapeDtypeStruct((rows, wide), BF16)
    return pl.pallas_call(
        spread_kernel,
        grid=(4,),
        in_specs=[
            pl.BlockSpec(memory_space=pltpu.SMEM),
            pl.BlockSpec((block, x.shape[1]), lambda i: (i, 0)),
        ]
        + [whole(w) for w in weights],
        out_specs=pl.BlockSpec((block, wide), lambda i: (i, 0)),
        out_shape=out,
        compiler_params=pltpu.CompilerParams(vmem_limit_bytes=VMEM_BYTES),
        cost_estimate=cost(2 * rows * x.shape[1] * wide, [x, *weights, out]),
        name="spread",
    )(length, x, *weights)


def inner_kernel(x_ref, *refs):
    w_refs, (gate_ref, up_ref, inner_ref) = refs[:-3], refs[-3:]
    both = nt(x_ref[...], joined(w_refs))
    gate, up = both[:, :UNIT_BLOCK], both[:, UNIT_BLOCK:]
    gate_ref[...] = gate
    up_ref[...] = up
    inner_ref[...] = (gate * jax.nn.sigmoid(gate) * up).astype(BF16)


def inner_units(x, weights):
    rows = x.shape[0]
    total = weights[0].shape[0] // 2
    spec = pl.BlockSpec((rows, UNIT_BLOCK), lambda i: (0, i))
    outs = [jax.ShapeDtypeStruct((rows, total), t) for t in (F32, F32, BF16)]
    return pl.pallas_call(
        inner_kernel,
        grid=(total // UNIT_BLOCK,),
        in_specs=[whole(x)]
        + [pl.BlockSpec((2 * UNIT_BLOCK, w.shape[1]), lambda i: (i, 0)) for w in weights],
        out_specs=[spec] * 3,
        out_shape=outs,
        compiler_params=pltpu.CompilerParams(vmem_limit_bytes=VMEM_BYTES),
        cost_estimate=cost(4 * rows * x.shape[1] * total, [x, *weights, *outs]),
        name="inner_units",
    )(x, *weights)


def inner_grads_kernel(x_ref, gate_ref, up_ref, *refs):
    down_refs, pre_ref = refs[:-1], refs[-1]
    grad = nt(x_ref[...], joined(down_refs))
    gate, up = gate_ref[...], up_ref[...]
    sig = jax.nn.sigmoid(gate)
    pre_ref[:, :UNIT_BLOCK] = (grad * up * (sig * (1.0 + gate * (1.0 - sig)))).astype(BF16)
    pre_ref[:, UNIT_BLOCK:] = (grad * (gate * sig)).astype(BF16)


def inner_grads(x, gate, up, down):
    rows, cols = x.shape
    total = gate.shape[1]
    spec = pl.BlockSpec((rows, UNIT_BLOCK), lambda i: (0, i))
    out = jax.ShapeDtypeStruct((rows, 2 * total), BF16)
    return pl.pallas_call(
        inner_grads_kernel,
        grid=(total // UNIT_BLOCK,),
        in_specs=[whole(x), spec, spec]
        + [pl.BlockSpec((UNIT_BLOCK, w.shape[1]), lambda i: (i, 0)) for w in down],
        out_specs=pl.BlockSpec((rows, 2 * UNIT_BLOCK), lambda i: (0, i)),
        out_shape=out,
        compiler_params=pltpu.CompilerParams(vmem_limit_bytes=VMEM_BYTES),
        cost_estimate=cost(2 * rows * cols * total, [x, gate, up, *down, out]),
        name="inner_grads",
    )(x, gate, up, *down)


def half_products(left_refs, right, side):
    parts = []
    for ref, narrow in left_refs:
        got = dot_first(ref[...], right)
        if narrow:
            few = got.shape[0] // 2
            got = jnp.where(side == 0, got[:few], got[few:])
        parts.append(got)
    return parts


def term_kernel(*refs, narrow, side):
    count = len(narrow)
    right_ref, add_refs, out_ref = refs[count], refs[count + 1 : -1], refs[-1]
    at = 0
    for part in half_products(list(zip(refs[:count], narrow)), right_ref[...], side):
        rows = slice(at, at + part.shape[0])
        for add in add_refs:
            part = part + add[rows, :].astype(F32)
        out_ref[rows, :] = part.astype(BF16)
        at += part.shape[0]


def left_specs(lefts, steps, block):
    specs, narrow = [], []
    for left in lefts:
        rows, cols = left.shape
        wide = cols // (2 * steps)
        narrow.append(wide % 128 != 0)
        if wide % 128:
            specs.append(pl.BlockSpec((rows, cols), lambda i: (0, 0)))
        else:
            specs.append(pl.BlockSpec((rows, wide), lambda i: (0, block(i))))
    return specs, tuple(narrow)


def chunks_of(lefts):
    half = lefts[0].shape[1] // 2
    return max(1, half // 512) if len(lefts) == 1 else 1


def term_sum(lefts, right, side, r, wide, adds=()):
    steps = chunks_of(lefts)
    half = sum(left.shape[1] for left in lefts) // 2
    specs, narrow = left_specs(lefts, steps, lambda i: side * steps + i)
    part = pl.BlockSpec((half // steps, wide), lambda i: (i, 0))
    out = jax.ShapeDtypeStruct((half, wide), BF16)
    return pl.pallas_call(
        functools.partial(term_kernel, narrow=narrow, side=side),
        grid=(steps,),
        in_specs=specs
        + [pl.BlockSpec((right.shape[0], wide), lambda i: (0, r))]
        + [part] * len(adds),
        out_specs=part,
        out_shape=out,
        compiler_params=pltpu.CompilerParams(vmem_limit_bytes=VMEM_BYTES),
        cost_estimate=cost(2 * right.shape[0] * half * wide, [*adds, out, out]),
        name="term_sum",
    )(*lefts, right, *adds)


def total_kernel(*refs, narrow, steps):
    count = len(narrow)
    right_ref, tops, lows, out_ref = refs[count], refs[count + 1 : -3], refs[-3:-1], refs[-1]
    step = pl.program_id(0)
    side = step // steps
    parts = half_products(list(zip(refs[:count], narrow)), right_ref[...], side)
    if count == 1:
        places = [parts]
    else:
        places = [
            [part[n * (part.shape[0] // 2) : (n + 1) * (part.shape[0] // 2)] for part in parts]
            for n in range(2)
        ]
    for this, adds in ((0, tops), (1, lows)):

        @pl.when(side == this)
        def _():
            at = 0
            for n, place in enumerate(places):
                off = 0
                for part, whole_part in zip(place, parts):
                    few = part.shape[0]
                    start = off + n * few if count > 1 else 0
                    got = part
                    for add in adds:
                        got = got + add[start : start + few, :].astype(F32)
                    out_ref[at : at + few, :] = got.astype(BF16)
                    at += few
                    off += whole_part.shape[0]


def total_sum(lefts, right, tops, lows, wide):
    steps = chunks_of(lefts)
    full = sum(left.shape[1] for left in lefts)
    block = full // (2 * steps)
    specs, narrow = left_specs(lefts, steps, lambda i: i)
    out = jax.ShapeDtypeStruct((full, wide), BF16)
    return pl.pallas_call(
        functools.partial(total_kernel, narrow=narrow, steps=steps),
        grid=(2 * steps,),
        in_specs=specs
        + [pl.BlockSpec((right.shape[0], wide), lambda i: (0, 0))]
        + [pl.BlockSpec((block, wide), lambda i: (jnp.minimum(i, steps - 1), 0))] * 2
        + [pl.BlockSpec((block, wide), lambda i: (jnp.maximum(i - steps, 0), 0))] * 2,
        out_specs=pl.BlockSpec((block, wide), lambda i: (i, 0)),
        out_shape=out,
        compiler_params=pltpu.CompilerParams(vmem_limit_bytes=VMEM_BYTES),
        cost_estimate=cost(2 * right.shape[0] * full * wide, [out, out, out]),
        name="total_sum",
    )(*lefts, right, *tops, *lows)


class Plan:
    def __init__(self, ways_dp, ways_tensor):
        self.ways_dp = ways_dp
        self.ways_tensor = ways_tensor
        self.chips = ways_dp // 2
        self.bits = self.chips.bit_length() - 1
        assert self.chips == 1 << self.bits and ways_tensor == 4
        dp = lax.axis_index("dp")
        self.chip = dp // 2
        self.core = dp % 2
        self.place = lax.axis_index("tensor")
        self.core_perm = [(i, i ^ 1) for i in range(ways_dp)]

    def swap_core(self, array):
        return lax.ppermute(array, "dp", self.core_perm)

    def swap_chip(self, array, bit):
        perm = [(i, i ^ (2 << bit)) for i in range(self.ways_dp)]
        return lax.ppermute(array, "dp", perm)

    def route(self, turn):
        pairs = []
        for chip in range(self.chips):
            for core in range(2):
                for z in range(4):
                    micro = (z + turn) % 2
                    source = (2 * chip + core) * 4 + z
                    target = (2 * chip + z // 2) * 4 + 2 * micro + core
                    pairs.append((source, target))
        return pairs

    def by_chip(self, array):
        lead = array.shape[:-1]
        wide = array.shape[-1] // self.chips
        parts = [
            lax.dynamic_slice_in_dim(array, (self.chip ^ r) * wide, wide, axis=-1)
            for r in range(self.chips)
        ]
        return jnp.concatenate(parts, axis=-1).reshape(*lead, -1)

    def to_chip(self, array):
        got = []
        for turn in range(2):
            micro = (self.place + turn) % 2
            part = lax.dynamic_index_in_dim(array, micro, 0, keepdims=False)
            got.append(lax.ppermute(self.by_chip(part), ("dp", "tensor"), self.route(turn)))
        first = self.place // 2 == 0
        return jnp.concatenate(
            [jnp.where(first, got[0], got[1]), jnp.where(first, got[1], got[0])], axis=0
        )

    def from_chip(self, array):
        rows = array.shape[0] // 2
        got = []
        for turn in range(2):
            block = (self.place // 2 + turn) % 2
            part = lax.dynamic_slice_in_dim(array, block * rows, rows, axis=0)
            back = [(b, a) for a, b in self.route(turn)]
            got.append(lax.ppermute(self.by_chip(part), ("dp", "tensor"), back))
        first = self.place % 2 == 0
        return jnp.stack([jnp.where(first, got[0], got[1]), jnp.where(first, got[1], got[0])])

    def both_rows(self, half):
        other = self.swap_core(half)
        first = self.core == 0
        return jnp.concatenate(
            [jnp.where(first, half, other), jnp.where(first, other, half)], axis=0
        )

    def sum_rows(self, give, keep):
        return keep + self.swap_core(give).astype(F32)

    def line_gather(self, shard):
        mine = lax.dynamic_index_in_dim(shard, self.core, 0, keepdims=False)
        theirs = lax.dynamic_index_in_dim(shard, 1 - self.core, 0, keepdims=False)
        other = self.swap_core(theirs)
        first = self.core == 0
        pair = jnp.concatenate(
            [jnp.where(first, mine, other), jnp.where(first, other, mine)], axis=1
        )
        return lax.all_gather(pair, "tensor", axis=0, tiled=True)

    def near_gather(self, own):
        if self.bits == 2:
            return [own, self.swap_chip(own, 0), self.swap_chip(own, 1)]
        parts = [own]
        for bit in range(self.bits):
            parts = parts + [self.swap_chip(p, bit) for p in parts]
        return [jnp.concatenate(parts, axis=1)]

    def far_gather(self, near):
        if self.bits != 2:
            return near
        own, by_x, by_y = near
        half = own.shape[0] // 2
        far_top = self.swap_chip(by_x[:half], 1)
        far_low = self.swap_chip(by_y[half:], 0)
        return [own, by_x, by_y, jnp.concatenate([far_top, far_low], axis=0)]

    def scatter(self, total):
        return lax.psum_scatter(total, "tensor", scatter_dimension=0, tiled=True)

    def share(self, pair):
        narrow = pair.shape[1] // 2
        mine = lax.dynamic_slice_in_dim(pair, self.core * narrow, narrow, axis=1)
        theirs = lax.dynamic_slice_in_dim(pair, (1 - self.core) * narrow, narrow, axis=1)
        other = self.swap_core(theirs)
        first = self.core == 0
        return jnp.stack([jnp.where(first, mine, other), jnp.where(first, other, mine)]).astype(F32)

    def sum_all(self, vector):
        vector = vector + self.swap_core(vector)
        for bit in range(self.bits):
            vector = vector + self.swap_chip(vector, bit)
        for bit in range(2):
            perm = [(z, z ^ (1 << bit)) for z in range(4)]
            vector = vector + lax.ppermute(vector, "tensor", perm)
        return vector


class Reduction:
    def __init__(self, plan, lefts, right):
        self.plan, self.lefts, self.right = plan, lefts, right
        self.wide = right.shape[1] // plan.chips
        self.staged = plan.bits == 2
        if self.staged:
            if len(lefts) == 1:
                self.first = [
                    self.top(3).astype(BF16),
                    self.low(3).astype(BF16),
                    self.low(1).astype(BF16),
                    self.top(2).astype(BF16),
                ]
            else:
                self.first = [self.sent(0, 3), self.sent(1, 3), self.sent(1, 1), self.sent(0, 2)]
        else:
            self.first = [
                jnp.concatenate([self.top(r), self.low(r)], axis=0) for r in range(plan.chips)
            ]

    def term(self, r, side):
        right = self.right[:, r * self.wide : (r + 1) * self.wide]
        parts = []
        for left in self.lefts:
            half = left.shape[1] // 2
            parts.append(dot_first(left[:, side * half : (side + 1) * half], right))
        return parts[0] if len(parts) == 1 else jnp.concatenate(parts, axis=0)

    def sent(self, side, r, *adds):
        return term_sum(self.lefts, self.right, side, r, self.wide, adds)

    def top(self, r):
        return self.term(r, 0)

    def low(self, r):
        return self.term(r, 1)

    def by_place(self, half):
        if len(self.lefts) == 1:
            return half
        parts, at = [], 0
        for left in self.lefts:
            parts.append((at, left.shape[1] // 4))
            at += left.shape[1] // 2
        return jnp.concatenate(
            [half[at + n * few : at + (n + 1) * few] for n in range(2) for at, few in parts], axis=0
        )

    def send_first(self):
        if self.staged:
            a, b, c, d = self.first
            swap = self.plan.swap_chip
            self.got = [swap(a, 1), swap(b, 0), swap(c, 0), swap(d, 1)]
        else:
            self.got = list(self.first)

    def prepare_second(self):
        if self.staged:
            far_top, far_low = self.got[:2]
            self.second = [self.sent(0, 1, far_top), self.sent(1, 2, far_low)]
        else:
            self.second = []

    def send_second(self):
        if self.staged:
            self.last = [self.plan.swap_chip(self.second[0], 0), self.plan.swap_chip(self.second[1], 1)]
        else:
            self.last = []

    def finish(self):
        if self.staged:
            x_top, y_low = self.last
            x_low, y_top = self.got[2:]
            return total_sum(self.lefts, self.right, (x_top, y_top), (x_low, y_low), self.wide)
        else:
            parts = self.got
            for bit in reversed(range(self.plan.bits)):
                keep, give = parts[: 1 << bit], parts[1 << bit :]
                parts = [
                    k + self.plan.swap_chip(g.astype(BF16), bit).astype(F32)
                    for k, g in zip(keep, give)
                ]
            half = parts[0].shape[0] // 2
            total = jnp.concatenate(
                [self.by_place(parts[0][:half]), self.by_place(parts[0][half:])], axis=0
            )
        return total.astype(BF16)


class Direct:
    def __init__(self, plan, lefts, right):
        self.plan, self.left, self.right = plan, lefts[0], right
        self.wide = right.shape[1] // plan.chips
        self.first = [self.term(r).astype(BF16) for r in range(1, plan.chips)]

    def term(self, r):
        return dot_first(self.left, self.right[:, r * self.wide : (r + 1) * self.wide])

    def send_first(self):
        ways = range(self.plan.ways_dp)
        self.got = [
            lax.ppermute(part, "dp", [(i, i ^ (2 * (n + 1))) for i in ways])
            for n, part in enumerate(self.first)
        ]

    def prepare_second(self):
        self.second = []

    def send_second(self):
        self.last = []

    def finish(self):
        total = self.term(0)
        for part in self.got:
            total = total + part.astype(F32)
        return total.astype(BF16)


def together(*groups):
    return lax.optimization_barrier(groups)


def split_columns(matrix):
    return matrix.T.reshape(2, matrix.shape[1] // 2, matrix.shape[0])


def split_rows(matrix):
    return matrix.reshape(2, matrix.shape[0] // 2, matrix.shape[1])


def body(
    inputs,
    seq_lengths,
    seq_assign,
    norm1_gain,
    w_query,
    w_key,
    w_value,
    w_forget,
    forget_bias,
    w_out,
    norm2_gain,
    w_gate,
    w_up,
    w_down,
    out_grad,
):
    plan = Plan(lax.axis_size("dp"), lax.axis_size("tensor"))
    core, place = plan.core, plan.place
    part_rows = inputs.shape[1]
    seq_rows = part_rows * 4
    half_rows = seq_rows // 2
    heads_shard = w_forget.shape[1] // 2
    heads_here = heads_shard * 4
    shard_cols = w_query.shape[1] // 2
    blocks = w_gate.shape[1] // 2 // UNIT_BLOCK

    def by_block(matrix):
        return split_columns(matrix).reshape(2, blocks, 1, UNIT_BLOCK, matrix.shape[0])

    forget_part = jnp.pad(
        split_columns(w_forget), ((0, 0), (0, FORGET_PAD - heads_shard), (0, 0))
    )
    line_one = plan.line_gather(
        jnp.concatenate(
            [split_columns(w_query), split_columns(w_key), split_columns(w_value), forget_part],
            axis=1,
        )
    )
    inputs, line_one = together(inputs, line_one)
    rows_one = line_one.shape[0] // 4

    def by_kind(piece):
        piece = piece.reshape(4, rows_one, -1)
        edges = [0, shard_cols, 2 * shard_cols, 3 * shard_cols, rows_one]
        parts = [piece[:, a:b].reshape(-1, piece.shape[-1]) for a, b in zip(edges, edges[1:])]
        return jnp.concatenate(parts, axis=0)

    full_one = plan.far_gather(plan.near_gather(line_one))
    rows_in = plan.to_chip(inputs)
    rows_in, full_one = together(rows_in, full_one)
    rows_in = rows_in.astype(F32)
    line_mid = plan.line_gather(
        jnp.concatenate([split_rows(w_out), split_rows(w_down)], axis=1)
    )
    line_mid, full_one = together(line_mid, full_one)
    line_mid = line_mid.reshape(4, -1, line_mid.shape[-1])
    near_out = plan.near_gather(line_mid[:, :shard_cols].reshape(4 * shard_cols, -1))
    near_down = plan.near_gather(line_mid[:, shard_cols:].reshape(-1, line_mid.shape[-1]))
    two_part = jnp.concatenate([by_block(w_gate), by_block(w_up)], axis=2)
    line_two = plan.line_gather(two_part.reshape(2, -1, two_part.shape[-1]))

    other_assign = plan.swap_core(seq_assign)
    assign_both = jnp.where(
        core == 0,
        jnp.concatenate([seq_assign, other_assign], axis=1),
        jnp.concatenate([other_assign, seq_assign], axis=1),
    ).reshape(4)
    seq_id = jnp.sum(jnp.where(jnp.arange(4) == place, assign_both, 0))
    length = jnp.sum(jnp.where(jnp.arange(seq_lengths.shape[0]) == seq_id, seq_lengths, 0))
    count = length.reshape(1)
    valid_here = (core * half_rows + jnp.arange(half_rows) < length).astype(F32)[:, None]

    gain_one = plan.by_chip(norm1_gain)
    gain_two = plan.by_chip(norm2_gain)
    bias_here = lax.dynamic_index_in_dim(
        forget_bias.reshape(4, 2, heads_shard), core, 1, keepdims=False
    ).reshape(-1)

    scale_one = row_scale(rows_in)
    normed_one = plan.both_rows((rows_in * scale_one * gain_one).astype(BF16))
    queries, key_rows, value_rows, logits = project(
        normed_one, full_one, shard_cols, heads_shard
    )
    forget_logit = logits + bias_here
    cumul_gate = jnp.cumsum(jax.nn.log_sigmoid(forget_logit), axis=0)
    gate_pairs = cumul_gate.reshape(seq_rows, heads_here // 2, 2).transpose(1, 0, 2)
    near_out, gate_pairs = together(near_out, gate_pairs)
    full_out, line_two, gate_pairs = together(plan.far_gather(near_out), line_two, gate_pairs)
    mixed_low, log_total = attn_fwd(count, queries, key_rows, value_rows, gate_pairs)
    mixed_low, near_down, full_one = together(mixed_low, near_down, full_one)
    kinds_one = [by_kind(piece) for piece in full_one]
    full_down = plan.far_gather(near_down)
    near_two, out_grad = together(plan.near_gather(line_two), out_grad)
    full_two = plan.far_gather(near_two)
    cotangent = plan.to_chip(out_grad).astype(F32)
    hidden_in = rows_in + plan.sum_rows(*combine(core, [mixed_low], full_out))

    scale_two = row_scale(hidden_in)
    normed_two = plan.both_rows((hidden_in * scale_two * gain_two).astype(BF16))
    normed_two, full_down, kinds_one = together(normed_two, full_down, kinds_one)
    gate_pre, up_pre, inner_low = inner_units(normed_two, full_two)
    grad_ffn = plan.both_rows((valid_here * cotangent).astype(BF16))
    down_sum = Reduction(plan, [inner_low], grad_ffn)
    down_sum.first, gate_pre = together(down_sum.first, gate_pre)
    down_sum.send_first()

    grad_pre = inner_grads(grad_ffn, gate_pre, up_pre, full_down)
    down_far, grad_pre = together(down_sum.got[:2], grad_pre)
    down_sum.got = [*down_far, *down_sum.got[2:]]
    two_sum = Reduction(plan, [grad_pre], normed_two)
    two_sum.first, down_sum.got, grad_pre, inner_low = together(
        two_sum.first, down_sum.got, grad_pre, inner_low
    )
    two_sum.send_first()
    down_sum.prepare_second()
    give_two, keep_two = combine(core, [grad_pre], full_two)
    give_ffn, keep_ffn = combine(core, [inner_low], full_down)
    down_sum.send_second()
    two_far, down_sum.last, give_two, give_ffn = together(
        two_sum.got[:2], down_sum.last, give_two, give_ffn
    )
    two_sum.got = [*two_far, *two_sum.got[2:]]
    grad_normed_two = plan.sum_rows(give_two, keep_two)
    gain_two_term = jnp.sum(grad_normed_two * hidden_in * scale_two, axis=0)
    grad_hidden = valid_here * cotangent + norm_back(
        hidden_in, scale_two, gain_two, grad_normed_two
    )

    grad_attn = plan.both_rows(grad_hidden.astype(BF16))
    out_sum = (Direct if plan.bits == 2 else Reduction)(plan, [mixed_low], grad_attn)
    two_sum.prepare_second()
    out_sum.first, two_sum.second, grad_attn = together(
        out_sum.first, two_sum.second, grad_attn
    )
    two_sum.send_second()
    out_sum.send_first()
    ffn_rows = plan.sum_rows(give_ffn, keep_ffn)
    outputs = (valid_here * (hidden_in + ffn_rows)).astype(BF16)
    grad_mixed = spread(count, grad_attn, full_out)
    query_low, key_low, value_low, grad_cumul = attn_bwd(
        count, queries, key_rows, value_rows, gate_pairs, log_total, mixed_low, grad_mixed
    )
    two_sum.got, two_sum.last, out_sum.got, query_low, key_low, value_low, grad_cumul = together(
        two_sum.got, two_sum.last, out_sum.got, query_low, key_low, value_low, grad_cumul
    )
    out_sum.prepare_second()
    out_sum.send_second()
    out_total, grad_cumul = together(out_sum.finish(), grad_cumul)
    down_pair = plan.scatter(down_sum.finish())
    out_total, down_pair = together(out_total, down_pair)
    out_pair = plan.scatter(out_total)
    grad_logf = jnp.flip(jnp.cumsum(jnp.flip(grad_cumul, 0), axis=0), 0)
    grad_logit = grad_logf * jax.nn.sigmoid(-forget_logit)
    bias_term = jnp.sum(grad_logit, axis=0)
    logit_low = jnp.pad(
        grad_logit.astype(BF16).reshape(seq_rows, 4, heads_shard),
        ((0, 0), (0, 0), (0, FORGET_PAD - heads_shard)),
    ).reshape(seq_rows, -1)
    grad_one = [query_low, key_low, value_low, logit_low]
    one_sum = Reduction(plan, grad_one, normed_one)
    one_sum.first, two_sum.last, outputs = together(one_sum.first, two_sum.last, outputs)
    one_sum.send_first()
    outputs = plan.from_chip(outputs)
    one_sum.prepare_second()
    one_sum.send_second()
    two_total, out_pair = together(two_sum.finish(), out_pair)
    two_pair = plan.scatter(two_total)
    one_total, two_pair, grad_one = together(one_sum.finish(), two_pair, grad_one)
    one_pair = plan.scatter(one_total)
    grad_normed_one = plan.sum_rows(*combine(core, grad_one, kinds_one))
    gain_one_term = jnp.sum(grad_normed_one * rows_in * scale_one, axis=0)
    input_grad = plan.from_chip(
        (grad_hidden + norm_back(rows_in, scale_one, gain_one, grad_normed_one)).astype(BF16)
    )

    bias_full = jnp.where(
        (jnp.arange(2) == core)[None, :, None], bias_term.reshape(4, 1, heads_shard), 0.0
    ).reshape(-1)
    wide = norm1_gain.shape[0]
    small = plan.sum_all(
        jnp.concatenate([plan.by_chip(gain_one_term), plan.by_chip(gain_two_term), bias_full])
    )

    down_shard, two_shard = plan.share(down_pair), plan.share(two_pair)
    out_shard, one_shard = plan.share(out_pair), plan.share(one_pair)

    two_shard = two_shard.reshape(2, blocks, 2, UNIT_BLOCK, -1)

    def columns(shard):
        return shard.reshape(-1, shard.shape[-1]).T

    def rows(shard):
        return shard.reshape(-1, shard.shape[-1])

    return (
        outputs,
        input_grad,
        small[:wide],
        columns(one_shard[:, :shard_cols]),
        columns(one_shard[:, shard_cols : 2 * shard_cols]),
        columns(one_shard[:, 2 * shard_cols : 3 * shard_cols]),
        columns(one_shard[:, 3 * shard_cols : 3 * shard_cols + heads_shard]),
        small[2 * wide :],
        rows(out_shard),
        small[wide : 2 * wide],
        columns(two_shard[:, :, 0]),
        columns(two_shard[:, :, 1]),
        rows(down_shard),
    )


def solution(mesh):
    return jax.shard_map(
        body,
        mesh=mesh,
        in_specs=(
            P(None, ("dp", "tensor"), None),
            P(),
            P(None, "dp"),
            P(),
            P("dp", "tensor"),
            P("dp", "tensor"),
            P("dp", "tensor"),
            P("dp", "tensor"),
            P(),
            P("tensor", "dp"),
            P(),
            P("dp", "tensor"),
            P("dp", "tensor"),
            P("tensor", "dp"),
            P(None, ("dp", "tensor"), None),
        ),
        out_specs=(
            P(None, ("dp", "tensor"), None),
            P(None, ("dp", "tensor"), None),
            P(),
            P("dp", "tensor"),
            P("dp", "tensor"),
            P("dp", "tensor"),
            P("dp", "tensor"),
            P(),
            P("tensor", "dp"),
            P(),
            P("dp", "tensor"),
            P("dp", "tensor"),
            P("tensor", "dp"),
        ),
        check_vma=False,
    )
```

```python
import functools

import jax
import jax.numpy as jnp
from jax import lax
from jax.experimental import pallas as pl
from jax.experimental.pallas import tpu as pltpu
from jax.sharding import PartitionSpec as P

EPS = 1e-06
NEG_BIG = -1e30
F32 = jnp.float32
BF16 = jnp.bfloat16
FORGET_PAD = 16
UNIT_BLOCK = 256
VMEM_BYTES = 60 << 20


def row_scale(tokens):
    return lax.rsqrt(jnp.mean(tokens * tokens, axis=-1, keepdims=True) + EPS)


def norm_back(tokens, scaling, gain, grad_out):
    weighted = grad_out * gain
    cubed = scaling * scaling * scaling
    return scaling * weighted - tokens * cubed * jnp.mean(weighted * tokens, axis=-1, keepdims=True)


def dot_first(left, right):
    return lax.dot_general(left, right, (((0,), (0,)), ((), ())), preferred_element_type=F32)

def nt(a, b):
    return lax.dot_general(a, b, (((1,), (1,)), ((), ())), preferred_element_type=F32)

def nn(a, b):
    return lax.dot_general(a, b, (((1,), (0,)), ((), ())), preferred_element_type=F32)

def pieces(x):
    top = x.astype(BF16).astype(F32)
    rest = x - top
    mid = rest.astype(BF16).astype(F32)
    return top, mid, rest - mid

def side(lane, base, values, rest):
    for n, value in enumerate(values):
        rest = jnp.where(lane == base + n, value, rest)
    return rest

def gate_column(c_ref, which, length, rows):
    col = c_ref[0, :, which : which + 1]
    pos = lax.broadcasted_iota(jnp.int32, (rows, 1), 0)
    return jnp.where(pos < length, -col, NEG_BIG)

def attn_fwd_kernel(len_ref, q_ref, k_ref, v_ref, c_ref, o_ref, l_ref, *, blk):
    rows, wide = q_ref.shape
    hd = wide // 2
    length = len_ref[0]
    lane = lax.broadcasted_iota(jnp.int32, (rows, wide), 1)
    lane_b = lax.broadcasted_iota(jnp.int32, (blk, wide), 1)
    q = q_ref[...].astype(F32) * 0.125
    k = k_ref[...].astype(F32)
    v = v_ref[...].astype(F32)
    heads = []
    for h in range(2):
        inside = (lane < hd) if h == 0 else (lane >= hd)
        base = hd if h == 0 else 0
        bias = jnp.broadcast_to(gate_column(c_ref, h, length, rows), (rows, wide))
        kx = jnp.where(inside, k, side(lane, base, pieces(bias), 0.0)).astype(BF16)
        qx = jnp.where(inside, q, side(lane, base, (1.0, 1.0, 1.0), 0.0)).astype(BF16)
        vx = jnp.where(inside, v, 1.0).astype(BF16)
        heads.append((qx, kx, vx))
    tri = lax.broadcasted_iota(jnp.int32, (blk, blk), 1) <= lax.broadcasted_iota(jnp.int32, (blk, blk), 0)
    for i in range(rows // blk):
        lo, hi = i * blk, (i + 1) * blk
        got = []
        for h in range(2):
            qx, kx, vx = heads[h]
            s_d = jnp.where(tri, nt(qx[lo:hi], kx[lo:hi]), NEG_BIG)
            m = jnp.max(s_d, axis=1, keepdims=True)
            if i:
                s_o = nt(qx[lo:hi], kx[:lo])
                m = jnp.maximum(m, jnp.max(s_o, axis=1, keepdims=True))
            r = nn(jnp.exp(s_d - m).astype(BF16), vx[lo:hi])
            if i:
                r = r + nn(jnp.exp(s_o - m).astype(BF16), vx[:lo])
            total = pltpu.roll(r, hd, 1)
            got.append((r / total, m + jnp.log(total)))
        pos = lo + lax.broadcasted_iota(jnp.int32, (blk, wide), 0)
        o = jnp.where(lane_b < hd, got[0][0], got[1][0])
        o_ref[lo:hi, :] = jnp.where(pos < length, o, 0.0).astype(BF16)
        l_ref[lo:hi, :] = jnp.where(lane_b < hd, got[0][1], got[1][1])

def attn_fwd(length, q, k, v, c, blk=256):
    rows, cols = q.shape
    pairs = cols // 128
    spec = pl.BlockSpec((rows, 128), lambda p: (0, p))
    return pl.pallas_call(
        functools.partial(attn_fwd_kernel, blk=blk),
        grid=(pairs,),
        in_specs=[pl.BlockSpec(memory_space=pltpu.SMEM), spec, spec, spec,
                  pl.BlockSpec((1, rows, 2), lambda p: (p, 0, 0))],
        out_specs=[spec, spec],
        out_shape=[jax.ShapeDtypeStruct((rows, cols), BF16), jax.ShapeDtypeStruct((rows, cols), F32)],
        compiler_params=pltpu.CompilerParams(vmem_limit_bytes=VMEM_BYTES),
        cost_estimate=pl.CostEstimate(flops=rows*rows*128*4*pairs*2, bytes_accessed=rows*cols*12, transcendentals=rows*rows*pairs),
    )(length, q, k, v, c)

def attn_bwd_kernel(len_ref, q_ref, k_ref, v_ref, c_ref, l_ref, o_ref, g_ref, dq_ref, dk_ref, dv_ref, dc_ref, acc_k, acc_v, *, blk):
    rows, wide = q_ref.shape
    hd = wide // 2
    length = len_ref[0]
    lane = lax.broadcasted_iota(jnp.int32, (rows, wide), 1)
    q = q_ref[...].astype(F32) * 0.125
    k = k_ref[...].astype(F32)
    v = v_ref[...].astype(F32)
    g = g_ref[...].astype(F32)
    go = g * o_ref[...].astype(F32)
    tri = lax.broadcasted_iota(jnp.int32, (blk, blk), 0) <= lax.broadcasted_iota(jnp.int32, (blk, blk), 1)
    res = []
    for h in range(2):
        inside = (lane < hd) if h == 0 else (lane >= hd)
        base = hd if h == 0 else 0
        bias = jnp.broadcast_to(gate_column(c_ref, h, length, rows), (rows, wide))
        logt = l_ref[...]
        logt = jnp.where(inside, pltpu.roll(logt, hd, 1), logt)
        other = pltpu.roll(l_ref[...], hd, 1)
        logt = jnp.where(inside, l_ref[...], other)
        dot_o = jnp.broadcast_to(jnp.sum(jnp.where(inside, go, 0.0), axis=1, keepdims=True), (rows, wide))
        kx = jnp.where(inside, k, side(lane, base, pieces(bias) + (1.0, 1.0, 1.0), 0.0)).astype(BF16)
        qx = jnp.where(inside, q, side(lane, base, (1.0, 1.0, 1.0) + pieces(-logt), 0.0)).astype(BF16)
        vx = jnp.where(inside, v, side(lane, base, (1.0, 1.0, 1.0), 0.0)).astype(BF16)
        gx = jnp.where(inside, g, side(lane, base, pieces(-dot_o), 0.0)).astype(BF16)
        kt = kx.T
        dq_parts = []
        for i in range(rows // blk):
            lo, hi = i * blk, (i + 1) * blk
            dqt = None
            for a, b, diag in ((lo, hi, True),) + (((0, lo, False),) if i else ()):
                s = nt(kx[a:b], qx[lo:hi])
                if diag:
                    s = jnp.where(tri, s, NEG_BIG)
                p = jnp.exp(s)
                ds = (p * nt(vx[a:b], gx[lo:hi])).astype(BF16)
                dv = nn(p.astype(BF16), g_ref[lo:hi, :])
                dk = nn(ds, qx[lo:hi])
                t = nn(kt[:, a:b], ds)
                dqt = t if dqt is None else dqt + t
                if diag:
                    acc_v[a:b, :] = dv
                    acc_k[a:b, :] = dk
                else:
                    acc_v[a:b, :] += dv
                    acc_k[a:b, :] += dk
            dq_parts.append(dqt.T)
        dq = jnp.concatenate(dq_parts, axis=0)
        dk = acc_k[...]
        res.append((dq, dk, acc_v[...], dq - pltpu.roll(dk, 3, 1)))
    first = lane < hd
    dq_ref[...] = jnp.where(first, res[0][0] * 0.125, res[1][0] * 0.125).astype(BF16)
    dk_ref[...] = jnp.where(first, res[0][1], res[1][1]).astype(BF16)
    dv_ref[...] = jnp.where(first, res[0][2], res[1][2]).astype(BF16)
    dc_ref[...] = jnp.where(first, res[1][3], res[0][3])

def attn_bwd(length, q, k, v, c, l, o, g, blk=256):
    rows, cols = q.shape
    pairs = cols // 128
    spec = pl.BlockSpec((rows, 128), lambda p: (0, p))
    low = jax.ShapeDtypeStruct((rows, cols), BF16)
    dq, dk, dv, dc = pl.pallas_call(
        functools.partial(attn_bwd_kernel, blk=blk),
        grid=(pairs,),
        in_specs=[pl.BlockSpec(memory_space=pltpu.SMEM), spec, spec, spec,
                  pl.BlockSpec((1, rows, 2), lambda p: (p, 0, 0)), spec, spec, spec],
        out_specs=[spec]*4,
        out_shape=[low, low, low, jax.ShapeDtypeStruct((rows, cols), F32)],
        scratch_shapes=[pltpu.VMEM((rows, 128), F32)]*2,
        compiler_params=pltpu.CompilerParams(vmem_limit_bytes=VMEM_BYTES),
        cost_estimate=pl.CostEstimate(flops=rows*rows*128*10*pairs*2, bytes_accessed=rows*cols*24, transcendentals=rows*rows*pairs),
    )(length, q, k, v, c, l, o, g)
    d3 = dc.reshape(rows, pairs, 128)
    grad_cumul = jnp.stack([d3[:, :, 67], d3[:, :, 3]], axis=2).reshape(rows, 2 * pairs)
    return dq, dk, dv, grad_cumul


def whole(array):
    return pl.BlockSpec(array.shape, lambda *_: (0,) * array.ndim, pipeline_mode=pl.Buffered(1))


def cost(flops, arrays, more=0):
    size = sum(a.size * a.dtype.itemsize for a in arrays)
    return pl.CostEstimate(flops=flops, bytes_accessed=size + more, transcendentals=0)


def joined(refs, lo=None, hi=None):
    if lo is None:
        return jnp.concatenate([r[...] for r in refs], axis=1)
    return jnp.concatenate([r[lo:hi, :] for r in refs], axis=1)


def project_kernel(x_ref, *refs, shard):
    w_refs, (q_ref, k_ref, v_ref, f_ref) = refs[:-4], refs[-4:]
    step = w_refs[0].shape[0] // 2
    x = x_ref[...]
    for kind, out in enumerate((q_ref, k_ref, v_ref)):
        rows = [joined(w_refs, t * step + kind * shard, t * step + (kind + 1) * shard) for t in range(2)]
        out[...] = nt(x, jnp.concatenate(rows, axis=0)).astype(BF16)
    rows = [joined(w_refs, t * step + 3 * shard, (t + 1) * step) for t in range(2)]
    f_ref[0] = nt(x, jnp.concatenate(rows, axis=0))


def project(x, weights, shard, few):
    rows = x.shape[0]
    step = weights[0].shape[0] // 2
    low = jax.ShapeDtypeStruct((rows, 4 * shard), BF16)
    spec = pl.BlockSpec((rows, 2 * shard), lambda i: (0, i))
    pad = step // 2 - 3 * shard
    q, k, v, f = pl.pallas_call(
        functools.partial(project_kernel, shard=shard),
        grid=(2,),
        in_specs=[whole(x)]
        + [pl.BlockSpec((step, w.shape[1]), lambda i: (i, 0)) for w in weights],
        out_specs=[spec, spec, spec, pl.BlockSpec((1, rows, 2 * pad), lambda i: (i, 0, 0))],
        out_shape=[low, low, low, jax.ShapeDtypeStruct((2, rows, 2 * pad), F32)],
        compiler_params=pltpu.CompilerParams(vmem_limit_bytes=VMEM_BYTES),
        cost_estimate=cost(2 * rows * x.shape[1] * 4 * step // 2, [x, *weights, low, low, low]),
        name="project",
    )(x, *weights)
    logits = f.reshape(2, rows, 2, pad)[..., :few].transpose(1, 0, 2, 3).reshape(rows, 4 * few)
    return q, k, v, logits


def combine_kernel(core_ref, *refs, lefts):
    left_refs, w_refs, (give_ref, keep_ref) = refs[:lefts], refs[lefts:-2], refs[-2:]
    step = pl.program_id(0)
    wide = w_refs[0].shape[1]
    for out, cond in ((give_ref, step < 2), (keep_ref, step >= 2)):

        @pl.when(cond)
        def _():
            for n, w in enumerate(w_refs):
                got, at = None, 0
                for left in left_refs:
                    deep = left.shape[1]
                    part = nn(left[...], w[at : at + deep, :])
                    got = part if got is None else got + part
                    at += deep
                out[:, n * wide : (n + 1) * wide] = got.astype(out.dtype)


def combine(core, lefts, weights):
    rows = lefts[0].shape[0]
    wide = weights[0].shape[1] * len(weights)
    block = rows // 4

    def place(i, core_ref):
        mine = core_ref[0]
        return (jnp.where(i < 2, (1 - mine) * 2 + i, mine * 2 + i - 2), 0)

    outs = [
        jax.ShapeDtypeStruct((rows // 2, wide), BF16),
        jax.ShapeDtypeStruct((rows // 2, wide), F32),
    ]
    return pl.pallas_call(
        functools.partial(combine_kernel, lefts=len(lefts)),
        grid_spec=pltpu.PrefetchScalarGridSpec(
            num_scalar_prefetch=1,
            grid=(4,),
            in_specs=[pl.BlockSpec((block, left.shape[1]), place) for left in lefts]
            + [whole(w) for w in weights],
            out_specs=[
                pl.BlockSpec((block, wide), lambda i, c: (jnp.minimum(i, 1), 0)),
                pl.BlockSpec((block, wide), lambda i, c: (jnp.maximum(i - 2, 0), 0)),
            ],
        ),
        out_shape=outs,
        compiler_params=pltpu.CompilerParams(vmem_limit_bytes=VMEM_BYTES),
        cost_estimate=cost(
            2 * rows * weights[0].shape[0] * wide, [*lefts, *weights, *outs]
        ),
        name="combine",
    )(core.reshape(1), *lefts, *weights)


def spread_kernel(len_ref, x_ref, *refs):
    w_refs, out_ref = refs[:-1], refs[-1]
    rows = x_ref.shape[0]
    got = nt(x_ref[...], joined(w_refs))
    pos = pl.program_id(0) * rows + lax.broadcasted_iota(jnp.int32, got.shape, 0)
    out_ref[...] = jnp.where(pos < len_ref[0], got, 0.0).astype(BF16)


def spread(length, x, weights):
    rows, wide = x.shape[0], weights[0].shape[0]
    block = rows // 4
    out = jax.ShapeDtypeStruct((rows, wide), BF16)
    return pl.pallas_call(
        spread_kernel,
        grid=(4,),
        in_specs=[
            pl.BlockSpec(memory_space=pltpu.SMEM),
            pl.BlockSpec((block, x.shape[1]), lambda i: (i, 0)),
        ]
        + [whole(w) for w in weights],
        out_specs=pl.BlockSpec((block, wide), lambda i: (i, 0)),
        out_shape=out,
        compiler_params=pltpu.CompilerParams(vmem_limit_bytes=VMEM_BYTES),
        cost_estimate=cost(2 * rows * x.shape[1] * wide, [x, *weights, out]),
        name="spread",
    )(length, x, *weights)


def inner_kernel(x_ref, *refs):
    w_refs, (gate_ref, up_ref, inner_ref) = refs[:-3], refs[-3:]
    both = nt(x_ref[...], joined(w_refs))
    gate, up = both[:, :UNIT_BLOCK], both[:, UNIT_BLOCK:]
    gate_ref[...] = gate
    up_ref[...] = up
    inner_ref[...] = (gate * jax.nn.sigmoid(gate) * up).astype(BF16)


def inner_units(x, weights):
    rows = x.shape[0]
    total = weights[0].shape[0] // 2
    spec = pl.BlockSpec((rows, UNIT_BLOCK), lambda i: (0, i))
    outs = [jax.ShapeDtypeStruct((rows, total), t) for t in (F32, F32, BF16)]
    return pl.pallas_call(
        inner_kernel,
        grid=(total // UNIT_BLOCK,),
        in_specs=[whole(x)]
        + [pl.BlockSpec((2 * UNIT_BLOCK, w.shape[1]), lambda i: (i, 0)) for w in weights],
        out_specs=[spec] * 3,
        out_shape=outs,
        compiler_params=pltpu.CompilerParams(vmem_limit_bytes=VMEM_BYTES),
        cost_estimate=cost(4 * rows * x.shape[1] * total, [x, *weights, *outs]),
        name="inner_units",
    )(x, *weights)


def inner_grads_kernel(x_ref, gate_ref, up_ref, *refs):
    down_refs, pre_ref = refs[:-1], refs[-1]
    grad = nt(x_ref[...], joined(down_refs))
    gate, up = gate_ref[...], up_ref[...]
    sig = jax.nn.sigmoid(gate)
    pre_ref[:, :UNIT_BLOCK] = (grad * up * (sig * (1.0 + gate * (1.0 - sig)))).astype(BF16)
    pre_ref[:, UNIT_BLOCK:] = (grad * (gate * sig)).astype(BF16)


def inner_grads(x, gate, up, down):
    rows, cols = x.shape
    total = gate.shape[1]
    spec = pl.BlockSpec((rows, UNIT_BLOCK), lambda i: (0, i))
    out = jax.ShapeDtypeStruct((rows, 2 * total), BF16)
    return pl.pallas_call(
        inner_grads_kernel,
        grid=(total // UNIT_BLOCK,),
        in_specs=[whole(x), spec, spec]
        + [pl.BlockSpec((UNIT_BLOCK, w.shape[1]), lambda i: (i, 0)) for w in down],
        out_specs=pl.BlockSpec((rows, 2 * UNIT_BLOCK), lambda i: (0, i)),
        out_shape=out,
        compiler_params=pltpu.CompilerParams(vmem_limit_bytes=VMEM_BYTES),
        cost_estimate=cost(2 * rows * cols * total, [x, gate, up, *down, out]),
        name="inner_grads",
    )(x, gate, up, *down)


def half_products(left_refs, right, side):
    parts = []
    for ref, narrow in left_refs:
        got = dot_first(ref[...], right)
        if narrow:
            few = got.shape[0] // 2
            got = jnp.where(side == 0, got[:few], got[few:])
        parts.append(got)
    return parts


def term_kernel(*refs, narrow, side):
    count = len(narrow)
    right_ref, add_refs, out_ref = refs[count], refs[count + 1 : -1], refs[-1]
    at = 0
    for part in half_products(list(zip(refs[:count], narrow)), right_ref[...], side):
        rows = slice(at, at + part.shape[0])
        for add in add_refs:
            part = part + add[rows, :].astype(F32)
        out_ref[rows, :] = part.astype(BF16)
        at += part.shape[0]


def left_specs(lefts, steps, block):
    specs, narrow = [], []
    for left in lefts:
        rows, cols = left.shape
        wide = cols // (2 * steps)
        narrow.append(wide % 128 != 0)
        if wide % 128:
            specs.append(pl.BlockSpec((rows, cols), lambda i: (0, 0)))
        else:
            specs.append(pl.BlockSpec((rows, wide), lambda i: (0, block(i))))
    return specs, tuple(narrow)


def chunks_of(lefts):
    half = lefts[0].shape[1] // 2
    return max(1, half // 512) if len(lefts) == 1 else 1


def term_sum(lefts, right, side, r, wide, adds=()):
    steps = chunks_of(lefts)
    half = sum(left.shape[1] for left in lefts) // 2
    specs, narrow = left_specs(lefts, steps, lambda i: side * steps + i)
    part = pl.BlockSpec((half // steps, wide), lambda i: (i, 0))
    out = jax.ShapeDtypeStruct((half, wide), BF16)
    return pl.pallas_call(
        functools.partial(term_kernel, narrow=narrow, side=side),
        grid=(steps,),
        in_specs=specs
        + [pl.BlockSpec((right.shape[0], wide), lambda i: (0, r))]
        + [part] * len(adds),
        out_specs=part,
        out_shape=out,
        compiler_params=pltpu.CompilerParams(vmem_limit_bytes=VMEM_BYTES),
        cost_estimate=cost(2 * right.shape[0] * half * wide, [*adds, out, out]),
        name="term_sum",
    )(*lefts, right, *adds)


def total_kernel(*refs, narrow, steps):
    count = len(narrow)
    right_ref, tops, lows, out_ref = refs[count], refs[count + 1 : -3], refs[-3:-1], refs[-1]
    step = pl.program_id(0)
    side = step // steps
    parts = half_products(list(zip(refs[:count], narrow)), right_ref[...], side)
    if count == 1:
        places = [parts]
    else:
        places = [
            [part[n * (part.shape[0] // 2) : (n + 1) * (part.shape[0] // 2)] for part in parts]
            for n in range(2)
        ]
    for this, adds in ((0, tops), (1, lows)):

        @pl.when(side == this)
        def _():
            at = 0
            for n, place in enumerate(places):
                off = 0
                for part, whole_part in zip(place, parts):
                    few = part.shape[0]
                    start = off + n * few if count > 1 else 0
                    got = part
                    for add in adds:
                        got = got + add[start : start + few, :].astype(F32)
                    out_ref[at : at + few, :] = got.astype(BF16)
                    at += few
                    off += whole_part.shape[0]


def total_sum(lefts, right, tops, lows, wide):
    steps = chunks_of(lefts)
    full = sum(left.shape[1] for left in lefts)
    block = full // (2 * steps)
    specs, narrow = left_specs(lefts, steps, lambda i: i)
    out = jax.ShapeDtypeStruct((full, wide), BF16)
    return pl.pallas_call(
        functools.partial(total_kernel, narrow=narrow, steps=steps),
        grid=(2 * steps,),
        in_specs=specs
        + [pl.BlockSpec((right.shape[0], wide), lambda i: (0, 0))]
        + [pl.BlockSpec((block, wide), lambda i: (jnp.minimum(i, steps - 1), 0))] * 2
        + [pl.BlockSpec((block, wide), lambda i: (jnp.maximum(i - steps, 0), 0))] * 2,
        out_specs=pl.BlockSpec((block, wide), lambda i: (i, 0)),
        out_shape=out,
        compiler_params=pltpu.CompilerParams(vmem_limit_bytes=VMEM_BYTES),
        cost_estimate=cost(2 * right.shape[0] * full * wide, [out, out, out]),
        name="total_sum",
    )(*lefts, right, *tops, *lows)


class Plan:
    def __init__(self, ways_dp, ways_tensor):
        self.ways_dp = ways_dp
        self.ways_tensor = ways_tensor
        self.chips = ways_dp // 2
        self.bits = self.chips.bit_length() - 1
        assert self.chips == 1 << self.bits and ways_tensor == 4
        dp = lax.axis_index("dp")
        self.chip = dp // 2
        self.core = dp % 2
        self.place = lax.axis_index("tensor")
        self.core_perm = [(i, i ^ 1) for i in range(ways_dp)]

    def swap_core(self, array):
        return lax.ppermute(array, "dp", self.core_perm)

    def swap_chip(self, array, bit):
        perm = [(i, i ^ (2 << bit)) for i in range(self.ways_dp)]
        return lax.ppermute(array, "dp", perm)

    def route(self, turn):
        pairs = []
        for chip in range(self.chips):
            for core in range(2):
                for z in range(4):
                    micro = (z + turn) % 2
                    source = (2 * chip + core) * 4 + z
                    target = (2 * chip + z // 2) * 4 + 2 * micro + core
                    pairs.append((source, target))
        return pairs

    def by_chip(self, array):
        lead = array.shape[:-1]
        wide = array.shape[-1] // self.chips
        parts = [
            lax.dynamic_slice_in_dim(array, (self.chip ^ r) * wide, wide, axis=-1)
            for r in range(self.chips)
        ]
        return jnp.concatenate(parts, axis=-1).reshape(*lead, -1)

    def to_chip(self, array):
        got = []
        for turn in range(2):
            micro = (self.place + turn) % 2
            part = lax.dynamic_index_in_dim(array, micro, 0, keepdims=False)
            got.append(lax.ppermute(self.by_chip(part), ("dp", "tensor"), self.route(turn)))
        first = self.place // 2 == 0
        return jnp.concatenate(
            [jnp.where(first, got[0], got[1]), jnp.where(first, got[1], got[0])], axis=0
        )

    def from_chip(self, array):
        rows = array.shape[0] // 2
        got = []
        for turn in range(2):
            block = (self.place // 2 + turn) % 2
            part = lax.dynamic_slice_in_dim(array, block * rows, rows, axis=0)
            back = [(b, a) for a, b in self.route(turn)]
            got.append(lax.ppermute(self.by_chip(part), ("dp", "tensor"), back))
        first = self.place % 2 == 0
        return jnp.stack([jnp.where(first, got[0], got[1]), jnp.where(first, got[1], got[0])])

    def both_rows(self, half):
        other = self.swap_core(half)
        first = self.core == 0
        return jnp.concatenate(
            [jnp.where(first, half, other), jnp.where(first, other, half)], axis=0
        )

    def sum_rows(self, give, keep):
        return keep + self.swap_core(give).astype(F32)

    def line_gather(self, shard):
        mine = lax.dynamic_index_in_dim(shard, self.core, 0, keepdims=False)
        theirs = lax.dynamic_index_in_dim(shard, 1 - self.core, 0, keepdims=False)
        other = self.swap_core(theirs)
        first = self.core == 0
        pair = jnp.concatenate(
            [jnp.where(first, mine, other), jnp.where(first, other, mine)], axis=1
        )
        return lax.all_gather(pair, "tensor", axis=0, tiled=True)

    def near_gather(self, own):
        if self.bits == 2:
            return [own, self.swap_chip(own, 0), self.swap_chip(own, 1)]
        parts = [own]
        for bit in range(self.bits):
            parts = parts + [self.swap_chip(p, bit) for p in parts]
        return [jnp.concatenate(parts, axis=1)]

    def far_gather(self, near):
        if self.bits != 2:
            return near
        own, by_x, by_y = near
        half = own.shape[0] // 2
        far_top = self.swap_chip(by_x[:half], 1)
        far_low = self.swap_chip(by_y[half:], 0)
        return [own, by_x, by_y, jnp.concatenate([far_top, far_low], axis=0)]

    def scatter(self, total):
        return lax.psum_scatter(total, "tensor", scatter_dimension=0, tiled=True)

    def share(self, pair):
        narrow = pair.shape[1] // 2
        mine = lax.dynamic_slice_in_dim(pair, self.core * narrow, narrow, axis=1)
        theirs = lax.dynamic_slice_in_dim(pair, (1 - self.core) * narrow, narrow, axis=1)
        other = self.swap_core(theirs)
        first = self.core == 0
        return jnp.stack([jnp.where(first, mine, other), jnp.where(first, other, mine)]).astype(F32)

    def sum_all(self, vector):
        vector = vector + self.swap_core(vector)
        for bit in range(self.bits):
            vector = vector + self.swap_chip(vector, bit)
        for bit in range(2):
            perm = [(z, z ^ (1 << bit)) for z in range(4)]
            vector = vector + lax.ppermute(vector, "tensor", perm)
        return vector


class Reduction:
    def __init__(self, plan, lefts, right):
        self.plan, self.lefts, self.right = plan, lefts, right
        self.wide = right.shape[1] // plan.chips
        self.staged = plan.bits == 2
        if self.staged:
            if len(lefts) == 1:
                self.first = [
                    self.top(3).astype(BF16),
                    self.low(3).astype(BF16),
                    self.low(1).astype(BF16),
                    self.top(2).astype(BF16),
                ]
            else:
                self.first = [self.sent(0, 3), self.sent(1, 3), self.sent(1, 1), self.sent(0, 2)]
        else:
            self.first = [
                jnp.concatenate([self.top(r), self.low(r)], axis=0) for r in range(plan.chips)
            ]

    def term(self, r, side):
        right = self.right[:, r * self.wide : (r + 1) * self.wide]
        parts = []
        for left in self.lefts:
            half = left.shape[1] // 2
            parts.append(dot_first(left[:, side * half : (side + 1) * half], right))
        return parts[0] if len(parts) == 1 else jnp.concatenate(parts, axis=0)

    def sent(self, side, r, *adds):
        return term_sum(self.lefts, self.right, side, r, self.wide, adds)

    def top(self, r):
        return self.term(r, 0)

    def low(self, r):
        return self.term(r, 1)

    def by_place(self, half):
        if len(self.lefts) == 1:
            return half
        parts, at = [], 0
        for left in self.lefts:
            parts.append((at, left.shape[1] // 4))
            at += left.shape[1] // 2
        return jnp.concatenate(
            [half[at + n * few : at + (n + 1) * few] for n in range(2) for at, few in parts], axis=0
        )

    def send_first(self):
        if self.staged:
            a, b, c, d = self.first
            swap = self.plan.swap_chip
            self.got = [swap(a, 1), swap(b, 0), swap(c, 0), swap(d, 1)]
        else:
            self.got = list(self.first)

    def prepare_second(self):
        if self.staged:
            far_top, far_low = self.got[:2]
            self.second = [self.sent(0, 1, far_top), self.sent(1, 2, far_low)]
        else:
            self.second = []

    def send_second(self):
        if self.staged:
            self.last = [self.plan.swap_chip(self.second[0], 0), self.plan.swap_chip(self.second[1], 1)]
        else:
            self.last = []

    def finish(self):
        if self.staged:
            x_top, y_low = self.last
            x_low, y_top = self.got[2:]
            return total_sum(self.lefts, self.right, (x_top, y_top), (x_low, y_low), self.wide)
        else:
            parts = self.got
            for bit in reversed(range(self.plan.bits)):
                keep, give = parts[: 1 << bit], parts[1 << bit :]
                parts = [
                    k + self.plan.swap_chip(g.astype(BF16), bit).astype(F32)
                    for k, g in zip(keep, give)
                ]
            half = parts[0].shape[0] // 2
            total = jnp.concatenate(
                [self.by_place(parts[0][:half]), self.by_place(parts[0][half:])], axis=0
            )
        return total.astype(BF16)


class Direct:
    def __init__(self, plan, lefts, right):
        self.plan, self.left, self.right = plan, lefts[0], right
        self.wide = right.shape[1] // plan.chips
        self.first = [self.term(r).astype(BF16) for r in range(1, plan.chips)]

    def term(self, r):
        return dot_first(self.left, self.right[:, r * self.wide : (r + 1) * self.wide])

    def send_first(self):
        ways = range(self.plan.ways_dp)
        self.got = [
            lax.ppermute(part, "dp", [(i, i ^ (2 * (n + 1))) for i in ways])
            for n, part in enumerate(self.first)
        ]

    def prepare_second(self):
        self.second = []

    def send_second(self):
        self.last = []

    def finish(self):
        total = self.term(0)
        for part in self.got:
            total = total + part.astype(F32)
        return total.astype(BF16)


def together(*groups):
    return lax.optimization_barrier(groups)


def split_columns(matrix):
    return matrix.T.reshape(2, matrix.shape[1] // 2, matrix.shape[0])


def split_rows(matrix):
    return matrix.reshape(2, matrix.shape[0] // 2, matrix.shape[1])


def body(
    inputs,
    seq_lengths,
    seq_assign,
    norm1_gain,
    w_query,
    w_key,
    w_value,
    w_forget,
    forget_bias,
    w_out,
    norm2_gain,
    w_gate,
    w_up,
    w_down,
    out_grad,
):
    plan = Plan(lax.axis_size("dp"), lax.axis_size("tensor"))
    core, place = plan.core, plan.place
    part_rows = inputs.shape[1]
    seq_rows = part_rows * 4
    half_rows = seq_rows // 2
    heads_shard = w_forget.shape[1] // 2
    heads_here = heads_shard * 4
    shard_cols = w_query.shape[1] // 2
    blocks = w_gate.shape[1] // 2 // UNIT_BLOCK

    def by_block(matrix):
        return split_columns(matrix).reshape(2, blocks, 1, UNIT_BLOCK, matrix.shape[0])

    forget_part = jnp.pad(
        split_columns(w_forget), ((0, 0), (0, FORGET_PAD - heads_shard), (0, 0))
    )
    line_one = plan.line_gather(
        jnp.concatenate(
            [split_columns(w_query), split_columns(w_key), split_columns(w_value), forget_part],
            axis=1,
        )
    )
    inputs, line_one = together(inputs, line_one)
    rows_one = line_one.shape[0] // 4

    def by_kind(piece):
        piece = piece.reshape(4, rows_one, -1)
        edges = [0, shard_cols, 2 * shard_cols, 3 * shard_cols, rows_one]
        parts = [piece[:, a:b].reshape(-1, piece.shape[-1]) for a, b in zip(edges, edges[1:])]
        return jnp.concatenate(parts, axis=0)

    full_one = plan.far_gather(plan.near_gather(line_one))
    rows_in = plan.to_chip(inputs)
    rows_in, full_one = together(rows_in, full_one)
    rows_in = rows_in.astype(F32)
    line_mid = plan.line_gather(
        jnp.concatenate([split_rows(w_out), split_rows(w_down)], axis=1)
    )
    line_mid, full_one = together(line_mid, full_one)
    line_mid = line_mid.reshape(4, -1, line_mid.shape[-1])
    near_out = plan.near_gather(line_mid[:, :shard_cols].reshape(4 * shard_cols, -1))
    near_down = plan.near_gather(line_mid[:, shard_cols:].reshape(-1, line_mid.shape[-1]))
    two_part = jnp.concatenate([by_block(w_gate), by_block(w_up)], axis=2)
    line_two = plan.line_gather(two_part.reshape(2, -1, two_part.shape[-1]))

    other_assign = plan.swap_core(seq_assign)
    assign_both = jnp.where(
        core == 0,
        jnp.concatenate([seq_assign, other_assign], axis=1),
        jnp.concatenate([other_assign, seq_assign], axis=1),
    ).reshape(4)
    seq_id = jnp.sum(jnp.where(jnp.arange(4) == place, assign_both, 0))
    length = jnp.sum(jnp.where(jnp.arange(seq_lengths.shape[0]) == seq_id, seq_lengths, 0))
    count = length.reshape(1)
    valid_here = (core * half_rows + jnp.arange(half_rows) < length).astype(F32)[:, None]

    gain_one = plan.by_chip(norm1_gain)
    gain_two = plan.by_chip(norm2_gain)
    bias_here = lax.dynamic_index_in_dim(
        forget_bias.reshape(4, 2, heads_shard), core, 1, keepdims=False
    ).reshape(-1)

    scale_one = row_scale(rows_in)
    normed_one = plan.both_rows((rows_in * scale_one * gain_one).astype(BF16))
    queries, key_rows, value_rows, logits = project(
        normed_one, full_one, shard_cols, heads_shard
    )
    forget_logit = logits + bias_here
    cumul_gate = jnp.cumsum(jax.nn.log_sigmoid(forget_logit), axis=0)
    gate_pairs = cumul_gate.reshape(seq_rows, heads_here // 2, 2).transpose(1, 0, 2)
    near_out, gate_pairs = together(near_out, gate_pairs)
    full_out, line_two, gate_pairs = together(plan.far_gather(near_out), line_two, gate_pairs)
    mixed_low, log_total = attn_fwd(count, queries, key_rows, value_rows, gate_pairs)
    mixed_low, near_down, full_one = together(mixed_low, near_down, full_one)
    kinds_one = [by_kind(piece) for piece in full_one]
    full_down = plan.far_gather(near_down)
    near_two, out_grad = together(plan.near_gather(line_two), out_grad)
    full_two = plan.far_gather(near_two)
    cotangent = plan.to_chip(out_grad).astype(F32)
    hidden_in = rows_in + plan.sum_rows(*combine(core, [mixed_low], full_out))

    scale_two = row_scale(hidden_in)
    normed_two = plan.both_rows((hidden_in * scale_two * gain_two).astype(BF16))
    normed_two, full_down, kinds_one = together(normed_two, full_down, kinds_one)
    gate_pre, up_pre, inner_low = inner_units(normed_two, full_two)
    grad_ffn = plan.both_rows((valid_here * cotangent).astype(BF16))
    down_sum = Reduction(plan, [inner_low], grad_ffn)
    down_sum.first, gate_pre = together(down_sum.first, gate_pre)
    down_sum.send_first()

    grad_pre = inner_grads(grad_ffn, gate_pre, up_pre, full_down)
    down_far, grad_pre = together(down_sum.got[:2], grad_pre)
    down_sum.got = [*down_far, *down_sum.got[2:]]
    two_sum = Reduction(plan, [grad_pre], normed_two)
    two_sum.first, down_sum.got, grad_pre, inner_low = together(
        two_sum.first, down_sum.got, grad_pre, inner_low
    )
    two_sum.send_first()
    down_sum.prepare_second()
    give_two, keep_two = combine(core, [grad_pre], full_two)
    give_ffn, keep_ffn = combine(core, [inner_low], full_down)
    down_sum.send_second()
    two_far, down_sum.last, give_two, give_ffn = together(
        two_sum.got[:2], down_sum.last, give_two, give_ffn
    )
    two_sum.got = [*two_far, *two_sum.got[2:]]
    grad_normed_two = plan.sum_rows(give_two, keep_two)
    gain_two_term = jnp.sum(grad_normed_two * hidden_in * scale_two, axis=0)
    grad_hidden = valid_here * cotangent + norm_back(
        hidden_in, scale_two, gain_two, grad_normed_two
    )

    grad_attn = plan.both_rows(grad_hidden.astype(BF16))
    out_sum = (Direct if plan.bits == 2 else Reduction)(plan, [mixed_low], grad_attn)
    two_sum.prepare_second()
    out_sum.first, two_sum.second, grad_attn = together(
        out_sum.first, two_sum.second, grad_attn
    )
    two_sum.send_second()
    out_sum.send_first()
    ffn_rows = plan.sum_rows(give_ffn, keep_ffn)
    outputs = (valid_here * (hidden_in + ffn_rows)).astype(BF16)
    grad_mixed = spread(count, grad_attn, full_out)
    query_low, key_low, value_low, grad_cumul = attn_bwd(
        count, queries, key_rows, value_rows, gate_pairs, log_total, mixed_low, grad_mixed
    )
    two_sum.got, two_sum.last, out_sum.got, query_low, key_low, value_low, grad_cumul = together(
        two_sum.got, two_sum.last, out_sum.got, query_low, key_low, value_low, grad_cumul
    )
    out_sum.prepare_second()
    out_sum.send_second()
    out_total, grad_cumul = together(out_sum.finish(), grad_cumul)
    down_pair = plan.scatter(down_sum.finish())
    out_total, down_pair = together(out_total, down_pair)
    out_pair = plan.scatter(out_total)
    grad_logf = jnp.flip(jnp.cumsum(jnp.flip(grad_cumul, 0), axis=0), 0)
    grad_logit = grad_logf * jax.nn.sigmoid(-forget_logit)
    bias_term = jnp.sum(grad_logit, axis=0)
    logit_low = jnp.pad(
        grad_logit.astype(BF16).reshape(seq_rows, 4, heads_shard),
        ((0, 0), (0, 0), (0, FORGET_PAD - heads_shard)),
    ).reshape(seq_rows, -1)
    grad_one = [query_low, key_low, value_low, logit_low]
    one_sum = Reduction(plan, grad_one, normed_one)
    give_one, keep_one = combine(core, grad_one, kinds_one)
    one_sum.first, two_sum.last, outputs, give_one = together(
        one_sum.first, two_sum.last, outputs, give_one
    )
    one_sum.send_first()
    outputs = plan.from_chip(outputs)
    one_sum.prepare_second()
    one_sum.send_second()
    two_total, out_pair = together(two_sum.finish(), out_pair)
    two_pair = plan.scatter(two_total)
    one_total, two_pair = together(one_sum.finish(), two_pair)
    one_pair = plan.scatter(one_total)
    grad_normed_one = plan.sum_rows(give_one, keep_one)
    gain_one_term = jnp.sum(grad_normed_one * rows_in * scale_one, axis=0)
    input_grad = plan.from_chip(
        (grad_hidden + norm_back(rows_in, scale_one, gain_one, grad_normed_one)).astype(BF16)
    )

    bias_full = jnp.where(
        (jnp.arange(2) == core)[None, :, None], bias_term.reshape(4, 1, heads_shard), 0.0
    ).reshape(-1)
    wide = norm1_gain.shape[0]
    small = plan.sum_all(
        jnp.concatenate([plan.by_chip(gain_one_term), plan.by_chip(gain_two_term), bias_full])
    )

    down_shard, two_shard = plan.share(down_pair), plan.share(two_pair)
    out_shard, one_shard = plan.share(out_pair), plan.share(one_pair)

    two_shard = two_shard.reshape(2, blocks, 2, UNIT_BLOCK, -1)

    def columns(shard):
        return shard.reshape(-1, shard.shape[-1]).T

    def rows(shard):
        return shard.reshape(-1, shard.shape[-1])

    return (
        outputs,
        input_grad,
        small[:wide],
        columns(one_shard[:, :shard_cols]),
        columns(one_shard[:, shard_cols : 2 * shard_cols]),
        columns(one_shard[:, 2 * shard_cols : 3 * shard_cols]),
        columns(one_shard[:, 3 * shard_cols : 3 * shard_cols + heads_shard]),
        small[2 * wide :],
        rows(out_shard),
        small[wide : 2 * wide],
        columns(two_shard[:, :, 0]),
        columns(two_shard[:, :, 1]),
        rows(down_shard),
    )


def solution(mesh):
    return jax.shard_map(
        body,
        mesh=mesh,
        in_specs=(
            P(None, ("dp", "tensor"), None),
            P(),
            P(None, "dp"),
            P(),
            P("dp", "tensor"),
            P("dp", "tensor"),
            P("dp", "tensor"),
            P("dp", "tensor"),
            P(),
            P("tensor", "dp"),
            P(),
            P("dp", "tensor"),
            P("dp", "tensor"),
            P("tensor", "dp"),
            P(None, ("dp", "tensor"), None),
        ),
        out_specs=(
            P(None, ("dp", "tensor"), None),
            P(None, ("dp", "tensor"), None),
            P(),
            P("dp", "tensor"),
            P("dp", "tensor"),
            P("dp", "tensor"),
            P("dp", "tensor"),
            P(),
            P("tensor", "dp"),
            P(),
            P("dp", "tensor"),
            P("dp", "tensor"),
            P("tensor", "dp"),
        ),
        check_vma=False,
    )
```
